256 devices in a mesh: row: 16 (over z_lo, x, core), col: 16 (over z_hi, y).
Axes of the slice: x: 4, y: 4, z: 8 (z_hi: 4, z_lo: 2; z = z_hi * 2 + z_lo), core: 2. Of those that a mesh axis runs over, the one named last changes fastest.
Arguments:
- embeddings: bfloat16 [32768, 768], P(('row', 'col')), may hold values from -400 to 400
- tile_list: int32 [16, 16, 32, 2], P('row', 'col'), may hold values from -1 to 15, as said below
- seeds: int32 [32768], P(('row', 'col')), may hold values from 0 to 127
Outputs:
- scores: float32 [32768, 64], P(('row', 'col'))
The draws below stay inside these ranges and needn't reach their ends.
Inputs may be any that keep to these rules, and one draw needn't show every extreme that they name: tile_list[r, c] lists the tiles of the device at row index r and column index c: a live slot (a, b) stands for the tile of document block r * 16 + a against block b * 16 + c, with a < 16, b < 16 and r * 16 + a <= b * 16 + c. Live slots come first and are distinct, empty slots hold -1 in both entries, the tile (c, r) of a block against itself is always listed, and some device fills all 32 slots. `seeds`: values of 64 or more mark a document without a seed label.
All inputs are finite; a program needn't handle non-finite values.
Results may differ from the reference program's by a relative error of at most 0.00056.
Values may be sent and summed in bfloat16 or wider, within the bound.
No kernel may reach another device: no remote copies, remote signals or barrier semaphores. Data moves between devices by JAX's collectives and lax.ppermute only.
A program may use at most 64 MiB of HBM per device.

```python
import math
import jax
import jax.numpy as jnp
from jax import lax

E = 768
CLASSES = 64
ROWS = 128
ITERS = 3
TILES = 32
DOCS = 32768
N_ROW = 16
N_COL = 16


def draw_embeddings(key, part):
    key_base, key_column, key_row = jax.random.split(key, 3)
    column_scale = jnp.exp(jax.random.uniform(key_column, (E,), jnp.float32, math.log(0.5), math.log(5.0)))
    row_scale = jnp.exp(jax.random.uniform(key_row, (DOCS, 1), jnp.float32, 0.0, math.log(10.0)))
    base_values = jax.random.normal(key_base, (DOCS, E), jnp.float32)
    return (base_values * column_scale[None, :] * row_scale).astype(jnp.bfloat16)


def draw_tile_list(key, part):
    pair_total = N_ROW * N_COL
    pair_index = jnp.arange(pair_total, dtype=jnp.int32)
    first_local = pair_index // N_ROW
    second_local = pair_index % N_ROW

    def device_draw(device_key, device):
        row_at = device // N_COL
        col_at = device % N_COL
        allowed = row_at * N_COL + first_local <= second_local * N_COL + col_at
        self_pair = (first_local == col_at) & (second_local == row_at)
        key_coin, key_order = jax.random.split(device_key)
        coin_flip = jax.random.randint(key_coin, (pair_total,), 0, 2) == 1
        full_device = device == N_COL - 1
        chosen = allowed & (coin_flip | self_pair | full_device)
        shuffle = jax.random.permutation(key_order, pair_total).astype(jnp.int32)
        priority = jnp.where(self_pair, 0, jnp.where(chosen, 1 + shuffle, 2 * pair_total + shuffle))
        picked = jnp.argsort(priority, stable=True)[:TILES]
        filled = jnp.minimum(jnp.sum(chosen.astype(jnp.int32)), TILES)
        slot_index = jnp.arange(TILES, dtype=jnp.int32)
        row_pick = jnp.where(slot_index < filled, first_local[picked], -1)
        col_pick = jnp.where(slot_index < filled, second_local[picked], -1)
        return jnp.stack([row_pick, col_pick], axis=1)
    device_keys = jax.random.split(key, pair_total)
    drawn = jax.vmap(device_draw)(device_keys, jnp.arange(pair_total, dtype=jnp.int32))
    return drawn.reshape(N_ROW, N_COL, TILES, 2).astype(jnp.int32)


def with_ends(values, key, low, high):
    shape = values.shape
    place = [jax.random.randint(jax.random.fold_in(key, axis), (), 0, shape[axis]) for axis in range(len(shape))]
    values = values.at[tuple(place)].set(low)
    longest = shape.index(max(shape))
    place[longest] = (place[longest] + 1) % shape[longest]
    return values.at[tuple(place)].set(high)


def setup_inputs(seed: int = 0) -> dict:
    key_list = jax.random.split(jax.random.key(seed), 4)
    return {
        "embeddings": draw_embeddings(jax.random.fold_in(key_list[3], 71), 0),
        "tile_list": draw_tile_list(jax.random.fold_in(key_list[3], 71), 0),
        "seeds": with_ends(jax.random.randint(key_list[2], (DOCS,), 0, 2 * CLASSES), jax.random.fold_in(key_list[2], 1), 0, (2 * CLASSES) - 1).astype(jnp.int32),
    }


BLEND = 0.8
EPSILON = 1e-06

def reference(embeddings, tile_list, seeds):
    devices_all = N_ROW * N_COL
    sharpness = E ** 0.5
    highest = lax.Precision.HIGHEST
    features = embeddings.astype(jnp.float32)
    normed = (features * lax.rsqrt(lax.optimization_barrier(jnp.sum(features * features, axis=1, keepdims=True)) + EPSILON)).astype(jnp.bfloat16)
    blocks = normed.reshape(devices_all, ROWS, E)
    slot_pairs = tile_list.reshape(devices_all, TILES, 2)
    device = jnp.arange(devices_all, dtype=jnp.int32)
    slot_alive = slot_pairs[:, :, 0] >= 0
    first_block = ((device // N_COL)[:, None] * N_COL + jnp.maximum(slot_pairs[:, :, 0], 0)).astype(jnp.int32)
    second_block = (jnp.maximum(slot_pairs[:, :, 1], 0) * N_COL + (device % N_COL)[:, None]).astype(jnp.int32)
    diagonal = jnp.eye(ROWS, dtype=bool)

    def build_device(inputs):
        left_block, right_block, alive_now = inputs
        scores = jnp.einsum('sie,sje->sij', blocks[left_block].astype(jnp.float32), blocks[right_block].astype(jnp.float32), precision=highest)
        kernel = jnp.exp(sharpness * (scores - 1.0))
        masked = (left_block == right_block)[:, None, None] & diagonal[None] | ~alive_now[:, None, None]
        return jnp.where(masked, 0.0, kernel).astype(jnp.float32)
    kernels = lax.map(build_device, (first_block, second_block, slot_alive))

    def apply_graph(values):

        def add_tiles(summed, inputs):
            kernel, left_block, right_block = inputs
            to_rows = jnp.einsum('sij,sjk->sik', kernel, values[right_block].astype(jnp.float32), precision=highest)
            to_cols = jnp.einsum('sij,sik->sjk', kernel, values[left_block].astype(jnp.float32), precision=highest)
            return (summed.at[left_block].add(to_rows).at[right_block].add(to_cols), None)
        summed, _ = lax.scan(add_tiles, jnp.zeros(values.shape, jnp.float32), (kernels, first_block, second_block))
        return summed
    degree = apply_graph(jnp.ones((devices_all, ROWS, 1), jnp.float32))
    scale = lax.rsqrt(degree)
    seeded = (seeds.reshape(devices_all, ROWS, 1) == jnp.arange(CLASSES, dtype=jnp.int32)[None, None, :]).astype(jnp.float32)
    labels = seeded
    for sweep in range(ITERS):
        spread = scale * labels
        summed = apply_graph(spread)
        labels = BLEND * scale * summed + (1.0 - BLEND) * seeded
    return (CLASSES * labels).reshape(DOCS, CLASSES)
```

```python
import jax
import jax.numpy as jnp
import numpy as np
from jax import lax
from jax.experimental import pallas as pl
from jax.experimental.pallas import tpu as pltpu
from jax.sharding import Mesh
from jax.sharding import PartitionSpec as P

CLASSES = 64
BLEND = 0.8
EPSILON = 1e-06
AXES = ("zlo", "x", "core", "zhi", "y")
SIZES = (2, 4, 2, 4, 4)
ROW = ("zlo", "x", "core")
COL = ("zhi", "y")
GROUP = 16
BLOCKS = GROUP * GROUP
ROWS = 128
FEAT = 768
EXTRA = 8
CHUNK = 8
DEPTH = 4
VMEM = pl.BlockSpec(memory_space=pltpu.VMEM)
SMEM = pl.BlockSpec(memory_space=pltpu.SMEM)
ANY = pl.BlockSpec(memory_space=pl.ANY)


def prep_kernel(emb_ref, ids_ref, seeds_ref, out_ref):
    features = emb_ref[...].astype(jnp.float32)
    norm = lax.rsqrt(jnp.sum(features * features, axis=1, keepdims=True) + EPSILON)
    out_ref[:ROWS, :] = (features * norm).astype(jnp.bfloat16)
    lane = lax.broadcasted_iota(jnp.int32, (32, BLOCKS), 1)
    bits = jnp.sum((ids_ref[...] == lane).astype(jnp.float32), axis=0, keepdims=True)
    row = jnp.concatenate(
        [bits, seeds_ref[...].astype(jnp.float32), jnp.zeros((1, FEAT - BLOCKS - ROWS), jnp.float32)],
        axis=1,
    )
    out_ref[ROWS:, :] = jnp.broadcast_to(row, (EXTRA, FEAT)).astype(jnp.bfloat16)


def build_kernel(place_ref, count_ref, own_ref, other_ref, rows_ref,
                 tiles_ref, list_ref, deg_ref, cols_v, rows_v, stage, sums, in_sem, out_sem):
    core, diag_slot = place_ref[0], place_ref[1]
    copies = []
    for k in range(GROUP // 2):
        copies.append((own_ref.at[k, pl.ds(0, ROWS)], cols_v.at[2 * k + core]))
        copies.append((other_ref.at[k, pl.ds(0, ROWS)], cols_v.at[2 * k + 1 - core]))
    for k in range(GROUP):
        copies.append((rows_ref.at[k % 4, k // 4, pl.ds(0, ROWS)], rows_v.at[k]))
    copies = [pltpu.make_async_copy(src, dst, in_sem) for src, dst in copies]
    for copy in copies:
        copy.start()

    def add_slot(slot, found):
        live = count_ref[slot] > 0
        list_ref[found] = slot
        return found + live.astype(jnp.int32)

    found = lax.fori_loop(0, BLOCKS, add_slot, jnp.int32(0), unroll=8)
    chunks = (found + CHUNK - 1) // CHUNK

    def pad_slot(at, carry):
        list_ref[at] = -1
        return carry

    lax.fori_loop(found, chunks * CHUNK, pad_slot, 0)
    list_ref[BLOCKS] = chunks
    sums[...] = jnp.zeros_like(sums)
    sharpness = FEAT**0.5
    on_diag = (
        lax.broadcasted_iota(jnp.int32, (ROWS, ROWS), 0)
        == lax.broadcasted_iota(jnp.int32, (ROWS, ROWS), 1)
    ).astype(jnp.float32)
    for copy in copies:
        copy.wait()

    def out_copy(group):
        half = lax.rem(group, 2)
        return pltpu.make_async_copy(
            stage.at[half], tiles_ref.at[pl.ds(group * CHUNK, CHUNK)], out_sem.at[half]
        )

    def build_chunk(group, carry):
        half = lax.rem(group, 2)

        @pl.when(group >= 2)
        def _():
            out_copy(group - 2).wait()

        for k in range(CHUNK):
            listed = list_ref[group * CHUNK + k]
            slot = jnp.maximum(listed, 0)
            a, b = slot // GROUP, lax.rem(slot, GROUP)
            weight = jnp.where(listed >= 0, count_ref[slot], 0).astype(jnp.float32)
            off = jnp.where(listed == diag_slot, weight, 0.0)
            scores = lax.dot_general(
                cols_v[b], rows_v[a], (((1,), (1,)), ((), ())), preferred_element_type=jnp.float32
            )
            tile = jnp.exp(sharpness * (scores - 1.0)) * (weight - on_diag * off)
            high = tile.astype(jnp.bfloat16)
            stage[half, k, :ROWS, :] = high
            stage[half, k, ROWS:, :] = (tile - high.astype(jnp.float32)).astype(jnp.bfloat16)
            sums[b] += tile
        out_copy(group).start()
        return carry

    lax.fori_loop(0, chunks, build_chunk, 0)
    for back in (2, 1):
        @pl.when(chunks >= back)
        def _():
            out_copy(chunks - back).wait()
    for b in range(GROUP):
        deg_ref[pl.ds(b, 1), :] = jnp.sum(sums[b].T, axis=0, keepdims=True)


def apply_body(list_ref, tiles_ref, out_ref, wide, buf, sem):
    chunks = list_ref[BLOCKS]

    def fetch(group):
        at = lax.rem(group, DEPTH)
        return pltpu.make_async_copy(
            tiles_ref.at[pl.ds(group * CHUNK, CHUNK)], buf.at[at], sem.at[at]
        )

    def start(group):
        @pl.when(group < chunks)
        def _():
            fetch(group).start()

    return chunks, fetch, start


def split_into(wide, b, spread):
    high = spread.astype(jnp.bfloat16)
    low = (spread - high.astype(jnp.float32)).astype(jnp.bfloat16)
    wide[b, :CLASSES, :ROWS] = high
    wide[b, :CLASSES, ROWS:] = high
    wide[b, CLASSES:, :ROWS] = low
    wide[b, CLASSES:, ROWS:] = jnp.zeros_like(low)


def run_apply(list_ref, tiles_ref, out_ref, wide, buf, sem, fill):
    chunks, fetch, start = apply_body(list_ref, tiles_ref, out_ref, wide, buf, sem)
    for group in range(DEPTH - 1):
        start(group)
    fill()
    out_ref[...] = jnp.zeros_like(out_ref)

    def chunk_step(group, carry):
        fetch(group).wait()
        start(group + DEPTH - 1)
        at = lax.rem(group, DEPTH)
        for k in range(CHUNK):
            slot = jnp.maximum(list_ref[group * CHUNK + k], 0)
            a, b = slot // GROUP, lax.rem(slot, GROUP)
            both = jnp.dot(wide[b], buf[at, k], preferred_element_type=jnp.float32)
            out_ref[a] += both[:CLASSES] + both[CLASSES:]
        return carry

    lax.fori_loop(0, chunks, chunk_step, 0)


def first_kernel(list_ref, tiles_ref, seeds_ref, scale_ref, out_ref, wide, buf, sem):
    def fill():
        classes = lax.broadcasted_iota(jnp.int32, (CLASSES, ROWS), 0)
        for b in range(GROUP):
            seeded = classes == seeds_ref[pl.ds(b, 1), :]
            split_into(wide, b, jnp.where(seeded, scale_ref[pl.ds(b, 1), :], 0.0))

    run_apply(list_ref, tiles_ref, out_ref, wide, buf, sem, fill)


def next_kernel(list_ref, tiles_ref, spread_ref, out_ref, wide, buf, sem):
    def fill():
        for b in range(GROUP):
            split_into(wide, b, spread_ref[b])

    run_apply(list_ref, tiles_ref, out_ref, wide, buf, sem, fill)


APPLY = dict(
    out_shape=jax.ShapeDtypeStruct((GROUP, CLASSES, ROWS), jnp.float32),
    out_specs=VMEM,
    scratch_shapes=[
        pltpu.VMEM((GROUP, 2 * CLASSES, 2 * ROWS), jnp.bfloat16),
        pltpu.VMEM((DEPTH, CHUNK, 2 * ROWS, ROWS), jnp.bfloat16),
        pltpu.SemaphoreType.DMA((DEPTH,)),
    ],
    compiler_params=pltpu.CompilerParams(vmem_limit_bytes=48 << 20),
)


def exchange(blocks, axes):
    return lax.all_to_all(blocks, axes, 0, 0)


def gather(block, axes, count):
    return exchange(jnp.broadcast_to(block[None], (count,) + block.shape), axes)


def local(embeddings, tile_list, seeds):
    row_index = lax.axis_index(ROW)
    col_index = lax.axis_index(COL)
    core = lax.axis_index("core")
    slots = tile_list.reshape(-1, 2)
    ids = jnp.where(slots[:, :1] >= 0, slots[:, :1] * GROUP + slots[:, 1:], -1)
    block = pl.pallas_call(
        prep_kernel,
        out_shape=jax.ShapeDtypeStruct((ROWS + EXTRA, FEAT), jnp.bfloat16),
        in_specs=[VMEM] * 3,
        out_specs=VMEM,
    )(embeddings, ids, seeds[None, :])

    own = gather(block, ("zlo", "x"), 8)
    other = lax.ppermute(own, "core", [(0, 1), (1, 0)])
    even = jnp.where(core == 0, own[:, ROWS, : BLOCKS + ROWS], other[:, ROWS, : BLOCKS + ROWS])
    odd = jnp.where(core == 0, other[:, ROWS, : BLOCKS + ROWS], own[:, ROWS, : BLOCKS + ROWS])
    notes = jnp.stack([even, odd], axis=1).reshape(GROUP, BLOCKS + ROWS).astype(jnp.float32)
    seeds_cols = notes[:, BLOCKS:].astype(jnp.int32)
    bits = notes[:, :BLOCKS].reshape(GROUP, GROUP, GROUP)
    is_row = jnp.arange(GROUP) == row_index
    passed_on = jnp.sum(jnp.where(is_row, bits, 0.0), axis=2)
    mine = lax.dynamic_index_in_dim(notes, row_index, 0, keepdims=False)[:BLOCKS]

    passed_row = jnp.zeros((EXTRA, FEAT), jnp.float32)
    passed_row = passed_row.at[:, :GROUP].set(passed_on[:EXTRA])
    passed_row = passed_row.at[:, ROWS : ROWS + GROUP].set(passed_on[EXTRA:])
    block = jnp.concatenate([block[:ROWS], passed_row.astype(jnp.bfloat16)], axis=0)
    planes = lax.all_gather(block, "zhi")
    rows = gather(planes, "y", 4)
    passed = jnp.swapaxes(rows[:, :, ROWS:, : 2 * ROWS], 0, 1).reshape(GROUP, EXTRA, 2 * ROWS)
    passed = passed.astype(jnp.float32)
    is_col = jnp.arange(ROWS) == col_index
    low = jnp.sum(jnp.where(is_col, passed[:, :, :ROWS], 0.0), axis=2)
    high = jnp.sum(jnp.where(is_col, passed[:, :, ROWS:], 0.0), axis=2)
    mirrored = jnp.concatenate([low, high], axis=1)
    counts = (mine + mirrored.reshape(BLOCKS)).astype(jnp.int32)

    place = jnp.stack([core, col_index * GROUP + row_index]).astype(jnp.int32)
    tiles, listing, partial_degree = pl.pallas_call(
        build_kernel,
        out_shape=(
            jax.ShapeDtypeStruct((BLOCKS, 2 * ROWS, ROWS), jnp.bfloat16),
            jax.ShapeDtypeStruct((BLOCKS + 1,), jnp.int32),
            jax.ShapeDtypeStruct((GROUP, ROWS), jnp.float32),
        ),
        in_specs=[SMEM, SMEM, ANY, ANY, ANY],
        out_specs=(ANY, SMEM, VMEM),
        scratch_shapes=[
            pltpu.VMEM((GROUP, ROWS, FEAT), jnp.bfloat16),
            pltpu.VMEM((GROUP, ROWS, FEAT), jnp.bfloat16),
            pltpu.VMEM((2, CHUNK, 2 * ROWS, ROWS), jnp.bfloat16),
            pltpu.VMEM((GROUP, ROWS, ROWS), jnp.float32),
            pltpu.SemaphoreType.DMA,
            pltpu.SemaphoreType.DMA((2,)),
        ],
        compiler_params=pltpu.CompilerParams(vmem_limit_bytes=48 << 20),
    )(place, counts, own, other, rows)

    degree = jnp.sum(gather(partial_degree, ROW, GROUP), axis=0)
    scale = lax.rsqrt(degree)
    own_scale = lax.dynamic_index_in_dim(scale, row_index, 0)
    own_seeded = (seeds[None, :] == jnp.arange(CLASSES, dtype=jnp.int32)[:, None]).astype(jnp.float32)

    partial = pl.pallas_call(first_kernel, in_specs=[SMEM, ANY, VMEM, VMEM], **APPLY)(
        listing, tiles, seeds_cols, scale
    )
    labels = None
    for sweep in range(3):
        if sweep:
            spread = gather(own_scale * labels, ROW, GROUP)
            partial = pl.pallas_call(next_kernel, in_specs=[SMEM, ANY, VMEM], **APPLY)(
                listing, tiles, spread
            )
        summed = jnp.sum(exchange(partial, COL), axis=0)
        labels = BLEND * own_scale * summed + (1.0 - BLEND) * own_seeded
    return (CLASSES * labels).T


def solution(mesh):
    fine = Mesh(mesh.devices.reshape(SIZES), AXES)
    return jax.shard_map(
        local,
        mesh=fine,
        in_specs=(P(AXES, None), P(ROW, COL, None, None), P(AXES)),
        out_specs=P(AXES, None),
        check_vma=False,
    )
```

```python
import jax
import jax.numpy as jnp
import numpy as np
from jax import lax
from jax.experimental import pallas as pl
from jax.experimental.pallas import tpu as pltpu
from jax.sharding import Mesh
from jax.sharding import PartitionSpec as P

CLASSES = 64
BLEND = 0.8
EPSILON = 1e-06
AXES = ("zlo", "x", "core", "zhi", "y")
SIZES = (2, 4, 2, 4, 4)
ROW = ("zlo", "x", "core")
COL = ("zhi", "y")
GROUP = 16
BLOCKS = GROUP * GROUP
ROWS = 128
FEAT = 768
EXTRA = 8
CHUNK = 8
DEPTH = 4
VMEM = pl.BlockSpec(memory_space=pltpu.VMEM)
SMEM = pl.BlockSpec(memory_space=pltpu.SMEM)
ANY = pl.BlockSpec(memory_space=pl.ANY)


def prep_kernel(place_ref, emb_ref, slots_ref, seeds_ref, out_ref, bits_ref):
    features = emb_ref[...].astype(jnp.float32)
    norm = lax.rsqrt(jnp.sum(features * features, axis=1, keepdims=True) + EPSILON)
    out_ref[:ROWS, :] = (features * norm).astype(jnp.bfloat16)
    first, second = slots_ref[0:1, :], slots_ref[1:2, :]
    ids = jnp.where(first >= 0, first * GROUP + second, -1)
    hits = (lax.broadcasted_iota(jnp.int32, (BLOCKS, 32), 0) == ids).astype(jnp.float32)
    bits = lax.dot_general(
        jnp.ones((EXTRA, 32), jnp.float32), hits, (((1,), (1,)), ((), ())),
        preferred_element_type=jnp.float32,
    )
    bits_ref[...] = bits.astype(jnp.int32)
    out_ref[ROWS:, :BLOCKS] = bits.astype(jnp.bfloat16)
    out_ref[ROWS:, BLOCKS : BLOCKS + ROWS] = jnp.broadcast_to(
        seeds_ref[...].astype(jnp.float32), (EXTRA, ROWS)
    ).astype(jnp.bfloat16)
    out_ref[ROWS:, BLOCKS + ROWS :] = jnp.zeros((EXTRA, FEAT - BLOCKS - ROWS), jnp.bfloat16)


def relay_kernel(place_ref, block_ref, own_ref, other_ref, out_ref, seeds_ref, notes, sem, block_sem):
    core, row_index = place_ref[0], place_ref[2]
    keep = pltpu.make_async_copy(
        block_ref.at[pl.ds(0, ROWS)], out_ref.at[pl.ds(0, ROWS)], block_sem
    )
    keep.start()
    area = (pl.ds(ROWS, EXTRA), pl.ds(0, BLOCKS + ROWS))
    copies = []
    for k in range(GROUP // 2):
        copies.append((own_ref.at[(k, *area)], notes.at[2 * k + core]))
        copies.append((other_ref.at[(k, *area)], notes.at[2 * k + 1 - core]))
    copies = [pltpu.make_async_copy(src, dst, sem) for src, dst in copies]
    for copy in copies:
        copy.start()
    slot = lax.broadcasted_iota(jnp.int32, (BLOCKS, ROWS), 0)
    lane = lax.broadcasted_iota(jnp.int32, (BLOCKS, ROWS), 1)
    pick = (slot == lane * GROUP + row_index) & (lane < GROUP)
    pick = pick.astype(jnp.float32).astype(jnp.bfloat16)
    line = lax.broadcasted_iota(jnp.int32, (EXTRA, ROWS), 0)
    for copy in copies:
        copy.wait()
    for half in range(2):
        passed = jnp.zeros((EXTRA, ROWS), jnp.float32)
        seeds = jnp.zeros((EXTRA, ROWS), jnp.float32)
        for k in range(EXTRA):
            note = notes[half * EXTRA + k]
            picked = jnp.dot(note[:, :BLOCKS], pick, preferred_element_type=jnp.float32)
            passed = jnp.where(line == k, picked, passed)
            seeds = jnp.where(line == k, note[:, BLOCKS:].astype(jnp.float32), seeds)
        seeds_ref[half * EXTRA : (half + 1) * EXTRA, :] = seeds.astype(jnp.int32)
        out_ref[ROWS:, half * ROWS : (half + 1) * ROWS] = passed.astype(jnp.bfloat16)
    out_ref[ROWS:, 2 * ROWS :] = jnp.zeros((EXTRA, FEAT - 2 * ROWS), jnp.bfloat16)
    keep.wait()


def build_kernel(place_ref, bits_ref, own_ref, other_ref, rows_ref,
                 tiles_ref, list_ref, deg_ref, cols_v, rows_v, stage, sums,
                 notes, mirror_v, mirror_ref, count_ref, in_sem, out_sem, note_sem, mirror_sem):
    core, diag_slot = place_ref[0], place_ref[1]
    note_copies = [
        pltpu.make_async_copy(
            rows_ref.at[k % 4, k // 4, pl.ds(ROWS, EXTRA), pl.ds(0, 2 * ROWS)],
            notes.at[pl.ds(k * EXTRA, EXTRA)],
            note_sem,
        )
        for k in range(GROUP)
    ]
    for copy in note_copies:
        copy.start()
    copies = []
    for k in range(GROUP // 2):
        copies.append((own_ref.at[k, pl.ds(0, ROWS)], cols_v.at[2 * k + core]))
        copies.append((other_ref.at[k, pl.ds(0, ROWS)], cols_v.at[2 * k + 1 - core]))
    for k in range(GROUP):
        copies.append((rows_ref.at[k % 4, k // 4, pl.ds(0, ROWS)], rows_v.at[k]))
    copies = [pltpu.make_async_copy(src, dst, in_sem) for src, dst in copies]
    for copy in copies:
        copy.start()

    line = lax.broadcasted_iota(jnp.int32, (EXTRA, 2 * ROWS), 0)
    lane = lax.broadcasted_iota(jnp.int32, (EXTRA, 2 * ROWS), 1)
    pick = ((lane == line * ROWS + place_ref[3]) & (line < 2)).astype(jnp.float32)
    for copy in note_copies:
        copy.wait()
    mirror_v[...] = lax.dot_general(
        pick.astype(jnp.bfloat16), notes[...], (((1,), (1,)), ((), ())),
        preferred_element_type=jnp.float32,
    ).astype(jnp.int32)
    mirror_copy = pltpu.make_async_copy(mirror_v, mirror_ref, mirror_sem)
    mirror_copy.start()
    mirror_copy.wait()

    def add_slot(slot, found):
        a, b = slot // GROUP, lax.rem(slot, GROUP)
        count = bits_ref[0, slot] + mirror_ref[b // EXTRA, a * EXTRA + lax.rem(b, EXTRA)]
        count_ref[slot] = count
        list_ref[found] = slot
        return found + (count > 0).astype(jnp.int32)

    found = lax.fori_loop(0, BLOCKS, add_slot, jnp.int32(0), unroll=8)
    chunks = (found + CHUNK - 1) // CHUNK

    def pad_slot(at, carry):
        list_ref[at] = -1
        return carry

    lax.fori_loop(found, chunks * CHUNK, pad_slot, 0)
    list_ref[BLOCKS] = chunks
    sums[...] = jnp.zeros_like(sums)
    sharpness = FEAT**0.5
    on_diag = (
        lax.broadcasted_iota(jnp.int32, (ROWS, ROWS), 0)
        == lax.broadcasted_iota(jnp.int32, (ROWS, ROWS), 1)
    ).astype(jnp.float32)
    for copy in copies:
        copy.wait()

    def out_copy(group):
        half = lax.rem(group, 2)
        return pltpu.make_async_copy(
            stage.at[half], tiles_ref.at[pl.ds(group * CHUNK, CHUNK)], out_sem.at[half]
        )

    def build_chunk(group, carry):
        half = lax.rem(group, 2)

        @pl.when(group >= 2)
        def _():
            out_copy(group - 2).wait()

        for k in range(CHUNK):
            listed = list_ref[group * CHUNK + k]
            slot = jnp.maximum(listed, 0)
            a, b = slot // GROUP, lax.rem(slot, GROUP)
            weight = jnp.where(listed >= 0, count_ref[slot], 0).astype(jnp.float32)
            off = jnp.where(listed == diag_slot, weight, 0.0)
            scores = lax.dot_general(
                cols_v[b], rows_v[a], (((1,), (1,)), ((), ())), preferred_element_type=jnp.float32
            )
            tile = jnp.exp(sharpness * (scores - 1.0)) * (weight - on_diag * off)
            high = tile.astype(jnp.bfloat16)
            stage[half, k, :ROWS, :] = high
            stage[half, k, ROWS:, :] = (tile - high.astype(jnp.float32)).astype(jnp.bfloat16)
            sums[b] += tile
        out_copy(group).start()
        return carry

    lax.fori_loop(0, chunks, build_chunk, 0)
    for back in (2, 1):
        @pl.when(chunks >= back)
        def _():
            out_copy(chunks - back).wait()
    for b in range(GROUP):
        deg_ref[pl.ds(b, 1), :] = jnp.sum(sums[b].T, axis=0, keepdims=True)


def apply_body(list_ref, tiles_ref, out_ref, wide, buf, sem):
    chunks = list_ref[BLOCKS]

    def fetch(group):
        at = lax.rem(group, DEPTH)
        return pltpu.make_async_copy(
            tiles_ref.at[pl.ds(group * CHUNK, CHUNK)], buf.at[at], sem.at[at]
        )

    def start(group):
        @pl.when(group < chunks)
        def _():
            fetch(group).start()

    return chunks, fetch, start


def split_into(wide, b, spread):
    high = spread.astype(jnp.bfloat16)
    low = (spread - high.astype(jnp.float32)).astype(jnp.bfloat16)
    wide[b, :CLASSES, :ROWS] = high
    wide[b, :CLASSES, ROWS:] = high
    wide[b, CLASSES:, :ROWS] = low
    wide[b, CLASSES:, ROWS:] = jnp.zeros_like(low)


def run_apply(list_ref, tiles_ref, out_ref, wide, buf, sem, fill):
    chunks, fetch, start = apply_body(list_ref, tiles_ref, out_ref, wide, buf, sem)
    for group in range(DEPTH - 1):
        start(group)
    fill()
    out_ref[...] = jnp.zeros_like(out_ref)

    def chunk_step(group, carry):
        fetch(group).wait()
        start(group + DEPTH - 1)
        at = lax.rem(group, DEPTH)
        for k in range(CHUNK):
            slot = jnp.maximum(list_ref[group * CHUNK + k], 0)
            a, b = slot // GROUP, lax.rem(slot, GROUP)
            both = jnp.dot(wide[b], buf[at, k], preferred_element_type=jnp.float32)
            out_ref[a] += both[:CLASSES] + both[CLASSES:]
        return carry

    lax.fori_loop(0, chunks, chunk_step, 0)


def seeded_block(seeds_ref, b):
    classes = lax.broadcasted_iota(jnp.int32, (CLASSES, ROWS), 0)
    return classes == seeds_ref[pl.ds(b, 1), :]


def first_kernel(place_ref, list_ref, tiles_ref, seeds_ref, parts_ref,
                 out_ref, scale_ref, own_ref, total, wide, buf, sem):
    def fill():
        scale_ref[...] = lax.rsqrt(jnp.sum(parts_ref[...], axis=0))
        own_ref[...] = scale_ref[pl.ds(place_ref[2], 1), :]
        for b in range(GROUP):
            split_into(wide, b, jnp.where(seeded_block(seeds_ref, b), scale_ref[b : b + 1, :], 0.0))

    run_apply(list_ref, tiles_ref, total, wide, buf, sem, fill)
    out_ref[...] = total[...].astype(jnp.bfloat16)


def next_kernel(list_ref, tiles_ref, seeds_ref, scale_ref, smooth_ref,
                out_ref, total, wide, buf, sem):
    def fill():
        for b in range(GROUP):
            seed_part = jnp.where(
                seeded_block(seeds_ref, b), (1.0 - BLEND) * scale_ref[b : b + 1, :], 0.0
            )
            split_into(wide, b, smooth_ref[b].astype(jnp.float32) + seed_part)

    run_apply(list_ref, tiles_ref, total, wide, buf, sem, fill)
    out_ref[...] = total[...].astype(jnp.bfloat16)


PARTIAL = jax.ShapeDtypeStruct((GROUP, CLASSES, ROWS), jnp.bfloat16)
APPLY = dict(
    scratch_shapes=[
        pltpu.VMEM((GROUP, CLASSES, ROWS), jnp.float32),
        pltpu.VMEM((GROUP, 2 * CLASSES, 2 * ROWS), jnp.bfloat16),
        pltpu.VMEM((DEPTH, CHUNK, 2 * ROWS, ROWS), jnp.bfloat16),
        pltpu.SemaphoreType.DMA((DEPTH,)),
    ],
    compiler_params=pltpu.CompilerParams(vmem_limit_bytes=8 << 20),
)


def exchange(blocks, axes):
    return lax.all_to_all(blocks, axes, 0, 0)


def gather(block, axes, count):
    return exchange(jnp.broadcast_to(block[None], (count,) + block.shape), axes)


def local(embeddings, tile_list, seeds):
    row_index = lax.axis_index(ROW)
    col_index = lax.axis_index(COL)
    place = jnp.stack(
        [lax.axis_index("core"), col_index * GROUP + row_index, row_index, col_index]
    ).astype(jnp.int32)
    block, bits = pl.pallas_call(
        prep_kernel,
        out_shape=(
            jax.ShapeDtypeStruct((ROWS + EXTRA, FEAT), jnp.bfloat16),
            jax.ShapeDtypeStruct((EXTRA, BLOCKS), jnp.int32),
        ),
        in_specs=[SMEM] + [VMEM] * 3,
        out_specs=(VMEM, VMEM),
        compiler_params=pltpu.CompilerParams(vmem_limit_bytes=4 << 20),
    )(place, embeddings, tile_list.reshape(-1, 2).T, seeds[None, :])

    own = gather(block, ("zlo", "x"), 8)
    other = lax.ppermute(own, "core", [(0, 1), (1, 0)])
    block, seeds_cols = pl.pallas_call(
        relay_kernel,
        out_shape=(
            jax.ShapeDtypeStruct((ROWS + EXTRA, FEAT), jnp.bfloat16),
            jax.ShapeDtypeStruct((GROUP, ROWS), jnp.int32),
        ),
        in_specs=[SMEM, ANY, ANY, ANY],
        out_specs=(VMEM, VMEM),
        scratch_shapes=[
            pltpu.VMEM((GROUP, EXTRA, BLOCKS + ROWS), jnp.bfloat16),
            pltpu.SemaphoreType.DMA,
            pltpu.SemaphoreType.DMA,
        ],
        compiler_params=pltpu.CompilerParams(vmem_limit_bytes=4 << 20),
    )(place, block, own, other)

    planes = lax.all_gather(block, "zhi")
    rows = gather(planes, "y", 4)

    tiles, listing, partial_degree = pl.pallas_call(
        build_kernel,
        out_shape=(
            jax.ShapeDtypeStruct((BLOCKS, 2 * ROWS, ROWS), jnp.bfloat16),
            jax.ShapeDtypeStruct((BLOCKS + 1,), jnp.int32),
            jax.ShapeDtypeStruct((GROUP, ROWS), jnp.float32),
        ),
        in_specs=[SMEM, SMEM, ANY, ANY, ANY],
        out_specs=(ANY, SMEM, VMEM),
        scratch_shapes=[
            pltpu.VMEM((GROUP, ROWS, FEAT), jnp.bfloat16),
            pltpu.VMEM((GROUP, ROWS, FEAT), jnp.bfloat16),
            pltpu.VMEM((2, CHUNK, 2 * ROWS, ROWS), jnp.bfloat16),
            pltpu.VMEM((GROUP, ROWS, ROWS), jnp.float32),
            pltpu.VMEM((GROUP * EXTRA, 2 * ROWS), jnp.bfloat16),
            pltpu.VMEM((EXTRA, ROWS), jnp.int32),
            pltpu.SMEM((EXTRA, ROWS), jnp.int32),
            pltpu.SMEM((BLOCKS,), jnp.int32),
            pltpu.SemaphoreType.DMA,
            pltpu.SemaphoreType.DMA((2,)),
            pltpu.SemaphoreType.DMA,
            pltpu.SemaphoreType.DMA,
        ],
        compiler_params=pltpu.CompilerParams(vmem_limit_bytes=14 << 20),
    )(place, bits, own, other, rows)

    partial, scale, own_scale = pl.pallas_call(
        first_kernel,
        out_shape=(
            PARTIAL,
            jax.ShapeDtypeStruct((GROUP, ROWS), jnp.float32),
            jax.ShapeDtypeStruct((1, ROWS), jnp.float32),
        ),
        in_specs=[SMEM, SMEM, ANY, VMEM, VMEM],
        out_specs=(VMEM, VMEM, VMEM),
        **APPLY,
    )(place, listing, tiles, seeds_cols, gather(partial_degree, ROW, GROUP))
    for sweep in range(3):
        if sweep:
            smooth = gather((BLEND * own_scale * own_scale * summed).astype(jnp.bfloat16), ROW, GROUP)
            partial = pl.pallas_call(
                next_kernel,
                out_shape=PARTIAL,
                in_specs=[SMEM, ANY, VMEM, VMEM, VMEM],
                out_specs=VMEM,
                **APPLY,
            )(listing, tiles, seeds_cols, scale, smooth)
        summed, own_scale, seeds = lax.optimization_barrier((exchange(partial, COL), own_scale, seeds))
        summed = jnp.sum(summed.astype(jnp.float32), axis=0)
    seeded = seeds[None, :] == jnp.arange(CLASSES, dtype=jnp.int32)[:, None]
    labels = BLEND * own_scale * summed + (1.0 - BLEND) * seeded.astype(jnp.float32)
    return (CLASSES * labels).T


def solution(mesh):
    fine = Mesh(mesh.devices.reshape(SIZES), AXES)
    return jax.shard_map(
        local,
        mesh=fine,
        in_specs=(P(AXES, None), P(ROW, COL, None, None), P(AXES)),
        out_specs=P(AXES, None),
        check_vma=False,
    )
```

```python
import jax
import jax.numpy as jnp
from jax import lax
from jax.experimental import pallas as pl
from jax.experimental.pallas import tpu as pltpu
from jax.sharding import Mesh
from jax.sharding import PartitionSpec as P

CLASSES = 64
BLEND = 0.8
EPSILON = 1e-06
AXES = ("zlo", "x", "core", "zhi", "y")
SIZES = (2, 4, 2, 4, 4)
ROW = ("zlo", "x", "core")
COL = ("zhi", "y")
PLANE = ("x", "y")
LINE = ("zlo", "core", "zhi")
GROUP = 16
BLOCKS = GROUP * GROUP
ROWS = 128
FEAT = 768
EXTRA = 8
CHUNK = 8
VMEM = pl.BlockSpec(memory_space=pltpu.VMEM)
SMEM = pl.BlockSpec(memory_space=pltpu.SMEM)
ANY = pl.BlockSpec(memory_space=pl.ANY)


def prep_kernel(place_ref, emb_ref, slots_ref, seeds_ref, block_ref, noted_ref, seeds_out):
    features = emb_ref[...].astype(jnp.float32)
    norm = lax.rsqrt(jnp.sum(features * features, axis=1, keepdims=True) + EPSILON)
    normed = (features * norm).astype(jnp.bfloat16)
    block_ref[...] = normed
    noted_ref[:ROWS, :] = normed
    first, second = slots_ref[0:1, :], slots_ref[1:2, :]
    ids = jnp.where(first >= 0, first * GROUP + second, -1)
    hits = (lax.broadcasted_iota(jnp.int32, (BLOCKS, 32), 0) == ids).astype(jnp.float32)
    bits = lax.dot_general(
        jnp.ones((EXTRA, 32), jnp.float32), hits, (((1,), (1,)), ((), ())),
        preferred_element_type=jnp.float32,
    )
    noted_ref[ROWS:, :BLOCKS] = bits.astype(jnp.bfloat16)
    noted_ref[ROWS:, BLOCKS:] = jnp.zeros((EXTRA, FEAT - BLOCKS), jnp.bfloat16)
    seeds_out[...] = seeds_ref[...].astype(jnp.float32)


def relay_kernel(place_ref, plane_ref, seeds_ref, out_ref):
    x, y = place_ref[0], place_ref[1]
    row = lax.broadcasted_iota(jnp.int32, (EXTRA, BLOCKS), 0)
    passed = jnp.zeros((EXTRA, BLOCKS), jnp.float32)
    for k in range(4):
        for at, line in ((k * 4 + y, k), (x * 4 + k, 4 + k)):
            note = plane_ref[at, ROWS:, :BLOCKS].astype(jnp.float32)
            passed = jnp.where(row == line, note, passed)
    out_ref[:, :BLOCKS] = passed
    out_ref[:, BLOCKS:] = jnp.broadcast_to(seeds_ref[...], (EXTRA, ROWS))


def make_list(place_ref, notes_ref, list_v):
    x, y, zlo, core, zhi = (place_ref[k] for k in range(5))
    shape = (BLOCKS, BLOCKS)
    row = lax.broadcasted_iota(jnp.int32, shape, 0)
    lane = lax.broadcasted_iota(jnp.int32, shape, 1)
    u_zhi, u_x = row >> 6, (row >> 4) & 3
    v_zlo, v_core, v_y = (row >> 3) & 1, (row >> 2) & 1, row & 3
    a_zhi, a_y = lane >> 6, (lane >> 4) & 3
    b_zlo, b_x, b_core = (lane >> 3) & 1, (lane >> 1) & 3, lane & 1
    forward = (a_zhi == zhi) & (b_x == x) & (a_y == v_y) & (b_zlo == v_zlo) & (b_core == v_core)
    mirror = (a_zhi == u_zhi) & (a_y == y) & (b_zlo == zlo) & (b_x == u_x) & (b_core == core)
    ahead = []
    for u in range(GROUP):
        note = notes_ref[zlo * 8 + core * 4 + u // 4, u % 4 : u % 4 + 1, :BLOCKS]
        ahead.append(jnp.broadcast_to(note, (GROUP, BLOCKS)))
    back = [notes_ref[at * 4 + zhi, 4:8, :BLOCKS] for at in range(4)]
    ahead = jnp.concatenate(ahead, axis=0)
    back = jnp.concatenate(back * GROUP, axis=0)
    hits = jnp.where(forward, ahead, 0.0) + jnp.where(mirror, back, 0.0)
    counts = jnp.dot(
        hits.astype(jnp.bfloat16), jnp.ones(shape, jnp.bfloat16), preferred_element_type=jnp.float32
    )
    live = (counts > 0.0).astype(jnp.float32)
    upto = jnp.dot(
        (lane <= row).astype(jnp.float32).astype(jnp.bfloat16), live.astype(jnp.bfloat16),
        preferred_element_type=jnp.float32,
    )
    spot = jnp.where(lane.astype(jnp.float32) == upto - 1.0, live, 0.0)
    slot_lane = lax.broadcasted_iota(jnp.int32, (EXTRA, BLOCKS), 1)
    code = (
        (((slot_lane >> 4) & 3) * 4 + (slot_lane & 3)) * GROUP
        + ((slot_lane >> 3) & 1) * 8 + ((slot_lane >> 2) & 1) * 4 + (slot_lane >> 6)
    ).astype(jnp.float32).astype(jnp.bfloat16)
    ones = jnp.ones((EXTRA, BLOCKS), jnp.bfloat16)
    codes = jnp.dot(code, spot.astype(jnp.bfloat16), preferred_element_type=jnp.float32)
    weights = jnp.dot(ones, (spot * counts).astype(jnp.bfloat16), preferred_element_type=jnp.float32)
    found = jnp.dot(ones, live.astype(jnp.bfloat16), preferred_element_type=jnp.float32)
    line = lax.broadcasted_iota(jnp.int32, (EXTRA, BLOCKS), 0)
    table = jnp.where(line == 0, codes, jnp.where(line == 1, weights, found))
    list_v[...] = (table + 0.5).astype(jnp.int32)


def build_kernel(place_ref, notes_ref, plane_ref, own_ref, mate_ref, far_ref, far_mate_ref,
                 tiles_ref, list_ref, deg_ref, seeds_ref, line_v, sums, list_v, list_sem, line_sem):
    mine = place_ref[5]
    parts = [
        pltpu.make_async_copy(part, line_v.at[pl.ds(at * 4, 4)], line_sem)
        for at, part in enumerate((own_ref, mate_ref, far_ref, far_mate_ref))
    ]
    for part in parts:
        part.start()
    make_list(place_ref, notes_ref, list_v)
    list_copy = pltpu.make_async_copy(list_v, list_ref, list_sem)
    list_copy.start()
    for b in range(GROUP):
        seeds_ref[b : b + 1, :] = notes_ref[b, 0:1, BLOCKS:].astype(jnp.int32)
    sums[...] = jnp.zeros_like(sums)
    sharpness = FEAT**0.5
    diag_slot = place_ref[6]
    on_diag = (
        lax.broadcasted_iota(jnp.int32, (ROWS, ROWS), 0)
        == lax.broadcasted_iota(jnp.int32, (ROWS, ROWS), 1)
    ).astype(jnp.float32)
    list_copy.wait()
    for part in parts:
        part.wait()

    def build_chunk(group, carry):
        for k in range(CHUNK):
            at = group * CHUNK + k
            slot = list_ref[0, at]
            a, b = slot >> 4, slot & 15
            weight = list_ref[1, at].astype(jnp.float32)
            off = jnp.where(slot == diag_slot, weight, 0.0)
            scores = lax.dot_general(
                line_v[b ^ mine], plane_ref[a, :ROWS, :], (((1,), (1,)), ((), ())),
                preferred_element_type=jnp.float32,
            )
            tile = jnp.exp(sharpness * (scores - 1.0)) * (weight - on_diag * off)
            high = tile.astype(jnp.bfloat16)
            tiles_ref[at, :ROWS, :] = high
            tiles_ref[at, ROWS:, :] = (tile - high.astype(jnp.float32)).astype(jnp.bfloat16)
            sums[b] += tile
        return carry

    lax.fori_loop(0, (list_ref[2, 0] + CHUNK - 1) // CHUNK, build_chunk, 0)
    for b in range(GROUP):
        deg_ref[b : b + 1, :] = jnp.sum(sums[b].T, axis=0, keepdims=True)


def split_into(wide, b, spread):
    high = spread.astype(jnp.bfloat16)
    low = (spread - high.astype(jnp.float32)).astype(jnp.bfloat16)
    wide[b, :CLASSES, :ROWS] = high
    wide[b, :CLASSES, ROWS:] = high
    wide[b, CLASSES:, :ROWS] = low
    wide[b, CLASSES:, ROWS:] = jnp.zeros_like(low)


def run_apply(list_ref, tiles_ref, out_ref, total, wide):
    total[...] = jnp.zeros_like(total)

    def chunk_step(group, carry):
        for k in range(CHUNK):
            at = group * CHUNK + k
            slot = list_ref[0, at]
            both = jnp.dot(wide[slot & 15], tiles_ref[at], preferred_element_type=jnp.float32)
            total[slot >> 4] += both[:CLASSES] + both[CLASSES:]
        return carry

    lax.fori_loop(0, (list_ref[2, 0] + CHUNK - 1) // CHUNK, chunk_step, 0)
    out_ref[...] = total[...].astype(jnp.bfloat16)


def seeded_block(seeds_ref, b):
    classes = lax.broadcasted_iota(jnp.int32, (CLASSES, ROWS), 0)
    return classes == seeds_ref[b : b + 1, :]


def first_kernel(place_ref, list_ref, tiles_ref, seeds_ref, parts_ref,
                 out_ref, scale_ref, own_ref, total, wide):
    scale_ref[...] = lax.rsqrt(jnp.sum(parts_ref[...], axis=0))
    own_ref[...] = scale_ref[pl.ds(place_ref[5], 1), :]
    for b in range(GROUP):
        split_into(wide, b, jnp.where(seeded_block(seeds_ref, b), scale_ref[b : b + 1, :], 0.0))
    run_apply(list_ref, tiles_ref, out_ref, total, wide)


def next_kernel(list_ref, tiles_ref, seeds_ref, scale_ref, smooth_ref, out_ref, total, wide):
    for b in range(GROUP):
        seed_part = jnp.where(
            seeded_block(seeds_ref, b), (1.0 - BLEND) * scale_ref[b : b + 1, :], 0.0
        )
        split_into(wide, b, smooth_ref[b].astype(jnp.float32) + seed_part)
    run_apply(list_ref, tiles_ref, out_ref, total, wide)


def call(kernel, outs, ins, out_specs, scratch=(), limit=8):
    return pl.pallas_call(
        kernel,
        out_shape=outs,
        in_specs=ins,
        out_specs=out_specs,
        scratch_shapes=list(scratch),
        compiler_params=pltpu.CompilerParams(vmem_limit_bytes=limit << 20),
    )


def array(*shape, dtype=jnp.float32):
    return jax.ShapeDtypeStruct(shape, dtype)


def exchange(blocks, axes):
    return lax.all_to_all(blocks, axes, 0, 0)


def gather(block, axes):
    return exchange(jnp.broadcast_to(block[None], (GROUP,) + block.shape), axes)


def pairs(count, step):
    return [(k, k ^ step) for k in range(count)]


def local(embeddings, tile_list, seeds):
    x, y, zlo, core, zhi = (lax.axis_index(name) for name in ("x", "y", "zlo", "core", "zhi"))
    mine = zlo * 8 + core * 4 + zhi
    place = jnp.stack([x, y, zlo, core, zhi, mine, (x * 4 + y) * GROUP + mine]).astype(jnp.int32)
    block, noted, own_seeds = call(
        prep_kernel,
        (
            array(ROWS, FEAT, dtype=jnp.bfloat16),
            array(ROWS + EXTRA, FEAT, dtype=jnp.bfloat16),
            array(1, ROWS),
        ),
        [SMEM] + [VMEM] * 3,
        (VMEM,) * 3,
        limit=4,
    )(place, embeddings, tile_list.reshape(-1, 2).T, seeds[None, :])

    hops = [lax.ppermute(block, "zhi", pairs(4, step)) for step in (1, 2, 3)]
    plane = gather(noted, PLANE)
    own = jnp.stack([block] + hops)
    mate = lax.ppermute(own, "core", pairs(2, 1))
    far = lax.ppermute(own, "zlo", pairs(2, 1))
    note = call(
        relay_kernel, array(EXTRA, BLOCKS + ROWS), [SMEM, VMEM, VMEM], VMEM, limit=4
    )(place, plane, own_seeds)
    notes = gather(note, LINE)
    far_mate = lax.ppermute(far, "core", pairs(2, 1))

    tiles, listing, partial_degree, line_seeds = call(
        build_kernel,
        (
            array(BLOCKS, 2 * ROWS, ROWS, dtype=jnp.bfloat16),
            array(EXTRA, BLOCKS, dtype=jnp.int32),
            array(GROUP, ROWS),
            array(GROUP, ROWS, dtype=jnp.int32),
        ),
        [SMEM] + [VMEM] * 2 + [ANY] * 4,
        (VMEM, SMEM, VMEM, VMEM),
        (
            pltpu.VMEM((GROUP, ROWS, FEAT), jnp.bfloat16),
            pltpu.VMEM((GROUP, ROWS, ROWS), jnp.float32),
            pltpu.VMEM((EXTRA, BLOCKS), jnp.int32),
            pltpu.SemaphoreType.DMA,
            pltpu.SemaphoreType.DMA,
        ),
        limit=14,
    )(place, notes, plane, own, mate, far, far_mate)

    scratch = (
        pltpu.VMEM((GROUP, CLASSES, ROWS), jnp.float32),
        pltpu.VMEM((GROUP, 2 * CLASSES, 2 * ROWS), jnp.bfloat16),
    )
    sums_out = array(GROUP, CLASSES, ROWS, dtype=jnp.bfloat16)
    partial, scale, own_scale = call(
        first_kernel,
        (sums_out, array(GROUP, ROWS), array(1, ROWS)),
        [SMEM, SMEM, VMEM, VMEM, VMEM],
        (VMEM,) * 3,
        scratch,
        limit=6,
    )(place, listing, tiles, line_seeds, gather(partial_degree, LINE))
    for sweep in range(3):
        if sweep:
            smooth = gather((BLEND * own_scale * own_scale * summed).astype(jnp.bfloat16), LINE)
            partial = call(
                next_kernel, sums_out, [SMEM] + [VMEM] * 4, VMEM, scratch, limit=6
            )(listing, tiles, line_seeds, scale, smooth)
        summed, own_scale, seeds = lax.optimization_barrier((exchange(partial, PLANE), own_scale, seeds))
        summed = jnp.sum(summed.astype(jnp.float32), axis=0)
    seeded = seeds[None, :] == jnp.arange(CLASSES, dtype=jnp.int32)[:, None]
    labels = BLEND * own_scale * summed + (1.0 - BLEND) * seeded.astype(jnp.float32)
    return (CLASSES * labels).T


def solution(mesh):
    fine = Mesh(mesh.devices.reshape(SIZES), AXES)
    return jax.shard_map(
        local,
        mesh=fine,
        in_specs=(P(AXES, None), P(ROW, COL, None, None), P(AXES)),
        out_specs=P(AXES, None),
        check_vma=False,
    )
```

```python
import jax
import jax.numpy as jnp
from jax import lax
from jax.experimental import pallas as pl
from jax.experimental.pallas import tpu as pltpu
from jax.sharding import Mesh
from jax.sharding import PartitionSpec as P


CLASSES = 64
BLEND = 0.8
EPSILON = 1e-06
AXES = ("zlo", "x", "core", "zhi", "y")
SIZES = (2, 4, 2, 4, 4)
ROW = ("zlo", "x", "core")
COL = ("zhi", "y")
PLANE = ("x", "y")
LINE = ("zlo", "core", "zhi")
GROUP = 16
BLOCKS = GROUP * GROUP
ROWS = 128
FEAT = 768
EXTRA = 8
CHUNK = 8
VMEM = pl.BlockSpec(memory_space=pltpu.VMEM)
SMEM = pl.BlockSpec(memory_space=pltpu.SMEM)
ANY = pl.BlockSpec(memory_space=pl.ANY)


def prep_kernel(place_ref, emb_hbm, slots_hbm, seeds_hbm, block_ref, noted_ref, seeds_out,
                emb_ref, slots_ref, seeds_ref, emb_sem, slots_sem, seeds_sem):
    copies = [
        pltpu.make_async_copy(emb_hbm, emb_ref, emb_sem),
        pltpu.make_async_copy(slots_hbm, slots_ref, slots_sem),
        pltpu.make_async_copy(seeds_hbm, seeds_ref, seeds_sem),
    ]
    for copy in copies:
        copy.start()
    for copy in copies:
        copy.wait()
    features = emb_ref[...].astype(jnp.float32)
    norm = lax.rsqrt(jnp.sum(features * features, axis=1, keepdims=True) + EPSILON)
    normed = (features * norm).astype(jnp.bfloat16)
    block_ref[...] = normed
    noted_ref[:ROWS, :] = normed
    first, second = slots_ref[0:1, :], slots_ref[1:2, :]
    ids = jnp.where(first >= 0, first * GROUP + second, -1)
    hits = (lax.broadcasted_iota(jnp.int32, (BLOCKS, 32), 0) == ids).astype(jnp.float32)
    bits = lax.dot_general(
        jnp.ones((EXTRA, 32), jnp.float32), hits, (((1,), (1,)), ((), ())),
        preferred_element_type=jnp.float32,
    )
    noted_ref[ROWS:, :BLOCKS] = bits.astype(jnp.bfloat16)
    noted_ref[ROWS:, BLOCKS:] = jnp.zeros((EXTRA, FEAT - BLOCKS), jnp.bfloat16)
    seeds_out[...] = seeds_ref[...].astype(jnp.float32)


def relay_kernel(place_ref, plane_ref, seeds_ref, out_ref):
    x, y = place_ref[0], place_ref[1]
    row = lax.broadcasted_iota(jnp.int32, (EXTRA, BLOCKS), 0)
    passed = jnp.zeros((EXTRA, BLOCKS), jnp.float32)
    for k in range(4):
        for at, line in ((k * 4 + y, k), (x * 4 + k, 4 + k)):
            note = plane_ref[at, ROWS:, :BLOCKS].astype(jnp.float32)
            passed = jnp.where(row == line, note, passed)
    out_ref[:, :BLOCKS] = passed
    out_ref[:, BLOCKS:] = jnp.broadcast_to(seeds_ref[...], (EXTRA, ROWS))


def make_list(place_ref, notes_ref, list_v):
    x, y, zlo, core, zhi = (place_ref[k] for k in range(5))
    shape = (BLOCKS, BLOCKS)
    row = lax.broadcasted_iota(jnp.int32, shape, 0)
    lane = lax.broadcasted_iota(jnp.int32, shape, 1)
    u_zhi, u_x = row >> 6, (row >> 4) & 3
    v_zlo, v_core, v_y = (row >> 3) & 1, (row >> 2) & 1, row & 3
    a_zhi, a_y = lane >> 6, (lane >> 4) & 3
    b_zlo, b_x, b_core = (lane >> 3) & 1, (lane >> 1) & 3, lane & 1
    forward = (a_zhi == zhi) & (b_x == x) & (a_y == v_y) & (b_zlo == v_zlo) & (b_core == v_core)
    mirror = (a_zhi == u_zhi) & (a_y == y) & (b_zlo == zlo) & (b_x == u_x) & (b_core == core)
    ahead = []
    for u in range(GROUP):
        note = notes_ref[zlo * 8 + core * 4 + u // 4, u % 4 : u % 4 + 1, :BLOCKS]
        ahead.append(jnp.broadcast_to(note, (GROUP, BLOCKS)))
    back = [notes_ref[at * 4 + zhi, 4:8, :BLOCKS] for at in range(4)]
    ahead = jnp.concatenate(ahead, axis=0)
    back = jnp.concatenate(back * GROUP, axis=0)
    hits = jnp.where(forward, ahead, 0.0) + jnp.where(mirror, back, 0.0)
    counts = jnp.dot(
        hits.astype(jnp.bfloat16), jnp.ones(shape, jnp.bfloat16), preferred_element_type=jnp.float32
    )
    live = (counts > 0.0).astype(jnp.float32)
    upto = jnp.dot(
        (lane <= row).astype(jnp.float32).astype(jnp.bfloat16), live.astype(jnp.bfloat16),
        preferred_element_type=jnp.float32,
    )
    spot = jnp.where(lane.astype(jnp.float32) == upto - 1.0, live, 0.0)
    slot_lane = lax.broadcasted_iota(jnp.int32, (EXTRA, BLOCKS), 1)
    code = (
        (((slot_lane >> 4) & 3) * 4 + (slot_lane & 3)) * GROUP
        + ((slot_lane >> 3) & 1) * 8 + ((slot_lane >> 2) & 1) * 4 + (slot_lane >> 6)
    ).astype(jnp.float32).astype(jnp.bfloat16)
    ones = jnp.ones((EXTRA, BLOCKS), jnp.bfloat16)
    codes = jnp.dot(code, spot.astype(jnp.bfloat16), preferred_element_type=jnp.float32)
    weights = jnp.dot(ones, (spot * counts).astype(jnp.bfloat16), preferred_element_type=jnp.float32)
    found = jnp.dot(ones, live.astype(jnp.bfloat16), preferred_element_type=jnp.float32)
    line = lax.broadcasted_iota(jnp.int32, (EXTRA, BLOCKS), 0)
    table = jnp.where(line == 0, codes, jnp.where(line == 1, weights, found))
    list_v[...] = (table + 0.5).astype(jnp.int32)


def build_kernel(place_ref, notes_ref, plane_ref, own_ref, mate_ref, far_ref, far_mate_ref,
                 tiles_ref, list_ref, deg_ref, seeds_ref, line_v, sums, list_v, list_sem, line_sem):
    mine = place_ref[5]
    parts = [
        pltpu.make_async_copy(part, line_v.at[pl.ds(at * 4, 4)], line_sem)
        for at, part in enumerate((own_ref, mate_ref, far_ref, far_mate_ref))
    ]
    for part in parts:
        part.start()
    make_list(place_ref, notes_ref, list_v)
    list_copy = pltpu.make_async_copy(list_v, list_ref, list_sem)
    list_copy.start()
    for b in range(GROUP):
        seeds_ref[b : b + 1, :] = notes_ref[b, 0:1, BLOCKS:].astype(jnp.int32)
    sums[...] = jnp.zeros_like(sums)
    sharpness = FEAT**0.5
    diag_slot = place_ref[6]
    on_diag = (
        lax.broadcasted_iota(jnp.int32, (ROWS, ROWS), 0)
        == lax.broadcasted_iota(jnp.int32, (ROWS, ROWS), 1)
    ).astype(jnp.float32)
    list_copy.wait()
    for part in parts:
        part.wait()

    def build_chunk(group, carry):
        for k in range(CHUNK):
            at = group * CHUNK + k
            slot = list_ref[0, at]
            a, b = slot >> 4, slot & 15
            weight = list_ref[1, at].astype(jnp.float32)
            off = jnp.where(slot == diag_slot, weight, 0.0)
            scores = lax.dot_general(
                line_v[b ^ mine], plane_ref[a, :ROWS, :], (((1,), (1,)), ((), ())),
                preferred_element_type=jnp.float32,
            )
            tile = jnp.exp(sharpness * (scores - 1.0)) * (weight - on_diag * off)
            high = tile.astype(jnp.bfloat16)
            tiles_ref[at, :ROWS, :] = high
            tiles_ref[at, ROWS:, :] = (tile - high.astype(jnp.float32)).astype(jnp.bfloat16)
            sums[b] += tile
        return carry

    lax.fori_loop(0, (list_ref[2, 0] + CHUNK - 1) // CHUNK, build_chunk, 0)
    for b in range(GROUP):
        deg_ref[b : b + 1, :] = jnp.sum(sums[b].T, axis=0, keepdims=True)


def split_into(wide, b, spread):
    high = spread.astype(jnp.bfloat16)
    low = (spread - high.astype(jnp.float32)).astype(jnp.bfloat16)
    wide[b, :CLASSES, :ROWS] = high
    wide[b, :CLASSES, ROWS:] = high
    wide[b, CLASSES:, :ROWS] = low
    wide[b, CLASSES:, ROWS:] = jnp.zeros_like(low)


def run_apply(list_ref, tiles_ref, out_ref, total, wide):
    total[...] = jnp.zeros_like(total)

    def chunk_step(group, carry):
        for k in range(CHUNK):
            at = group * CHUNK + k
            slot = list_ref[0, at]
            both = jnp.dot(wide[slot & 15], tiles_ref[at], preferred_element_type=jnp.float32)
            total[slot >> 4] += both[:CLASSES] + both[CLASSES:]
        return carry

    lax.fori_loop(0, (list_ref[2, 0] + CHUNK - 1) // CHUNK, chunk_step, 0)
    out_ref[...] = total[...].astype(jnp.bfloat16)


def seeded_block(seeds_ref, b):
    classes = lax.broadcasted_iota(jnp.int32, (CLASSES, ROWS), 0)
    return classes == seeds_ref[b : b + 1, :]


def first_kernel(place_ref, list_ref, tiles_ref, seeds_ref, parts_ref,
                 out_ref, scale_ref, own_ref, total, wide):
    scale_ref[...] = lax.rsqrt(jnp.sum(parts_ref[...], axis=0))
    own_ref[...] = scale_ref[pl.ds(place_ref[5], 1), :]
    for b in range(GROUP):
        split_into(wide, b, jnp.where(seeded_block(seeds_ref, b), scale_ref[b : b + 1, :], 0.0))
    run_apply(list_ref, tiles_ref, out_ref, total, wide)


def next_kernel(list_ref, tiles_ref, seeds_ref, scale_ref, smooth_ref, out_ref, total, wide):
    for b in range(GROUP):
        seed_part = jnp.where(
            seeded_block(seeds_ref, b), (1.0 - BLEND) * scale_ref[b : b + 1, :], 0.0
        )
        split_into(wide, b, smooth_ref[b].astype(jnp.float32) + seed_part)
    run_apply(list_ref, tiles_ref, out_ref, total, wide)


def call(kernel, outs, ins, out_specs, scratch=(), limit=8):
    return pl.pallas_call(
        kernel,
        out_shape=outs,
        in_specs=ins,
        out_specs=out_specs,
        scratch_shapes=list(scratch),
        compiler_params=pltpu.CompilerParams(vmem_limit_bytes=limit << 20),
    )


def array(*shape, dtype=jnp.float32):
    return jax.ShapeDtypeStruct(shape, dtype)


def exchange(blocks, axes):
    return lax.all_to_all(blocks, axes, 0, 0)


def gather(block, axes):
    return exchange(jnp.broadcast_to(block[None], (GROUP,) + block.shape), axes)


def pairs(count, step):
    return [(k, k ^ step) for k in range(count)]


def local(embeddings, tile_list, seeds):
    x, y, zlo, core, zhi = (lax.axis_index(name) for name in ("x", "y", "zlo", "core", "zhi"))
    mine = zlo * 8 + core * 4 + zhi
    place = jnp.stack([x, y, zlo, core, zhi, mine, (x * 4 + y) * GROUP + mine]).astype(jnp.int32)
    block, noted, own_seeds = call(
        prep_kernel,
        (
            array(ROWS, FEAT, dtype=jnp.bfloat16),
            array(ROWS + EXTRA, FEAT, dtype=jnp.bfloat16),
            array(1, ROWS),
        ),
        [SMEM] + [ANY] * 3,
        (VMEM,) * 3,
        (
            pltpu.VMEM((ROWS, FEAT), jnp.bfloat16),
            pltpu.VMEM((2, 32), jnp.int32),
            pltpu.VMEM((1, ROWS), jnp.int32),
        )
        + (pltpu.SemaphoreType.DMA,) * 3,
        limit=62,
    )(place, embeddings, tile_list.reshape(-1, 2).T, seeds[None, :])

    hops = []
    for step in (1, 2, 3):
        hops.append(lax.ppermute(block, "zhi", pairs(4, step)))
    plane = gather(noted, PLANE)
    own = jnp.stack([block] + hops)
    mate = lax.ppermute(own, "core", pairs(2, 1))
    far = lax.ppermute(own, "zlo", pairs(2, 1))
    note = call(
        relay_kernel, array(EXTRA, BLOCKS + ROWS), [SMEM, VMEM, VMEM], VMEM, limit=4
    )(place, plane, own_seeds)
    notes = gather(note, LINE)
    far, notes = lax.optimization_barrier((far, notes))
    far_mate = lax.ppermute(far, "core", pairs(2, 1))

    tiles, listing, partial_degree, line_seeds = call(
        build_kernel,
        (
            array(BLOCKS, 2 * ROWS, ROWS, dtype=jnp.bfloat16),
            array(EXTRA, BLOCKS, dtype=jnp.int32),
            array(GROUP, ROWS),
            array(GROUP, ROWS, dtype=jnp.int32),
        ),
        [SMEM] + [VMEM] * 2 + [ANY] * 4,
        (VMEM, SMEM, VMEM, VMEM),
        (
            pltpu.VMEM((GROUP, ROWS, FEAT), jnp.bfloat16),
            pltpu.VMEM((GROUP, ROWS, ROWS), jnp.float32),
            pltpu.VMEM((EXTRA, BLOCKS), jnp.int32),
            pltpu.SemaphoreType.DMA,
            pltpu.SemaphoreType.DMA,
        ),
        limit=14,
    )(place, notes, plane, own, mate, far, far_mate)

    scratch = (
        pltpu.VMEM((GROUP, CLASSES, ROWS), jnp.float32),
        pltpu.VMEM((GROUP, 2 * CLASSES, 2 * ROWS), jnp.bfloat16),
    )
    sums_out = array(GROUP, CLASSES, ROWS, dtype=jnp.bfloat16)
    partial, scale, own_scale = call(
        first_kernel,
        (sums_out, array(GROUP, ROWS), array(1, ROWS)),
        [SMEM, SMEM, VMEM, VMEM, VMEM],
        (VMEM,) * 3,
        scratch,
        limit=6,
    )(place, listing, tiles, line_seeds, gather(partial_degree, LINE))
    for sweep in range(3):
        if sweep:
            smooth = gather((BLEND * own_scale * own_scale * summed).astype(jnp.bfloat16), LINE)
            partial = call(
                next_kernel, sums_out, [SMEM] + [VMEM] * 4, VMEM, scratch, limit=6
            )(listing, tiles, line_seeds, scale, smooth)
        summed, own_scale, seeds = lax.optimization_barrier((exchange(partial, PLANE), own_scale, seeds))
        summed = jnp.sum(summed.astype(jnp.float32), axis=0)
    seeded = seeds[None, :] == jnp.arange(CLASSES, dtype=jnp.int32)[:, None]
    labels = BLEND * own_scale * summed + (1.0 - BLEND) * seeded.astype(jnp.float32)
    return (CLASSES * labels).T


def solution(mesh):
    fine = Mesh(mesh.devices.reshape(SIZES), AXES)
    return jax.shard_map(
        local,
        mesh=fine,
        in_specs=(P(AXES, None), P(ROW, COL, None, None), P(AXES)),
        out_specs=P(AXES, None),
        check_vma=False,
    )
```

```python
import jax
import jax.numpy as jnp
from jax import lax
from jax.experimental import pallas as pl
from jax.experimental.pallas import tpu as pltpu
from jax.sharding import Mesh
from jax.sharding import PartitionSpec as P

CLASSES = 64
BLEND = 0.8
EPSILON = 1e-06
AXES = ("zlo", "x", "core", "zhi", "y")
SIZES = (2, 4, 2, 4, 4)
ROW = ("zlo", "x", "core")
COL = ("zhi", "y")
PLANE = ("x", "y")
LINE = ("zlo", "core", "zhi")
GROUP = 16
BLOCKS = GROUP * GROUP
ROWS = 128
FEAT = 768
EXTRA = 8
CHUNK = 8
VMEM = pl.BlockSpec(memory_space=pltpu.VMEM)
SMEM = pl.BlockSpec(memory_space=pltpu.SMEM)
ANY = pl.BlockSpec(memory_space=pl.ANY)


def prep_kernel(emb_hbm, slots_hbm, block_ref, bits_ref, emb_ref, slots_ref, emb_sem, slots_sem):
    copies = [
        pltpu.make_async_copy(emb_hbm, emb_ref, emb_sem),
        pltpu.make_async_copy(slots_hbm, slots_ref, slots_sem),
    ]
    for copy in copies:
        copy.start()
    for copy in copies:
        copy.wait()
    features = emb_ref[...].astype(jnp.float32)
    norm = lax.rsqrt(jnp.sum(features * features, axis=1, keepdims=True) + EPSILON)
    block_ref[...] = (features * norm).astype(jnp.bfloat16)
    first, second = slots_ref[0:1, :], slots_ref[1:2, :]
    ids = jnp.where(first >= 0, first * GROUP + second, -1)
    hits = (lax.broadcasted_iota(jnp.int32, (BLOCKS, 32), 0) == ids).astype(jnp.float32)
    bits = lax.dot_general(
        jnp.ones((EXTRA, 32), jnp.float32), hits, (((1,), (1,)), ((), ())),
        preferred_element_type=jnp.float32,
    )
    bits_ref[...] = bits[0:1]


def make_list(place_ref, ahead_ref, back_ref, list_v):
    x, y, zlo, core, zhi = (place_ref[k] for k in range(5))
    shape = (BLOCKS, BLOCKS)
    row = lax.broadcasted_iota(jnp.int32, shape, 0)
    lane = lax.broadcasted_iota(jnp.int32, shape, 1)
    u_zhi, u_x = (row >> 6) ^ zhi, ((row >> 4) & 3) ^ x
    v_zlo, v_core, v_y = ((row >> 3) & 1) ^ zlo, ((row >> 2) & 1) ^ core, (row & 3) ^ y
    a_zhi, a_y = lane >> 6, (lane >> 4) & 3
    b_zlo, b_x, b_core = (lane >> 3) & 1, (lane >> 1) & 3, lane & 1
    forward = (a_zhi == zhi) & (b_x == x) & (a_y == v_y) & (b_zlo == v_zlo) & (b_core == v_core)
    mirror = (a_zhi == u_zhi) & (a_y == y) & (b_zlo == zlo) & (b_x == u_x) & (b_core == core)
    ahead = jnp.concatenate(
        [jnp.broadcast_to(ahead_ref[u : u + 1, :], (GROUP, BLOCKS)) for u in range(GROUP)], axis=0
    )
    back = jnp.concatenate([back_ref[...]] * GROUP, axis=0)
    hits = jnp.where(forward, ahead, 0.0) + jnp.where(mirror, back, 0.0)
    counts = jnp.dot(
        hits.astype(jnp.bfloat16), jnp.ones(shape, jnp.bfloat16), preferred_element_type=jnp.float32
    )
    live = (counts > 0.0).astype(jnp.float32)
    upto = jnp.dot(
        (lane <= row).astype(jnp.float32).astype(jnp.bfloat16), live.astype(jnp.bfloat16),
        preferred_element_type=jnp.float32,
    )
    spot = jnp.where(lane.astype(jnp.float32) == upto - 1.0, live, 0.0)
    slot_lane = lax.broadcasted_iota(jnp.int32, (EXTRA, BLOCKS), 1)
    code = (
        (((slot_lane >> 4) & 3) * 4 + (slot_lane & 3)) * GROUP
        + ((slot_lane >> 3) & 1) * 8 + ((slot_lane >> 2) & 1) * 4 + (slot_lane >> 6)
    )
    code = (code ^ ((x * 4 + y) * GROUP + place_ref[5])).astype(jnp.float32).astype(jnp.bfloat16)
    ones = jnp.ones((EXTRA, BLOCKS), jnp.bfloat16)
    codes = jnp.dot(code, spot.astype(jnp.bfloat16), preferred_element_type=jnp.float32)
    weights = jnp.dot(ones, (spot * counts).astype(jnp.bfloat16), preferred_element_type=jnp.float32)
    found = jnp.dot(ones, live.astype(jnp.bfloat16), preferred_element_type=jnp.float32)
    line = lax.broadcasted_iota(jnp.int32, (EXTRA, BLOCKS), 0)
    table = jnp.where(line == 0, codes, jnp.where(line == 1, weights, found))
    list_v[...] = (table + 0.5).astype(jnp.int32)


def build_kernel(place_ref, ahead_ref, back_ref, seeds_ref, plane_ref, own_ref, mate_ref, far_ref, far_mate_ref,
                 tiles_ref, list_ref, deg_ref, line_v, sums, list_v, list_sem, line_sem):
    mine = place_ref[5]
    parts = [
        pltpu.make_async_copy(part, line_v.at[pl.ds(at * 4, 4)], line_sem)
        for at, part in enumerate((own_ref, mate_ref, far_ref, far_mate_ref))
    ]
    for part in parts:
        part.start()
    make_list(place_ref, ahead_ref, back_ref, list_v)
    list_copy = pltpu.make_async_copy(list_v, list_ref, list_sem)
    list_copy.start()
    sums[...] = jnp.zeros_like(sums)
    sharpness = FEAT**0.5
    diag_slot = place_ref[6]
    on_diag = (
        lax.broadcasted_iota(jnp.int32, (ROWS, ROWS), 0)
        == lax.broadcasted_iota(jnp.int32, (ROWS, ROWS), 1)
    ).astype(jnp.float32)
    list_copy.wait()
    for part in parts:
        part.wait()

    def build_chunk(group, carry):
        for k in range(CHUNK):
            at = group * CHUNK + k
            slot = list_ref[0, at]
            a, b = slot >> 4, slot & 15
            weight = list_ref[1, at].astype(jnp.float32)
            off = jnp.where(slot == diag_slot, weight, 0.0)
            scores = lax.dot_general(
                line_v[b ^ mine], plane_ref[a], (((1,), (1,)), ((), ())),
                preferred_element_type=jnp.float32,
            )
            tile = jnp.exp(sharpness * (scores - 1.0)) * (weight - on_diag * off)
            high = tile.astype(jnp.bfloat16)
            tiles_ref[at, :ROWS, :] = high
            tiles_ref[at, ROWS:, :] = (tile - high.astype(jnp.float32)).astype(jnp.bfloat16)
            sums[b] += tile
        return carry

    lax.fori_loop(0, (list_ref[2, 0] + CHUNK - 1) // CHUNK, build_chunk, 0)
    for b in range(GROUP):
        deg_ref[b : b + 1, :] = jnp.sum(sums[b].T, axis=0, keepdims=True)
    deg_ref[GROUP:, :] = jnp.broadcast_to(seeds_ref[...].astype(jnp.float32), (EXTRA, ROWS))


def split_into(wide, b, spread):
    high = spread.astype(jnp.bfloat16)
    low = (spread - high.astype(jnp.float32)).astype(jnp.bfloat16)
    wide[b, :CLASSES, :ROWS] = high
    wide[b, :CLASSES, ROWS:] = high
    wide[b, CLASSES:, :ROWS] = low
    wide[b, CLASSES:, ROWS:] = jnp.zeros_like(low)


def run_apply(list_ref, tiles_ref, out_ref, total, wide):
    total[...] = jnp.zeros_like(total)

    def chunk_step(group, carry):
        for k in range(CHUNK):
            at = group * CHUNK + k
            slot = list_ref[0, at]
            both = jnp.dot(wide[slot & 15], tiles_ref[at], preferred_element_type=jnp.float32)
            total[slot >> 4] += both[:CLASSES] + both[CLASSES:]
        return carry

    lax.fori_loop(0, (list_ref[2, 0] + CHUNK - 1) // CHUNK, chunk_step, 0)
    out_ref[...] = total[...].astype(jnp.bfloat16)


def seeded_block(seeds_ref, b):
    classes = lax.broadcasted_iota(jnp.int32, (CLASSES, ROWS), 0)
    return classes == seeds_ref[b : b + 1, :]


def first_kernel(place_ref, list_ref, tiles_ref, parts_ref,
                 out_ref, scale_ref, own_ref, seeds_ref, total, wide):
    scale_ref[...] = lax.rsqrt(jnp.sum(parts_ref[:, :GROUP, :], axis=0))
    for b in range(GROUP):
        seeds_ref[b : b + 1, :] = parts_ref[b, GROUP : GROUP + 1, :].astype(jnp.int32)
    own_ref[...] = scale_ref[pl.ds(place_ref[5], 1), :]
    for b in range(GROUP):
        split_into(wide, b, jnp.where(seeded_block(seeds_ref, b), scale_ref[b : b + 1, :], 0.0))
    run_apply(list_ref, tiles_ref, out_ref, total, wide)


def next_kernel(list_ref, tiles_ref, seeds_ref, scale_ref, smooth_ref, out_ref, total, wide):
    for b in range(GROUP):
        seed_part = jnp.where(
            seeded_block(seeds_ref, b), (1.0 - BLEND) * scale_ref[b : b + 1, :], 0.0
        )
        split_into(wide, b, smooth_ref[b].astype(jnp.float32) + seed_part)
    run_apply(list_ref, tiles_ref, out_ref, total, wide)


def call(kernel, outs, ins, out_specs, scratch=(), limit=8):
    return pl.pallas_call(
        kernel,
        out_shape=outs,
        in_specs=ins,
        out_specs=out_specs,
        scratch_shapes=list(scratch),
        compiler_params=pltpu.CompilerParams(vmem_limit_bytes=limit << 20),
    )


def array(*shape, dtype=jnp.float32):
    return jax.ShapeDtypeStruct(shape, dtype)


def exchange(blocks, axes):
    return lax.all_to_all(blocks, axes, 0, 0)


def gather(block, axes):
    return exchange(jnp.broadcast_to(block[None], (GROUP,) + block.shape), axes)


def pairs(count, step):
    return [(k, k ^ step) for k in range(count)]


def doubling(rows, steps):
    for axis, count, step in steps:
        rows = jnp.concatenate([rows, lax.ppermute(rows, axis, pairs(count, step))], axis=0)
    return rows


def local(embeddings, tile_list, seeds):
    x, y, zlo, core, zhi = (lax.axis_index(name) for name in ("x", "y", "zlo", "core", "zhi"))
    mine = zlo * 8 + core * 4 + zhi
    place = jnp.stack([x, y, zlo, core, zhi, mine, (x * 4 + y) * GROUP + mine]).astype(jnp.int32)
    block, bits = call(
        prep_kernel,
        (array(ROWS, FEAT, dtype=jnp.bfloat16), array(1, BLOCKS)),
        [ANY] * 2,
        (VMEM,) * 2,
        (
            pltpu.VMEM((ROWS, FEAT), jnp.bfloat16),
            pltpu.VMEM((2, 32), jnp.int32),
            pltpu.SemaphoreType.DMA,
            pltpu.SemaphoreType.DMA,
        ),
        limit=60,
    )(embeddings, tile_list.reshape(-1, 2).T)

    plane = gather(block, PLANE)
    hops = [lax.ppermute(block, "zhi", pairs(4, step)) for step in (1, 2, 3)]
    ahead = doubling(bits, (("x", 4, 1), ("x", 4, 2)))
    back = doubling(bits, (("y", 4, 1), ("y", 4, 2)))
    hops, ahead, back = lax.optimization_barrier((hops, ahead, back))
    own = jnp.stack([block] + hops)
    mate = lax.ppermute(own, "core", pairs(2, 1))
    far = lax.ppermute(own, "zlo", pairs(2, 1))
    ahead = doubling(ahead, (("zhi", 4, 1), ("zhi", 4, 2)))
    back = doubling(back, (("core", 2, 1), ("zlo", 2, 1)))
    far, ahead, back = lax.optimization_barrier((far, ahead, back))
    far_mate = lax.ppermute(far, "core", pairs(2, 1))

    tiles, listing, parts = call(
        build_kernel,
        (
            array(BLOCKS, 2 * ROWS, ROWS, dtype=jnp.bfloat16),
            array(EXTRA, BLOCKS, dtype=jnp.int32),
            array(GROUP + EXTRA, ROWS),
        ),
        [SMEM] + [VMEM] * 4 + [ANY] * 4,
        (VMEM, SMEM, VMEM),
        (
            pltpu.VMEM((GROUP, ROWS, FEAT), jnp.bfloat16),
            pltpu.VMEM((GROUP, ROWS, ROWS), jnp.float32),
            pltpu.VMEM((EXTRA, BLOCKS), jnp.int32),
            pltpu.SemaphoreType.DMA,
            pltpu.SemaphoreType.DMA,
        ),
        limit=14,
    )(place, ahead, back, seeds[None, :], plane, own, mate, far, far_mate)

    scratch = (
        pltpu.VMEM((GROUP, CLASSES, ROWS), jnp.float32),
        pltpu.VMEM((GROUP, 2 * CLASSES, 2 * ROWS), jnp.bfloat16),
    )
    sums_out = array(GROUP, CLASSES, ROWS, dtype=jnp.bfloat16)
    partial, scale, own_scale, line_seeds = call(
        first_kernel,
        (sums_out, array(GROUP, ROWS), array(1, ROWS), array(GROUP, ROWS, dtype=jnp.int32)),
        [SMEM, SMEM, VMEM, VMEM],
        (VMEM,) * 4,
        scratch,
        limit=6,
    )(place, listing, tiles, gather(parts, LINE))
    for sweep in range(3):
        if sweep:
            smooth = gather((BLEND * own_scale * own_scale * summed).astype(jnp.bfloat16), LINE)
            partial = call(
                next_kernel, sums_out, [SMEM] + [VMEM] * 4, VMEM, scratch, limit=6
            )(listing, tiles, line_seeds, scale, smooth)
        summed, own_scale, seeds = lax.optimization_barrier((exchange(partial, PLANE), own_scale, seeds))
        summed = jnp.sum(summed.astype(jnp.float32), axis=0)
    seeded = seeds[None, :] == jnp.arange(CLASSES, dtype=jnp.int32)[:, None]
    labels = BLEND * own_scale * summed + (1.0 - BLEND) * seeded.astype(jnp.float32)
    return (CLASSES * labels).T


def solution(mesh):
    fine = Mesh(mesh.devices.reshape(SIZES), AXES)
    return jax.shard_map(
        local,
        mesh=fine,
        in_specs=(P(AXES, None), P(ROW, COL, None, None), P(AXES)),
        out_specs=P(AXES, None),
        check_vma=False,
    )
```

```python
import jax
import jax.numpy as jnp
from jax import lax
from jax.experimental import pallas as pl
from jax.experimental.pallas import tpu as pltpu
from jax.sharding import Mesh
from jax.sharding import PartitionSpec as P

CLASSES = 64
BLEND = 0.8
EPSILON = 1e-06
AXES = ("zlo", "x", "core", "zhi", "y")
SIZES = (2, 4, 2, 4, 4)
ROW = ("zlo", "x", "core")
COL = ("zhi", "y")
PLANE = ("x", "y")
LINE = ("zlo", "core", "zhi")
GROUP = 16
BLOCKS = GROUP * GROUP
ROWS = 128
FEAT = 768
EXTRA = 8
FOLDS = FEAT // ROWS
CHUNK = 8
VMEM = pl.BlockSpec(memory_space=pltpu.VMEM)
SMEM = pl.BlockSpec(memory_space=pltpu.SMEM)
ANY = pl.BlockSpec(memory_space=pl.ANY)


def prep_kernel(emb_hbm, slots_hbm, seeds_hbm, block_ref, folded_ref, seeds_out,
                emb_ref, slots_ref, seeds_ref, emb_sem, slots_sem, seeds_sem):
    copies = [
        pltpu.make_async_copy(emb_hbm, emb_ref, emb_sem),
        pltpu.make_async_copy(slots_hbm, slots_ref, slots_sem),
        pltpu.make_async_copy(seeds_hbm, seeds_ref, seeds_sem),
    ]
    for copy in copies:
        copy.start()
    for copy in copies:
        copy.wait()
    features = emb_ref[...].astype(jnp.float32)
    norm = lax.rsqrt(jnp.sum(features * features, axis=1, keepdims=True) + EPSILON)
    normed = (features * norm).astype(jnp.bfloat16)
    block_ref[...] = normed
    for k in range(FOLDS):
        folded_ref[k * ROWS : (k + 1) * ROWS, :] = normed[:, k * ROWS : (k + 1) * ROWS]
    first, second = slots_ref[0:1, :], slots_ref[1:2, :]
    ids = jnp.where(first >= 0, first * GROUP + second, -1)
    hits = (lax.broadcasted_iota(jnp.int32, (BLOCKS, 32), 0) == ids).astype(jnp.float32)
    bits = lax.dot_general(
        jnp.ones((EXTRA, 32), jnp.float32), hits, (((1,), (1,)), ((), ())),
        preferred_element_type=jnp.float32,
    )
    row = lax.broadcasted_iota(jnp.int32, (EXTRA, ROWS), 0)
    folded_ref[FEAT:, :] = jnp.where(row < 4, bits[:, :ROWS], bits[:, ROWS:]).astype(jnp.bfloat16)
    seeds_out[...] = seeds_ref[...].astype(jnp.float32)


def relay_kernel(place_ref, plane_ref, seeds_ref, out_ref):
    x, y = place_ref[0], place_ref[1]
    row = lax.broadcasted_iota(jnp.int32, (EXTRA, BLOCKS), 0)
    passed = jnp.zeros((EXTRA, BLOCKS), jnp.float32)
    for k in range(4):
        for at, line in ((k * 4 + y, k), (x * 4 + k, 4 + k)):
            note = plane_ref[at, FEAT:, :].astype(jnp.float32)
            note = jnp.concatenate([note[0:1], note[4:5]], axis=1)
            passed = jnp.where(row == line, note, passed)
    out_ref[:, :BLOCKS] = passed
    out_ref[:, BLOCKS:] = jnp.broadcast_to(seeds_ref[...], (EXTRA, ROWS))


def make_list(place_ref, notes_ref, list_v):
    x, y, zlo, core, zhi = (place_ref[k] for k in range(5))
    shape = (BLOCKS, BLOCKS)
    row = lax.broadcasted_iota(jnp.int32, shape, 0)
    lane = lax.broadcasted_iota(jnp.int32, shape, 1)
    u_zhi, u_x = row >> 6, (row >> 4) & 3
    v_zlo, v_core, v_y = (row >> 3) & 1, (row >> 2) & 1, row & 3
    a_zhi, a_y = lane >> 6, (lane >> 4) & 3
    b_zlo, b_x, b_core = (lane >> 3) & 1, (lane >> 1) & 3, lane & 1
    forward = (a_zhi == zhi) & (b_x == x) & (a_y == v_y) & (b_zlo == v_zlo) & (b_core == v_core)
    mirror = (a_zhi == u_zhi) & (a_y == y) & (b_zlo == zlo) & (b_x == u_x) & (b_core == core)
    ahead = []
    for u in range(GROUP):
        note = notes_ref[zlo * 8 + core * 4 + u // 4, u % 4 : u % 4 + 1, :BLOCKS]
        ahead.append(jnp.broadcast_to(note, (GROUP, BLOCKS)))
    back = [notes_ref[at * 4 + zhi, 4:8, :BLOCKS] for at in range(4)]
    ahead = jnp.concatenate(ahead, axis=0)
    back = jnp.concatenate(back * GROUP, axis=0)
    hits = jnp.where(forward, ahead, 0.0) + jnp.where(mirror, back, 0.0)
    counts = jnp.dot(
        hits.astype(jnp.bfloat16), jnp.ones(shape, jnp.bfloat16), preferred_element_type=jnp.float32
    )
    live = (counts > 0.0).astype(jnp.float32)
    upto = jnp.dot(
        (lane <= row).astype(jnp.float32).astype(jnp.bfloat16), live.astype(jnp.bfloat16),
        preferred_element_type=jnp.float32,
    )
    spot = jnp.where(lane.astype(jnp.float32) == upto - 1.0, live, 0.0)
    slot_lane = lax.broadcasted_iota(jnp.int32, (EXTRA, BLOCKS), 1)
    code = (
        (((slot_lane >> 4) & 3) * 4 + (slot_lane & 3)) * GROUP
        + ((slot_lane >> 3) & 1) * 8 + ((slot_lane >> 2) & 1) * 4 + (slot_lane >> 6)
    ).astype(jnp.float32).astype(jnp.bfloat16)
    ones = jnp.ones((EXTRA, BLOCKS), jnp.bfloat16)
    codes = jnp.dot(code, spot.astype(jnp.bfloat16), preferred_element_type=jnp.float32)
    weights = jnp.dot(ones, (spot * counts).astype(jnp.bfloat16), preferred_element_type=jnp.float32)
    found = jnp.dot(ones, live.astype(jnp.bfloat16), preferred_element_type=jnp.float32)
    line = lax.broadcasted_iota(jnp.int32, (EXTRA, BLOCKS), 0)
    table = jnp.where(line == 0, codes, jnp.where(line == 1, weights, found))
    list_v[...] = (table + 0.5).astype(jnp.int32)


def build_kernel(place_ref, notes_ref, plane_ref, own_ref, mate_ref, far_ref, far_mate_ref,
                 tiles_ref, list_ref, deg_ref, seeds_ref, line_v, sums, list_v, list_sem, line_sem):
    planes = place_ref[5] & 12
    parts = [
        pltpu.make_async_copy(part, line_v.at[pl.ds(at * 4, 4)], line_sem)
        for at, part in enumerate((own_ref, mate_ref, far_ref, far_mate_ref))
    ]
    for part in parts:
        part.start()
    make_list(place_ref, notes_ref, list_v)
    list_copy = pltpu.make_async_copy(list_v, list_ref, list_sem)
    list_copy.start()
    for b in range(GROUP):
        seeds_ref[b : b + 1, :] = notes_ref[b, 0:1, BLOCKS:].astype(jnp.int32)
    sums[...] = jnp.zeros_like(sums)
    sharpness = FEAT**0.5
    diag_slot = place_ref[6]
    on_diag = (
        lax.broadcasted_iota(jnp.int32, (ROWS, ROWS), 0)
        == lax.broadcasted_iota(jnp.int32, (ROWS, ROWS), 1)
    ).astype(jnp.float32)
    list_copy.wait()
    for part in parts:
        part.wait()

    def build_chunk(group, carry):
        for k in range(CHUNK):
            at = group * CHUNK + k
            slot = list_ref[0, at]
            a, b = slot >> 4, slot & 15
            weight = list_ref[1, at].astype(jnp.float32)
            off = jnp.where(slot == diag_slot, weight, 0.0)
            left = jnp.concatenate(
                [plane_ref[a, f * ROWS : (f + 1) * ROWS, :] for f in range(FOLDS)], axis=1
            )
            scores = lax.dot_general(
                line_v[b ^ planes], left, (((1,), (1,)), ((), ())),
                preferred_element_type=jnp.float32,
            )
            tile = jnp.exp(sharpness * (scores - 1.0)) * (weight - on_diag * off)
            tiles_ref[at] = tile.astype(jnp.bfloat16)
            sums[b] += tile
        return carry

    lax.fori_loop(0, (list_ref[2, 0] + CHUNK - 1) // CHUNK, build_chunk, 0)
    for b in range(GROUP):
        deg_ref[b : b + 1, :] = jnp.sum(sums[b].T, axis=0, keepdims=True)


def run_apply(list_ref, tiles_ref, out_ref, total, spread):
    total[...] = jnp.zeros_like(total)

    def chunk_step(group, carry):
        for k in range(CHUNK):
            at = group * CHUNK + k
            slot = list_ref[0, at]
            total[slot >> 4] += jnp.dot(
                spread[slot & 15], tiles_ref[at], preferred_element_type=jnp.float32
            )
        return carry

    lax.fori_loop(0, (list_ref[2, 0] + CHUNK - 1) // CHUNK, chunk_step, 0)
    out_ref[...] = total[...].astype(jnp.bfloat16)


def seeded_block(seeds_ref, b):
    classes = lax.broadcasted_iota(jnp.int32, (CLASSES, ROWS), 0)
    return classes == seeds_ref[b : b + 1, :]


def first_kernel(place_ref, list_ref, tiles_ref, seeds_ref, parts_ref,
                 out_ref, scale_ref, own_ref, total, spread):
    scale_ref[...] = lax.rsqrt(jnp.sum(parts_ref[...], axis=0))
    own_ref[...] = scale_ref[pl.ds(place_ref[5], 1), :]
    for b in range(GROUP):
        seeded = jnp.where(seeded_block(seeds_ref, b), scale_ref[b : b + 1, :], 0.0)
        spread[b] = seeded.astype(jnp.bfloat16)
    run_apply(list_ref, tiles_ref, out_ref, total, spread)


def next_kernel(list_ref, tiles_ref, seeds_ref, scale_ref, smooth_ref, out_ref, total, spread):
    for b in range(GROUP):
        seed_part = jnp.where(
            seeded_block(seeds_ref, b), (1.0 - BLEND) * scale_ref[b : b + 1, :], 0.0
        )
        spread[b] = (smooth_ref[b].astype(jnp.float32) + seed_part).astype(jnp.bfloat16)
    run_apply(list_ref, tiles_ref, out_ref, total, spread)


def call(kernel, outs, ins, out_specs, scratch=(), limit=8):
    return pl.pallas_call(
        kernel,
        out_shape=outs,
        in_specs=ins,
        out_specs=out_specs,
        scratch_shapes=list(scratch),
        compiler_params=pltpu.CompilerParams(vmem_limit_bytes=limit << 20),
    )


def array(*shape, dtype=jnp.float32):
    return jax.ShapeDtypeStruct(shape, dtype)


def exchange(blocks, axes):
    return lax.all_to_all(blocks, axes, 0, 0)


def gather(block, axes):
    return exchange(jnp.broadcast_to(block[None], (GROUP,) + block.shape), axes)


def pairs(count, step):
    return [(k, k ^ step) for k in range(count)]


def local(embeddings, tile_list, seeds):
    x, y, zlo, core, zhi = (lax.axis_index(name) for name in ("x", "y", "zlo", "core", "zhi"))
    mine = zlo * 8 + core * 4 + zhi
    place = jnp.stack([x, y, zlo, core, zhi, mine, (x * 4 + y) * GROUP + mine]).astype(jnp.int32)
    block, folded, own_seeds = call(
        prep_kernel,
        (
            array(ROWS, FEAT, dtype=jnp.bfloat16),
            array(FEAT + EXTRA, ROWS, dtype=jnp.bfloat16),
            array(1, ROWS),
        ),
        [ANY] * 3,
        (VMEM,) * 3,
        (
            pltpu.VMEM((ROWS, FEAT), jnp.bfloat16),
            pltpu.VMEM((2, 32), jnp.int32),
            pltpu.VMEM((1, ROWS), jnp.int32),
        )
        + (pltpu.SemaphoreType.DMA,) * 3,
        limit=60,
    )(embeddings, tile_list.reshape(-1, 2).T, seeds[None, :])

    plane = gather(folded, PLANE)
    own = lax.all_gather(block, "zhi")
    mate = lax.ppermute(own, "core", pairs(2, 1))
    far = lax.ppermute(own, "zlo", pairs(2, 1))
    far_mate = lax.ppermute(far, "core", pairs(2, 1))
    plane, own_seeds, place, mate, far_mate = lax.optimization_barrier(
        (plane, own_seeds, place, mate, far_mate)
    )
    note = call(
        relay_kernel, array(EXTRA, BLOCKS + ROWS), [SMEM, VMEM, VMEM], VMEM, limit=4
    )(place, plane, own_seeds)
    notes = gather(note, LINE)

    tiles, listing, partial_degree, line_seeds = call(
        build_kernel,
        (
            array(BLOCKS, ROWS, ROWS, dtype=jnp.bfloat16),
            array(EXTRA, BLOCKS, dtype=jnp.int32),
            array(GROUP, ROWS),
            array(GROUP, ROWS, dtype=jnp.int32),
        ),
        [SMEM] + [VMEM] * 2 + [ANY] * 4,
        (VMEM, SMEM, VMEM, VMEM),
        (
            pltpu.VMEM((GROUP, ROWS, FEAT), jnp.bfloat16),
            pltpu.VMEM((GROUP, ROWS, ROWS), jnp.float32),
            pltpu.VMEM((EXTRA, BLOCKS), jnp.int32),
            pltpu.SemaphoreType.DMA,
            pltpu.SemaphoreType.DMA,
        ),
        limit=14,
    )(place, notes, plane, own, mate, far, far_mate)

    scratch = (
        pltpu.VMEM((GROUP, CLASSES, ROWS), jnp.float32),
        pltpu.VMEM((GROUP, CLASSES, ROWS), jnp.bfloat16),
    )
    sums_out = array(GROUP, CLASSES, ROWS, dtype=jnp.bfloat16)
    partial, scale, own_scale = call(
        first_kernel,
        (sums_out, array(GROUP, ROWS), array(1, ROWS)),
        [SMEM, SMEM, VMEM, VMEM, VMEM],
        (VMEM,) * 3,
        scratch,
        limit=6,
    )(place, listing, tiles, line_seeds, gather(partial_degree, LINE))
    for sweep in range(3):
        if sweep:
            smooth = gather((BLEND * own_scale * own_scale * summed).astype(jnp.bfloat16), LINE)
            partial = call(
                next_kernel, sums_out, [SMEM] + [VMEM] * 4, VMEM, scratch, limit=6
            )(listing, tiles, line_seeds, scale, smooth)
        summed, own_scale, seeds = lax.optimization_barrier((exchange(partial, PLANE), own_scale, seeds))
        summed = jnp.sum(summed.astype(jnp.float32), axis=0)
    seeded = seeds[None, :] == jnp.arange(CLASSES, dtype=jnp.int32)[:, None]
    labels = BLEND * own_scale * summed + (1.0 - BLEND) * seeded.astype(jnp.float32)
    return (CLASSES * labels).T


def solution(mesh):
    fine = Mesh(mesh.devices.reshape(SIZES), AXES)
    return jax.shard_map(
        local,
        mesh=fine,
        in_specs=(P(AXES, None), P(ROW, COL, None, None), P(AXES)),
        out_specs=P(AXES, None),
        check_vma=False,
    )
```

```python
import jax
import jax.numpy as jnp
from jax import lax
from jax.experimental import pallas as pl
from jax.experimental.pallas import tpu as pltpu
from jax.sharding import Mesh
from jax.sharding import PartitionSpec as P

CLASSES = 64
BLEND = 0.8
EPSILON = 1e-06
AXES = ("zlo", "x", "core", "zhi", "y")
SIZES = (2, 4, 2, 4, 4)
ROW = ("zlo", "x", "core")
COL = ("zhi", "y")
PLANE = ("x", "y")
LINE = ("zlo", "core", "zhi")
GROUP = 16
BLOCKS = GROUP * GROUP
ROWS = 128
FEAT = 768
EXTRA = 24
FOLDS = FEAT // ROWS
CHUNK = 8
VMEM = pl.BlockSpec(memory_space=pltpu.VMEM)
SMEM = pl.BlockSpec(memory_space=pltpu.SMEM)
ANY = pl.BlockSpec(memory_space=pl.ANY)


def prep_kernel(emb_hbm, slots_hbm, folded_ref, bits_ref, emb_ref, slots_ref, emb_sem, slots_sem):
    copies = [
        pltpu.make_async_copy(emb_hbm, emb_ref, emb_sem),
        pltpu.make_async_copy(slots_hbm, slots_ref, slots_sem),
    ]
    for copy in copies:
        copy.start()
    for copy in copies:
        copy.wait()
    features = emb_ref[...].astype(jnp.float32)
    norm = lax.rsqrt(jnp.sum(features * features, axis=1, keepdims=True) + EPSILON)
    normed = (features * norm).astype(jnp.bfloat16)
    for k in range(FOLDS):
        folded_ref[k * ROWS : (k + 1) * ROWS, :] = normed[:, k * ROWS : (k + 1) * ROWS]
    first, second = slots_ref[0:1, :], slots_ref[1:2, :]
    ids = jnp.where(first >= 0, first * GROUP + second, -1)
    hits = (lax.broadcasted_iota(jnp.int32, (BLOCKS, 32), 0) == ids).astype(jnp.float32)
    bits = lax.dot_general(
        jnp.ones((8, 32), jnp.float32), hits, (((1,), (1,)), ((), ())),
        preferred_element_type=jnp.float32,
    )
    row = lax.broadcasted_iota(jnp.int32, (8, ROWS), 0)
    bits_ref[...] = jnp.where(row < 4, bits[:, :ROWS], bits[:, ROWS:]).astype(jnp.bfloat16)


def relay_kernel(place_ref, folded_ref, bits_ref, seeds_ref, out_ref):
    x, y = place_ref[0], place_ref[1]
    out_ref[:FEAT, :] = folded_ref[...]
    row = lax.broadcasted_iota(jnp.int32, (8, ROWS), 0)
    ahead = jnp.zeros((8, ROWS), jnp.float32)
    back = jnp.zeros((8, ROWS), jnp.float32)
    for k in range(4):
        note = bits_ref[k * 4 + y].astype(jnp.float32)
        ahead = jnp.where(row == 2 * k, note[0:1], jnp.where(row == 2 * k + 1, note[4:5], ahead))
        note = bits_ref[x * 4 + k].astype(jnp.float32)
        back = jnp.where(row == 2 * k, note[0:1], jnp.where(row == 2 * k + 1, note[4:5], back))
    seeds = jnp.broadcast_to(seeds_ref[...].astype(jnp.float32), (8, ROWS))
    out_ref[FEAT:, :] = jnp.concatenate([ahead, back, seeds], axis=0).astype(jnp.bfloat16)


def make_list(place_ref, notes, list_v):
    x, y, zlo, core, zhi = (place_ref[k] for k in range(5))
    shape = (BLOCKS, BLOCKS)
    row = lax.broadcasted_iota(jnp.int32, shape, 0)
    lane = lax.broadcasted_iota(jnp.int32, shape, 1)
    u_zhi, u_x = row >> 6, (row >> 4) & 3
    v_zlo, v_core, v_y = (row >> 3) & 1, (row >> 2) & 1, row & 3
    a_zhi, a_y = lane >> 6, (lane >> 4) & 3
    b_zlo, b_x, b_core = (lane >> 3) & 1, (lane >> 1) & 3, lane & 1
    forward = (a_zhi == zhi) & (b_x == x) & (a_y == v_y) & (b_zlo == v_zlo) & (b_core == v_core)
    mirror = (a_zhi == u_zhi) & (a_y == y) & (b_zlo == zlo) & (b_x == u_x) & (b_core == core)
    ahead, back = [], []
    for part in range(4):
        note = notes[part].astype(jnp.float32)
        for k in range(4):
            full = jnp.concatenate([note[2 * k : 2 * k + 1], note[2 * k + 1 : 2 * k + 2]], axis=1)
            ahead.append(jnp.broadcast_to(full, (GROUP, BLOCKS)))
        note = notes[(part ^ (place_ref[5] >> 2)) * 4 + zhi].astype(jnp.float32)
        for k in range(4, 8):
            full = jnp.concatenate([note[2 * k : 2 * k + 1], note[2 * k + 1 : 2 * k + 2]], axis=1)
            back.append(full)
    ahead = jnp.concatenate(ahead, axis=0)
    back = jnp.concatenate(back * GROUP, axis=0)
    hits = jnp.where(forward, ahead, 0.0) + jnp.where(mirror, back, 0.0)
    counts = jnp.dot(
        hits.astype(jnp.bfloat16), jnp.ones(shape, jnp.bfloat16), preferred_element_type=jnp.float32
    )
    live = (counts > 0.0).astype(jnp.float32)
    upto = jnp.dot(
        (lane <= row).astype(jnp.float32).astype(jnp.bfloat16), live.astype(jnp.bfloat16),
        preferred_element_type=jnp.float32,
    )
    spot = jnp.where(lane.astype(jnp.float32) == upto - 1.0, live, 0.0)
    slot_lane = lax.broadcasted_iota(jnp.int32, (8, BLOCKS), 1)
    code = (
        (((slot_lane >> 4) & 3) * 4 + (slot_lane & 3)) * GROUP
        + ((slot_lane >> 3) & 1) * 8 + ((slot_lane >> 2) & 1) * 4 + (slot_lane >> 6)
    ).astype(jnp.float32).astype(jnp.bfloat16)
    ones = jnp.ones((8, BLOCKS), jnp.bfloat16)
    codes = jnp.dot(code, spot.astype(jnp.bfloat16), preferred_element_type=jnp.float32)
    weights = jnp.dot(ones, (spot * counts).astype(jnp.bfloat16), preferred_element_type=jnp.float32)
    found = jnp.dot(ones, live.astype(jnp.bfloat16), preferred_element_type=jnp.float32)
    line = lax.broadcasted_iota(jnp.int32, (8, BLOCKS), 0)
    table = jnp.where(line == 0, codes, jnp.where(line == 1, weights, found))
    list_v[...] = (table + 0.5).astype(jnp.int32)


def unfold(blocks, at):
    return jnp.concatenate([blocks[at, f * ROWS : (f + 1) * ROWS, :] for f in range(FOLDS)], axis=1)


def build_kernel(place_ref, plane_ref, own_ref, mate_ref, far_ref, far_mate_ref,
                 tiles_ref, list_ref, deg_ref, seeds_ref, line_v, notes, sums, list_v, list_sem, line_sem, notes_sem):
    planes = place_ref[5] & 12
    arrays = tuple(enumerate((own_ref, mate_ref, far_ref, far_mate_ref)))
    extras = [
        pltpu.make_async_copy(
            part.at[:, pl.ds(FEAT, EXTRA)], notes.at[pl.ds(at * 4, 4)], notes_sem
        )
        for at, part in arrays
    ]
    parts = [
        pltpu.make_async_copy(part.at[:, pl.ds(0, FEAT)], line_v.at[pl.ds(at * 4, 4)], line_sem)
        for at, part in arrays
    ]
    for copy in extras + parts:
        copy.start()
    for copy in extras:
        copy.wait()
    make_list(place_ref, notes, list_v)
    list_copy = pltpu.make_async_copy(list_v, list_ref, list_sem)
    list_copy.start()
    for b in range(GROUP):
        seeds_ref[b : b + 1, :] = notes[b ^ planes, GROUP:, :].astype(jnp.float32)[0:1].astype(jnp.int32)
    sums[...] = jnp.zeros_like(sums)
    sharpness = FEAT**0.5
    diag_slot = place_ref[6]
    on_diag = (
        lax.broadcasted_iota(jnp.int32, (ROWS, ROWS), 0)
        == lax.broadcasted_iota(jnp.int32, (ROWS, ROWS), 1)
    ).astype(jnp.float32)
    list_copy.wait()
    for part in parts:
        part.wait()

    def build_chunk(group, carry):
        for k in range(CHUNK):
            at = group * CHUNK + k
            slot = list_ref[0, at]
            a, b = slot >> 4, slot & 15
            weight = list_ref[1, at].astype(jnp.float32)
            off = jnp.where(slot == diag_slot, weight, 0.0)
            scores = lax.dot_general(
                unfold(line_v, b ^ planes), unfold(plane_ref, a), (((1,), (1,)), ((), ())),
                preferred_element_type=jnp.float32,
            )
            tile = jnp.exp(sharpness * (scores - 1.0)) * (weight - on_diag * off)
            tiles_ref[at] = tile.astype(jnp.bfloat16)
            sums[b] += tile
        return carry

    lax.fori_loop(0, (list_ref[2, 0] + CHUNK - 1) // CHUNK, build_chunk, 0)
    for b in range(GROUP):
        deg_ref[b : b + 1, :] = jnp.sum(sums[b].T, axis=0, keepdims=True)


def run_apply(list_ref, tiles_ref, out_ref, total, spread):
    total[...] = jnp.zeros_like(total)

    def chunk_step(group, carry):
        for k in range(CHUNK):
            at = group * CHUNK + k
            slot = list_ref[0, at]
            total[slot >> 4] += jnp.dot(
                spread[slot & 15], tiles_ref[at], preferred_element_type=jnp.float32
            )
        return carry

    lax.fori_loop(0, (list_ref[2, 0] + CHUNK - 1) // CHUNK, chunk_step, 0)
    out_ref[...] = total[...].astype(jnp.bfloat16)


def seeded_block(seeds_ref, b):
    classes = lax.broadcasted_iota(jnp.int32, (CLASSES, ROWS), 0)
    return classes == seeds_ref[b : b + 1, :]


def first_kernel(place_ref, list_ref, tiles_ref, seeds_ref, parts_ref,
                 out_ref, scale_ref, own_ref, total, spread):
    scale_ref[...] = lax.rsqrt(jnp.sum(parts_ref[...], axis=0))
    own_ref[...] = scale_ref[pl.ds(place_ref[5], 1), :]
    for b in range(GROUP):
        seeded = jnp.where(seeded_block(seeds_ref, b), scale_ref[b : b + 1, :], 0.0)
        spread[b] = seeded.astype(jnp.bfloat16)
    run_apply(list_ref, tiles_ref, out_ref, total, spread)


def next_kernel(list_ref, tiles_ref, seeds_ref, scale_ref, smooth_ref, out_ref, total, spread):
    for b in range(GROUP):
        seed_part = jnp.where(
            seeded_block(seeds_ref, b), (1.0 - BLEND) * scale_ref[b : b + 1, :], 0.0
        )
        spread[b] = (smooth_ref[b].astype(jnp.float32) + seed_part).astype(jnp.bfloat16)
    run_apply(list_ref, tiles_ref, out_ref, total, spread)


def call(kernel, outs, ins, out_specs, scratch=(), limit=8):
    return pl.pallas_call(
        kernel,
        out_shape=outs,
        in_specs=ins,
        out_specs=out_specs,
        scratch_shapes=list(scratch),
        compiler_params=pltpu.CompilerParams(vmem_limit_bytes=limit << 20),
    )


def array(*shape, dtype=jnp.float32):
    return jax.ShapeDtypeStruct(shape, dtype)


def exchange(blocks, axes):
    return lax.all_to_all(blocks, axes, 0, 0)


def gather(block, axes):
    return exchange(jnp.broadcast_to(block[None], (GROUP,) + block.shape), axes)


def pairs(count, step):
    return [(k, k ^ step) for k in range(count)]


def local(embeddings, tile_list, seeds):
    x, y, zlo, core, zhi = (lax.axis_index(name) for name in ("x", "y", "zlo", "core", "zhi"))
    mine = zlo * 8 + core * 4 + zhi
    place = jnp.stack([x, y, zlo, core, zhi, mine, (x * 4 + y) * GROUP + mine]).astype(jnp.int32)
    folded, bits = call(
        prep_kernel,
        (array(FEAT, ROWS, dtype=jnp.bfloat16), array(8, ROWS, dtype=jnp.bfloat16)),
        [ANY] * 2,
        (VMEM,) * 2,
        (
            pltpu.VMEM((ROWS, FEAT), jnp.bfloat16),
            pltpu.VMEM((2, 32), jnp.int32),
            pltpu.SemaphoreType.DMA,
            pltpu.SemaphoreType.DMA,
        ),
        limit=60,
    )(embeddings, tile_list.reshape(-1, 2).T)
    bits = gather(bits, PLANE)
    folded, bits = lax.optimization_barrier((folded, bits))

    block = call(
        relay_kernel,
        array(FEAT + EXTRA, ROWS, dtype=jnp.bfloat16),
        [SMEM] + [VMEM] * 3,
        VMEM,
        limit=60,
    )(place, folded, bits, seeds[None, :])
    plane = gather(folded, PLANE)
    own = pltpu.with_memory_space_constraint(lax.all_gather(block, "zhi"), pltpu.HBM)
    mate = lax.ppermute(own, "core", pairs(2, 1))
    far = lax.ppermute(own, "zlo", pairs(2, 1))
    far_mate = lax.ppermute(far, "core", pairs(2, 1))

    tiles, listing, partial_degree, line_seeds = call(
        build_kernel,
        (
            array(BLOCKS, ROWS, ROWS, dtype=jnp.bfloat16),
            array(8, BLOCKS, dtype=jnp.int32),
            array(GROUP, ROWS),
            array(GROUP, ROWS, dtype=jnp.int32),
        ),
        [SMEM, VMEM] + [ANY] * 4,
        (VMEM, SMEM, VMEM, VMEM),
        (
            pltpu.VMEM((GROUP, FEAT, ROWS), jnp.bfloat16),
            pltpu.VMEM((GROUP, EXTRA, ROWS), jnp.bfloat16),
            pltpu.VMEM((GROUP, ROWS, ROWS), jnp.float32),
            pltpu.VMEM((8, BLOCKS), jnp.int32),
            pltpu.SemaphoreType.DMA,
            pltpu.SemaphoreType.DMA,
            pltpu.SemaphoreType.DMA,
        ),
        limit=14,
    )(place, plane, own, mate, far, far_mate)

    scratch = (
        pltpu.VMEM((GROUP, CLASSES, ROWS), jnp.float32),
        pltpu.VMEM((GROUP, CLASSES, ROWS), jnp.bfloat16),
    )
    sums_out = array(GROUP, CLASSES, ROWS, dtype=jnp.bfloat16)
    partial, scale, own_scale = call(
        first_kernel,
        (sums_out, array(GROUP, ROWS), array(1, ROWS)),
        [SMEM, SMEM, VMEM, VMEM, VMEM],
        (VMEM,) * 3,
        scratch,
        limit=6,
    )(place, listing, tiles, line_seeds, gather(partial_degree, LINE))
    for sweep in range(3):
        if sweep:
            smooth = gather((BLEND * own_scale * own_scale * summed).astype(jnp.bfloat16), LINE)
            partial = call(
                next_kernel, sums_out, [SMEM] + [VMEM] * 4, VMEM, scratch, limit=6
            )(listing, tiles, line_seeds, scale, smooth)
        summed, own_scale, seeds = lax.optimization_barrier((exchange(partial, PLANE), own_scale, seeds))
        summed = jnp.sum(summed.astype(jnp.float32), axis=0)
    seeded = seeds[None, :] == jnp.arange(CLASSES, dtype=jnp.int32)[:, None]
    labels = BLEND * own_scale * summed + (1.0 - BLEND) * seeded.astype(jnp.float32)
    return (CLASSES * labels).T


def solution(mesh):
    fine = Mesh(mesh.devices.reshape(SIZES), AXES)
    return jax.shard_map(
        local,
        mesh=fine,
        in_specs=(P(AXES, None), P(ROW, COL, None, None), P(AXES)),
        out_specs=P(AXES, None),
        check_vma=False,
    )
```

```python
import jax
import jax.numpy as jnp
from jax import lax
from jax.experimental import pallas as pl
from jax.experimental.pallas import tpu as pltpu
from jax.sharding import Mesh
from jax.sharding import PartitionSpec as P

CLASSES = 64
BLEND = 0.8
EPSILON = 1e-06
AXES = ("zlo", "x", "core", "zhi", "y")
SIZES = (2, 4, 2, 4, 4)
ROW = ("zlo", "x", "core")
COL = ("zhi", "y")
PLANE = ("x", "y")
LINE = ("zlo", "core", "zhi")
GROUP = 16
BLOCKS = GROUP * GROUP
ROWS = 128
FEAT = 768
EXTRA = 24
FOLDS = FEAT // ROWS
CHUNK = 8
VMEM = pl.BlockSpec(memory_space=pltpu.VMEM)
SMEM = pl.BlockSpec(memory_space=pltpu.SMEM)
ANY = pl.BlockSpec(memory_space=pl.ANY)


def position():
    x, y, zlo, core, zhi = (lax.axis_index(name) for name in ("x", "y", "zlo", "core", "zhi"))
    return x, y, zlo, core, zhi, zlo * 8 + core * 4 + zhi


def prep_kernel(emb_hbm, slots_hbm, folded_ref, copies_ref, bits_ref,
                emb_ref, slots_ref, emb_sem, slots_sem, out_sem):
    copies = [
        pltpu.make_async_copy(emb_hbm, emb_ref, emb_sem),
        pltpu.make_async_copy(slots_hbm, slots_ref, slots_sem),
    ]
    for copy in copies:
        copy.start()
    for copy in copies:
        copy.wait()
    features = emb_ref[...].astype(jnp.float32)
    norm = lax.rsqrt(jnp.sum(features * features, axis=1, keepdims=True) + EPSILON)
    normed = (features * norm).astype(jnp.bfloat16)
    for k in range(FOLDS):
        folded_ref[k * ROWS : (k + 1) * ROWS, :] = normed[:, k * ROWS : (k + 1) * ROWS]
    sends = [pltpu.make_async_copy(folded_ref, copies_ref.at[k], out_sem) for k in range(GROUP)]
    for send in sends:
        send.start()
    first, second = slots_ref[0:1, :], slots_ref[1:2, :]
    ids = jnp.where(first >= 0, first * GROUP + second, -1)
    hits = (lax.broadcasted_iota(jnp.int32, (BLOCKS, 32), 0) == ids).astype(jnp.float32)
    bits = lax.dot_general(
        jnp.ones((8, 32), jnp.float32), hits, (((1,), (1,)), ((), ())),
        preferred_element_type=jnp.float32,
    )
    row = lax.broadcasted_iota(jnp.int32, (8, ROWS), 0)
    halves = jnp.where(row < 4, bits[:, :ROWS], bits[:, ROWS:]).astype(jnp.bfloat16)
    bits_ref[...] = jnp.broadcast_to(halves[None], (GROUP, 8, ROWS))
    for send in sends:
        send.wait()


def relay_kernel(folded_ref, bits_ref, seeds_ref, out_ref):
    x, y, *_ = position()
    out_ref[:FEAT, :] = folded_ref[...]
    row = lax.broadcasted_iota(jnp.int32, (8, ROWS), 0)
    ahead = jnp.zeros((8, ROWS), jnp.float32)
    back = jnp.zeros((8, ROWS), jnp.float32)
    for k in range(4):
        note = bits_ref[k * 4 + y].astype(jnp.float32)
        ahead = jnp.where(row == 2 * k, note[0:1], jnp.where(row == 2 * k + 1, note[4:5], ahead))
        note = bits_ref[x * 4 + k].astype(jnp.float32)
        back = jnp.where(row == 2 * k, note[0:1], jnp.where(row == 2 * k + 1, note[4:5], back))
    seeds = jnp.broadcast_to(seeds_ref[...].astype(jnp.float32), (8, ROWS))
    out_ref[FEAT:, :] = jnp.concatenate([ahead, back, seeds], axis=0).astype(jnp.bfloat16)


def make_list(notes, list_v):
    x, y, zlo, core, zhi, mine = position()
    shape = (BLOCKS, BLOCKS)
    row = lax.broadcasted_iota(jnp.int32, shape, 0)
    lane = lax.broadcasted_iota(jnp.int32, shape, 1)
    u_zhi, u_x = row >> 6, (row >> 4) & 3
    v_zlo, v_core, v_y = (row >> 3) & 1, (row >> 2) & 1, row & 3
    a_zhi, a_y = lane >> 6, (lane >> 4) & 3
    b_zlo, b_x, b_core = (lane >> 3) & 1, (lane >> 1) & 3, lane & 1
    forward = (a_zhi == zhi) & (b_x == x) & (a_y == v_y) & (b_zlo == v_zlo) & (b_core == v_core)
    mirror = (a_zhi == u_zhi) & (a_y == y) & (b_zlo == zlo) & (b_x == u_x) & (b_core == core)
    ahead, back = [], []
    for part in range(4):
        note = notes[part].astype(jnp.float32)
        for k in range(4):
            full = jnp.concatenate([note[2 * k : 2 * k + 1], note[2 * k + 1 : 2 * k + 2]], axis=1)
            ahead.append(jnp.broadcast_to(full, (GROUP, BLOCKS)))
        note = notes[(part ^ (mine >> 2)) * 4 + zhi].astype(jnp.float32)
        for k in range(4, 8):
            full = jnp.concatenate([note[2 * k : 2 * k + 1], note[2 * k + 1 : 2 * k + 2]], axis=1)
            back.append(full)
    ahead = jnp.concatenate(ahead, axis=0)
    back = jnp.concatenate(back * GROUP, axis=0)
    hits = jnp.where(forward, ahead, 0.0) + jnp.where(mirror, back, 0.0)
    counts = jnp.dot(
        hits.astype(jnp.bfloat16), jnp.ones(shape, jnp.bfloat16), preferred_element_type=jnp.float32
    )
    live = (counts > 0.0).astype(jnp.float32)
    upto = jnp.dot(
        (lane <= row).astype(jnp.float32).astype(jnp.bfloat16), live.astype(jnp.bfloat16),
        preferred_element_type=jnp.float32,
    )
    spot = jnp.where(lane.astype(jnp.float32) == upto - 1.0, live, 0.0)
    slot_lane = lax.broadcasted_iota(jnp.int32, (8, BLOCKS), 1)
    code = (
        (((slot_lane >> 4) & 3) * 4 + (slot_lane & 3)) * GROUP
        + ((slot_lane >> 3) & 1) * 8 + ((slot_lane >> 2) & 1) * 4 + (slot_lane >> 6)
    ).astype(jnp.float32).astype(jnp.bfloat16)
    ones = jnp.ones((8, BLOCKS), jnp.bfloat16)
    codes = jnp.dot(code, spot.astype(jnp.bfloat16), preferred_element_type=jnp.float32)
    weights = jnp.dot(ones, (spot * counts).astype(jnp.bfloat16), preferred_element_type=jnp.float32)
    found = jnp.dot(ones, live.astype(jnp.bfloat16), preferred_element_type=jnp.float32)
    line = lax.broadcasted_iota(jnp.int32, (8, BLOCKS), 0)
    table = jnp.where(line == 0, codes, jnp.where(line == 1, weights, found))
    list_v[...] = (table + 0.5).astype(jnp.int32)


def unfold(blocks, at):
    return jnp.concatenate([blocks[at, f * ROWS : (f + 1) * ROWS, :] for f in range(FOLDS)], axis=1)


def build_kernel(plane_ref, own_ref, mate_ref, far_ref, far_mate_ref,
                 tiles_ref, list_ref, deg_ref, seeds_ref, line_v, notes, sums, list_v, list_sem, line_sem, notes_sem):
    x, y, *_, mine = position()
    planes = mine & 12
    arrays = tuple(enumerate((own_ref, mate_ref, far_ref, far_mate_ref)))
    extras = [
        pltpu.make_async_copy(
            part.at[:, pl.ds(FEAT, EXTRA)], notes.at[pl.ds(at * 4, 4)], notes_sem
        )
        for at, part in arrays
    ]
    parts = [
        pltpu.make_async_copy(part.at[:, pl.ds(0, FEAT)], line_v.at[pl.ds(at * 4, 4)], line_sem)
        for at, part in arrays
    ]
    for copy in extras + parts:
        copy.start()
    for copy in extras:
        copy.wait()
    make_list(notes, list_v)
    list_copy = pltpu.make_async_copy(list_v, list_ref, list_sem)
    list_copy.start()
    for b in range(GROUP):
        seeds_ref[b : b + 1, :] = notes[b ^ planes, GROUP:, :].astype(jnp.float32)[0:1].astype(jnp.int32)
    sums[...] = jnp.zeros_like(sums)
    sharpness = FEAT**0.5
    diag_slot = (x * 4 + y) * GROUP + mine
    on_diag = (
        lax.broadcasted_iota(jnp.int32, (ROWS, ROWS), 0)
        == lax.broadcasted_iota(jnp.int32, (ROWS, ROWS), 1)
    ).astype(jnp.float32)
    list_copy.wait()
    for part in parts:
        part.wait()

    def build_chunk(group, carry):
        for k in range(CHUNK):
            at = group * CHUNK + k
            slot = list_ref[0, at]
            a, b = slot >> 4, slot & 15
            weight = list_ref[1, at].astype(jnp.float32)
            off = jnp.where(slot == diag_slot, weight, 0.0)
            scores = lax.dot_general(
                unfold(line_v, b ^ planes), unfold(plane_ref, a), (((1,), (1,)), ((), ())),
                preferred_element_type=jnp.float32,
            )
            tile = jnp.exp(sharpness * (scores - 1.0)) * (weight - on_diag * off)
            tiles_ref[at] = tile.astype(jnp.bfloat16)
            sums[b] += tile
        return carry

    lax.fori_loop(0, (list_ref[2, 0] + CHUNK - 1) // CHUNK, build_chunk, 0)
    for b in range(GROUP):
        deg_ref[b : b + 1, :] = jnp.sum(sums[b].T, axis=0, keepdims=True)


def run_apply(list_ref, tiles_ref, out_ref, total, spread):
    total[...] = jnp.zeros_like(total)

    def chunk_step(group, carry):
        for k in range(CHUNK):
            at = group * CHUNK + k
            slot = list_ref[0, at]
            total[slot >> 4] += jnp.dot(
                spread[slot & 15], tiles_ref[at], preferred_element_type=jnp.float32
            )
        return carry

    lax.fori_loop(0, (list_ref[2, 0] + CHUNK - 1) // CHUNK, chunk_step, 0)
    out_ref[...] = total[...].astype(jnp.bfloat16)


def seeded_block(seeds_ref, b):
    classes = lax.broadcasted_iota(jnp.int32, (CLASSES, ROWS), 0)
    return classes == seeds_ref[b : b + 1, :]


def first_kernel(list_ref, tiles_ref, seeds_ref, parts_ref,
                 out_ref, scale_ref, own_ref, total, spread):
    scale_ref[...] = lax.rsqrt(jnp.sum(parts_ref[...], axis=0))
    own_ref[...] = scale_ref[pl.ds(position()[5], 1), :]
    for b in range(GROUP):
        seeded = jnp.where(seeded_block(seeds_ref, b), scale_ref[b : b + 1, :], 0.0)
        spread[b] = seeded.astype(jnp.bfloat16)
    run_apply(list_ref, tiles_ref, out_ref, total, spread)


def next_kernel(list_ref, tiles_ref, seeds_ref, scale_ref, own_ref, mate_ref,
                out_ref, total, spread):
    core = lax.axis_index("core")
    classes = lax.broadcasted_iota(jnp.int32, (CLASSES, ROWS), 0)
    for k in range(GROUP // 2):
        for smooth_ref, side in ((own_ref, core), (mate_ref, 1 - core)):
            b = (k // 4) * 8 + side * 4 + k % 4
            seeded = classes == seeds_ref[pl.ds(b, 1), :]
            seed_part = jnp.where(seeded, (1.0 - BLEND) * scale_ref[pl.ds(b, 1), :], 0.0)
            spread[b] = (smooth_ref[k].astype(jnp.float32) + seed_part).astype(jnp.bfloat16)
    run_apply(list_ref, tiles_ref, out_ref, total, spread)


def call(kernel, outs, ins, out_specs, scratch=(), limit=8):
    return pl.pallas_call(
        kernel,
        out_shape=outs,
        in_specs=ins,
        out_specs=out_specs,
        scratch_shapes=list(scratch),
        compiler_params=pltpu.CompilerParams(vmem_limit_bytes=limit << 20),
    )


def array(*shape, dtype=jnp.float32):
    return jax.ShapeDtypeStruct(shape, dtype)


def exchange(blocks, axes):
    return lax.all_to_all(blocks, axes, 0, 0)


def gather(block, axes, count=GROUP):
    return exchange(jnp.broadcast_to(block[None], (count,) + block.shape), axes)


def pairs(count, step):
    return [(k, k ^ step) for k in range(count)]


def local(embeddings, tile_list, seeds):
    folded, copies, bits = call(
        prep_kernel,
        (
            array(FEAT, ROWS, dtype=jnp.bfloat16),
            array(GROUP, FEAT, ROWS, dtype=jnp.bfloat16),
            array(GROUP, 8, ROWS, dtype=jnp.bfloat16),
        ),
        [ANY] * 2,
        (VMEM, ANY, VMEM),
        (
            pltpu.VMEM((ROWS, FEAT), jnp.bfloat16),
            pltpu.VMEM((2, 32), jnp.int32),
            pltpu.SemaphoreType.DMA,
            pltpu.SemaphoreType.DMA,
            pltpu.SemaphoreType.DMA,
        ),
        limit=60,
    )(embeddings, tile_list.reshape(-1, 2).T)
    bits = exchange(bits, PLANE)
    copies, bits = lax.optimization_barrier((copies, bits))

    block = call(
        relay_kernel,
        array(FEAT + EXTRA, ROWS, dtype=jnp.bfloat16),
        [VMEM] * 3,
        VMEM,
        limit=4,
    )(folded, bits, seeds[None, :])
    plane = exchange(copies, PLANE)
    own = pltpu.with_memory_space_constraint(lax.all_gather(block, "zhi"), pltpu.HBM)
    mate = lax.ppermute(own, "core", pairs(2, 1))
    far = lax.ppermute(own, "zlo", pairs(2, 1))
    far_mate = lax.ppermute(far, "core", pairs(2, 1))

    tiles, listing, partial_degree, line_seeds = call(
        build_kernel,
        (
            array(BLOCKS, ROWS, ROWS, dtype=jnp.bfloat16),
            array(8, BLOCKS, dtype=jnp.int32),
            array(GROUP, ROWS),
            array(GROUP, ROWS, dtype=jnp.int32),
        ),
        [VMEM] + [ANY] * 4,
        (VMEM, SMEM, VMEM, VMEM),
        (
            pltpu.VMEM((GROUP, FEAT, ROWS), jnp.bfloat16),
            pltpu.VMEM((GROUP, EXTRA, ROWS), jnp.bfloat16),
            pltpu.VMEM((GROUP, ROWS, ROWS), jnp.float32),
            pltpu.VMEM((8, BLOCKS), jnp.int32),
            pltpu.SemaphoreType.DMA,
            pltpu.SemaphoreType.DMA,
            pltpu.SemaphoreType.DMA,
        ),
        limit=14,
    )(plane, own, mate, far, far_mate)

    scratch = (
        pltpu.VMEM((GROUP, CLASSES, ROWS), jnp.float32),
        pltpu.VMEM((GROUP, CLASSES, ROWS), jnp.bfloat16),
    )
    sums_out = array(GROUP, CLASSES, ROWS, dtype=jnp.bfloat16)
    partial, scale, own_scale = call(
        first_kernel,
        (sums_out, array(GROUP, ROWS), array(1, ROWS)),
        [SMEM, VMEM, VMEM, VMEM],
        (VMEM,) * 3,
        scratch,
        limit=6,
    )(listing, tiles, line_seeds, gather(partial_degree, LINE))
    for sweep in range(3):
        if sweep:
            smooth = (BLEND * own_scale * own_scale * summed).astype(jnp.bfloat16)
            smooth = gather(smooth, ("zlo", "zhi"), GROUP // 2)
            partial = call(
                next_kernel, sums_out, [SMEM] + [VMEM] * 5, VMEM, scratch, limit=6
            )(listing, tiles, line_seeds, scale, smooth, lax.ppermute(smooth, "core", pairs(2, 1)))
        summed, own_scale, seeds = lax.optimization_barrier((exchange(partial, PLANE), own_scale, seeds))
        summed = jnp.sum(summed.astype(jnp.float32), axis=0)
    seeded = seeds[None, :] == jnp.arange(CLASSES, dtype=jnp.int32)[:, None]
    labels = BLEND * own_scale * summed + (1.0 - BLEND) * seeded.astype(jnp.float32)
    return (CLASSES * labels).T


def solution(mesh):
    fine = Mesh(mesh.devices.reshape(SIZES), AXES)
    return jax.shard_map(
        local,
        mesh=fine,
        in_specs=(P(AXES, None), P(ROW, COL, None, None), P(AXES)),
        out_specs=P(AXES, None),
        check_vma=False,
    )
```

```python
import jax
import jax.numpy as jnp
from jax import lax
from jax.experimental import pallas as pl
from jax.experimental.pallas import tpu as pltpu
from jax.sharding import Mesh
from jax.sharding import PartitionSpec as P


CLASSES = 64
BLEND = 0.8
EPSILON = 1e-06
AXES = ("zlo", "x", "core", "zhi", "y")
SIZES = (2, 4, 2, 4, 4)
ROW = ("zlo", "x", "core")
COL = ("zhi", "y")
PLANE = ("x", "y")
LINE = ("zlo", "core", "zhi")
GROUP = 16
BLOCKS = GROUP * GROUP
ROWS = 128
FEAT = 768
EXTRA = 24
FOLDS = FEAT // ROWS
CHUNK = 8
VMEM = pl.BlockSpec(memory_space=pltpu.VMEM)
SMEM = pl.BlockSpec(memory_space=pltpu.SMEM)
ANY = pl.BlockSpec(memory_space=pl.ANY)


def position():
    x, y, zlo, core, zhi = (lax.axis_index(name) for name in ("x", "y", "zlo", "core", "zhi"))
    return x, y, zlo, core, zhi, zlo * 8 + core * 4 + zhi


def prep_kernel(emb_hbm, slots_hbm, folded_ref, copies_ref, bits_ref,
                emb_ref, slots_ref, emb_sem, slots_sem, out_sem):
    copies = [
        pltpu.make_async_copy(emb_hbm, emb_ref, emb_sem),
        pltpu.make_async_copy(slots_hbm, slots_ref, slots_sem),
    ]
    for copy in copies:
        copy.start()
    for copy in copies:
        copy.wait()
    features = emb_ref[...].astype(jnp.float32)
    norm = lax.rsqrt(jnp.sum(features * features, axis=1, keepdims=True) + EPSILON)
    normed = (features * norm).astype(jnp.bfloat16)
    for k in range(FOLDS):
        folded_ref[k * ROWS : (k + 1) * ROWS, :] = normed[:, k * ROWS : (k + 1) * ROWS]
    sends = [pltpu.make_async_copy(folded_ref, copies_ref.at[k], out_sem) for k in range(GROUP)]
    for send in sends:
        send.start()
    first, second = slots_ref[0:1, :], slots_ref[1:2, :]
    ids = jnp.where(first >= 0, first * GROUP + second, -1)
    hits = (lax.broadcasted_iota(jnp.int32, (BLOCKS, 32), 0) == ids).astype(jnp.float32)
    bits = lax.dot_general(
        jnp.ones((8, 32), jnp.float32), hits, (((1,), (1,)), ((), ())),
        preferred_element_type=jnp.float32,
    )
    row = lax.broadcasted_iota(jnp.int32, (8, ROWS), 0)
    halves = jnp.where(row < 4, bits[:, :ROWS], bits[:, ROWS:]).astype(jnp.bfloat16)
    bits_ref[...] = halves
    for send in sends:
        send.wait()


def relay_kernel(folded_ref, seeds_ref, bits_ref, *refs):
    x, y, *_ = position()
    out_ref = refs[6]
    out_ref[:FEAT, :] = folded_ref[...]
    row = lax.broadcasted_iota(jnp.int32, (8, ROWS), 0)
    groups = []
    for own, others in ((x, refs[:3]), (y, refs[3:6])):
        rows = jnp.zeros((8, ROWS), jnp.float32)
        for step, ref in enumerate((bits_ref, *others)):
            at = 2 * (own ^ step)
            note = ref[...].astype(jnp.float32)
            rows = jnp.where(row == at, note[0:1], jnp.where(row == at + 1, note[4:5], rows))
        groups.append(rows)
    groups.append(jnp.broadcast_to(seeds_ref[...].astype(jnp.float32), (8, ROWS)))
    out_ref[FEAT:, :] = jnp.concatenate(groups, axis=0).astype(jnp.bfloat16)


def make_list(notes, list_v):
    x, y, zlo, core, zhi, mine = position()
    shape = (BLOCKS, BLOCKS)
    row = lax.broadcasted_iota(jnp.int32, shape, 0)
    lane = lax.broadcasted_iota(jnp.int32, shape, 1)
    u_zhi, u_x = row >> 6, (row >> 4) & 3
    v_zlo, v_core, v_y = (row >> 3) & 1, (row >> 2) & 1, row & 3
    a_zhi, a_y = lane >> 6, (lane >> 4) & 3
    b_zlo, b_x, b_core = (lane >> 3) & 1, (lane >> 1) & 3, lane & 1
    forward = (a_zhi == zhi) & (b_x == x) & (a_y == v_y) & (b_zlo == v_zlo) & (b_core == v_core)
    mirror = (a_zhi == u_zhi) & (a_y == y) & (b_zlo == zlo) & (b_x == u_x) & (b_core == core)
    ahead, back = [], []
    for part in range(4):
        note = notes[part].astype(jnp.float32)
        for k in range(4):
            full = jnp.concatenate([note[2 * k : 2 * k + 1], note[2 * k + 1 : 2 * k + 2]], axis=1)
            ahead.append(jnp.broadcast_to(full, (GROUP, BLOCKS)))
        note = notes[(part ^ (mine >> 2)) * 4 + zhi].astype(jnp.float32)
        for k in range(4, 8):
            full = jnp.concatenate([note[2 * k : 2 * k + 1], note[2 * k + 1 : 2 * k + 2]], axis=1)
            back.append(full)
    ahead = jnp.concatenate(ahead, axis=0)
    back = jnp.concatenate(back * GROUP, axis=0)
    hits = jnp.where(forward, ahead, 0.0) + jnp.where(mirror, back, 0.0)
    counts = jnp.dot(
        hits.astype(jnp.bfloat16), jnp.ones(shape, jnp.bfloat16), preferred_element_type=jnp.float32
    )
    live = (counts > 0.0).astype(jnp.float32)
    upto = jnp.dot(
        (lane <= row).astype(jnp.float32).astype(jnp.bfloat16), live.astype(jnp.bfloat16),
        preferred_element_type=jnp.float32,
    )
    spot = jnp.where(lane.astype(jnp.float32) == upto - 1.0, live, 0.0)
    slot_lane = lax.broadcasted_iota(jnp.int32, (8, BLOCKS), 1)
    code = (
        (((slot_lane >> 4) & 3) * 4 + (slot_lane & 3)) * GROUP
        + ((slot_lane >> 3) & 1) * 8 + ((slot_lane >> 2) & 1) * 4 + (slot_lane >> 6)
    ).astype(jnp.float32).astype(jnp.bfloat16)
    ones = jnp.ones((8, BLOCKS), jnp.bfloat16)
    codes = jnp.dot(code, spot.astype(jnp.bfloat16), preferred_element_type=jnp.float32)
    weights = jnp.dot(ones, (spot * counts).astype(jnp.bfloat16), preferred_element_type=jnp.float32)
    found = jnp.dot(ones, live.astype(jnp.bfloat16), preferred_element_type=jnp.float32)
    line = lax.broadcasted_iota(jnp.int32, (8, BLOCKS), 0)
    table = jnp.where(line == 0, codes, jnp.where(line == 1, weights, found))
    list_v[...] = (table + 0.5).astype(jnp.int32)


def unfold(blocks, at):
    return jnp.concatenate([blocks[at, f * ROWS : (f + 1) * ROWS, :] for f in range(FOLDS)], axis=1)


def build_kernel(plane_ref, own_ref, mate_ref, far_ref, far_mate_ref,
                 tiles_ref, list_ref, deg_ref, seeds_ref, line_v, notes, sums, list_v, list_sem, line_sem, notes_sem):
    x, y, *_, mine = position()
    planes = mine & 12
    arrays = tuple(enumerate((own_ref, mate_ref, far_ref, far_mate_ref)))
    extras = [
        pltpu.make_async_copy(
            part.at[:, pl.ds(FEAT, EXTRA)], notes.at[pl.ds(at * 4, 4)], notes_sem
        )
        for at, part in arrays
    ]
    parts = [
        pltpu.make_async_copy(part.at[:, pl.ds(0, FEAT)], line_v.at[pl.ds(at * 4, 4)], line_sem)
        for at, part in arrays
    ]
    for copy in extras + parts:
        copy.start()
    for copy in extras:
        copy.wait()
    make_list(notes, list_v)
    list_copy = pltpu.make_async_copy(list_v, list_ref, list_sem)
    list_copy.start()
    for b in range(GROUP):
        seeds_ref[b : b + 1, :] = notes[b ^ planes, GROUP:, :].astype(jnp.float32)[0:1].astype(jnp.int32)
    sums[...] = jnp.zeros_like(sums)
    sharpness = FEAT**0.5
    diag_slot = (x * 4 + y) * GROUP + mine
    on_diag = (
        lax.broadcasted_iota(jnp.int32, (ROWS, ROWS), 0)
        == lax.broadcasted_iota(jnp.int32, (ROWS, ROWS), 1)
    ).astype(jnp.float32)
    list_copy.wait()
    for part in parts:
        part.wait()

    def build_chunk(group, carry):
        for k in range(CHUNK):
            at = group * CHUNK + k
            slot = list_ref[0, at]
            a, b = slot >> 4, slot & 15
            weight = list_ref[1, at].astype(jnp.float32)
            off = jnp.where(slot == diag_slot, weight, 0.0)
            scores = lax.dot_general(
                unfold(line_v, b ^ planes), unfold(plane_ref, a), (((1,), (1,)), ((), ())),
                preferred_element_type=jnp.float32,
            )
            tile = jnp.exp(sharpness * (scores - 1.0)) * (weight - on_diag * off)
            tiles_ref[at] = tile.astype(jnp.bfloat16)
            sums[b] += tile
        return carry

    lax.fori_loop(0, (list_ref[2, 0] + CHUNK - 1) // CHUNK, build_chunk, 0)
    for b in range(GROUP):
        deg_ref[b : b + 1, :] = jnp.sum(sums[b].T, axis=0, keepdims=True)


def run_apply(list_ref, tiles_ref, out_ref, total, spread):
    total[...] = jnp.zeros_like(total)

    def chunk_step(group, carry):
        for k in range(CHUNK):
            at = group * CHUNK + k
            slot = list_ref[0, at]
            total[slot >> 4] += jnp.dot(
                spread[slot & 15], tiles_ref[at], preferred_element_type=jnp.float32
            )
        return carry

    lax.fori_loop(0, (list_ref[2, 0] + CHUNK - 1) // CHUNK, chunk_step, 0)
    out_ref[...] = total[...].astype(jnp.bfloat16)


def seeded_block(seeds_ref, b):
    classes = lax.broadcasted_iota(jnp.int32, (CLASSES, ROWS), 0)
    return classes == seeds_ref[b : b + 1, :]


def first_kernel(list_ref, tiles_ref, seeds_ref, parts_ref,
                 out_ref, scale_ref, own_ref, total, spread):
    scale_ref[...] = lax.rsqrt(jnp.sum(parts_ref[...], axis=0))
    own_ref[...] = scale_ref[pl.ds(position()[5], 1), :]
    for b in range(GROUP):
        seeded = jnp.where(seeded_block(seeds_ref, b), scale_ref[b : b + 1, :], 0.0)
        spread[b] = seeded.astype(jnp.bfloat16)
    run_apply(list_ref, tiles_ref, out_ref, total, spread)


def next_kernel(list_ref, tiles_ref, seeds_ref, scale_ref, own_ref, mate_ref,
                out_ref, total, spread):
    core = lax.axis_index("core")
    classes = lax.broadcasted_iota(jnp.int32, (CLASSES, ROWS), 0)
    for k in range(GROUP // 2):
        for smooth_ref, side in ((own_ref, core), (mate_ref, 1 - core)):
            b = (k // 4) * 8 + side * 4 + k % 4
            seeded = classes == seeds_ref[pl.ds(b, 1), :]
            seed_part = jnp.where(seeded, (1.0 - BLEND) * scale_ref[pl.ds(b, 1), :], 0.0)
            spread[b] = (smooth_ref[k].astype(jnp.float32) + seed_part).astype(jnp.bfloat16)
    run_apply(list_ref, tiles_ref, out_ref, total, spread)


def call(kernel, outs, ins, out_specs, scratch=(), limit=8):
    return pl.pallas_call(
        kernel,
        out_shape=outs,
        in_specs=ins,
        out_specs=out_specs,
        scratch_shapes=list(scratch),
        compiler_params=pltpu.CompilerParams(vmem_limit_bytes=limit << 20),
    )


def array(*shape, dtype=jnp.float32):
    return jax.ShapeDtypeStruct(shape, dtype)


def exchange(blocks, axes):
    return lax.all_to_all(blocks, axes, 0, 0)


def gather(block, axes, count=GROUP):
    return exchange(jnp.broadcast_to(block[None], (count,) + block.shape), axes)


def pairs(count, step):
    return [(k, k ^ step) for k in range(count)]


def local(embeddings, tile_list, seeds):
    folded, copies, bits = call(
        prep_kernel,
        (
            array(FEAT, ROWS, dtype=jnp.bfloat16),
            array(GROUP, FEAT, ROWS, dtype=jnp.bfloat16),
            array(8, ROWS, dtype=jnp.bfloat16),
        ),
        [ANY] * 2,
        (VMEM, ANY, VMEM),
        (
            pltpu.VMEM((ROWS, FEAT), jnp.bfloat16),
            pltpu.VMEM((2, 32), jnp.int32),
            pltpu.SemaphoreType.DMA,
            pltpu.SemaphoreType.DMA,
            pltpu.SemaphoreType.DMA,
        ),
        limit=60,
    )(embeddings, tile_list.reshape(-1, 2).T)
    others = []
    for axis in PLANE:
        for step in (1, 2, 3):
            others.append(lax.ppermute(bits, axis, pairs(4, step)))
    plane = exchange(copies, PLANE)
    block = call(
        relay_kernel,
        array(FEAT + EXTRA, ROWS, dtype=jnp.bfloat16),
        [VMEM] * 9,
        VMEM,
        limit=4,
    )(folded, seeds[None, :], bits, *others)
    own = pltpu.with_memory_space_constraint(lax.all_gather(block, "zhi"), pltpu.HBM)
    mate = lax.ppermute(own, "core", pairs(2, 1))
    far = lax.ppermute(own, "zlo", pairs(2, 1))
    far_mate = lax.ppermute(far, "core", pairs(2, 1))

    tiles, listing, partial_degree, line_seeds = call(
        build_kernel,
        (
            array(BLOCKS, ROWS, ROWS, dtype=jnp.bfloat16),
            array(8, BLOCKS, dtype=jnp.int32),
            array(GROUP, ROWS),
            array(GROUP, ROWS, dtype=jnp.int32),
        ),
        [VMEM] + [ANY] * 4,
        (VMEM, SMEM, VMEM, VMEM),
        (
            pltpu.VMEM((GROUP, FEAT, ROWS), jnp.bfloat16),
            pltpu.VMEM((GROUP, EXTRA, ROWS), jnp.bfloat16),
            pltpu.VMEM((GROUP, ROWS, ROWS), jnp.float32),
            pltpu.VMEM((8, BLOCKS), jnp.int32),
            pltpu.SemaphoreType.DMA,
            pltpu.SemaphoreType.DMA,
            pltpu.SemaphoreType.DMA,
        ),
        limit=14,
    )(plane, own, mate, far, far_mate)

    scratch = (
        pltpu.VMEM((GROUP, CLASSES, ROWS), jnp.float32),
        pltpu.VMEM((GROUP, CLASSES, ROWS), jnp.bfloat16),
    )
    sums_out = array(GROUP, CLASSES, ROWS, dtype=jnp.bfloat16)
    partial, scale, own_scale = call(
        first_kernel,
        (sums_out, array(GROUP, ROWS), array(1, ROWS)),
        [SMEM, VMEM, VMEM, VMEM],
        (VMEM,) * 3,
        scratch,
        limit=6,
    )(listing, tiles, line_seeds, gather(partial_degree, LINE))
    for sweep in range(3):
        if sweep:
            smooth = (BLEND * own_scale * own_scale * summed).astype(jnp.bfloat16)
            smooth = gather(smooth, ("zlo", "zhi"), GROUP // 2)
            partial = call(
                next_kernel, sums_out, [SMEM] + [VMEM] * 5, VMEM, scratch, limit=6
            )(listing, tiles, line_seeds, scale, smooth, lax.ppermute(smooth, "core", pairs(2, 1)))
        summed, own_scale, seeds = lax.optimization_barrier((exchange(partial, PLANE), own_scale, seeds))
        summed = jnp.sum(summed.astype(jnp.float32), axis=0)
    seeded = seeds[None, :] == jnp.arange(CLASSES, dtype=jnp.int32)[:, None]
    labels = BLEND * own_scale * summed + (1.0 - BLEND) * seeded.astype(jnp.float32)
    return (CLASSES * labels).T


def solution(mesh):
    fine = Mesh(mesh.devices.reshape(SIZES), AXES)
    return jax.shard_map(
        local,
        mesh=fine,
        in_specs=(P(AXES, None), P(ROW, COL, None, None), P(AXES)),
        out_specs=P(AXES, None),
        check_vma=False,
    )
```

```python
import jax
import jax.numpy as jnp
from jax import lax
from jax.experimental import pallas as pl
from jax.experimental.pallas import tpu as pltpu
from jax.sharding import Mesh
from jax.sharding import PartitionSpec as P


CLASSES = 64
BLEND = 0.8
EPSILON = 1e-06
AXES = ("zlo", "x", "core", "zhi", "y")
SIZES = (2, 4, 2, 4, 4)
ROW = ("zlo", "x", "core")
COL = ("zhi", "y")
PLANE = ("x", "y")
LINE = ("zlo", "core", "zhi")
GROUP = 16
BLOCKS = GROUP * GROUP
ROWS = 128
FEAT = 768
EXTRA = 24
FOLDS = FEAT // ROWS
CHUNK = 8
VMEM = pl.BlockSpec(memory_space=pltpu.VMEM)
SMEM = pl.BlockSpec(memory_space=pltpu.SMEM)
ANY = pl.BlockSpec(memory_space=pl.ANY)


def position():
    x, y, zlo, core, zhi = (lax.axis_index(name) for name in ("x", "y", "zlo", "core", "zhi"))
    return x, y, zlo, core, zhi, zlo * 8 + core * 4 + zhi


def prep_kernel(emb_hbm, slots_hbm, folded_ref, copies_ref, bits_ref,
                emb_ref, slots_ref, turned_ref, emb_sem, slots_sem, out_sem):
    copies = [
        pltpu.make_async_copy(emb_hbm, emb_ref, emb_sem),
        pltpu.make_async_copy(slots_hbm, slots_ref, slots_sem),
    ]
    for copy in copies:
        copy.start()
    for copy in copies:
        copy.wait()
    features = emb_ref[...].astype(jnp.float32)
    norm = lax.rsqrt(jnp.sum(features * features, axis=1, keepdims=True) + EPSILON)
    normed = features * norm
    for k in range(FOLDS):
        part = normed[:, k * ROWS : (k + 1) * ROWS]
        folded_ref[k * ROWS : (k + 1) * ROWS, :] = part.astype(jnp.bfloat16)
        turned_ref[k * ROWS : (k + 1) * ROWS, :] = part.T.astype(jnp.bfloat16)
    sends = [pltpu.make_async_copy(turned_ref, copies_ref.at[k], out_sem) for k in range(GROUP)]
    for send in sends:
        send.start()
    first, second = slots_ref[0:1, :], slots_ref[1:2, :]
    ids = jnp.where(first >= 0, first * GROUP + second, -1)
    hits = (lax.broadcasted_iota(jnp.int32, (BLOCKS, 32), 0) == ids).astype(jnp.float32)
    bits = lax.dot_general(
        jnp.ones((8, 32), jnp.float32), hits, (((1,), (1,)), ((), ())),
        preferred_element_type=jnp.float32,
    )
    row = lax.broadcasted_iota(jnp.int32, (8, ROWS), 0)
    halves = jnp.where(row < 4, bits[:, :ROWS], bits[:, ROWS:]).astype(jnp.bfloat16)
    bits_ref[...] = halves
    for send in sends:
        send.wait()


def relay_kernel(folded_ref, seeds_ref, bits_ref, *refs):
    x, y, *_ = position()
    out_ref = refs[6]
    out_ref[:FEAT, :] = folded_ref[...]
    row = lax.broadcasted_iota(jnp.int32, (8, ROWS), 0)
    groups = []
    for own, others in ((x, refs[:3]), (y, refs[3:6])):
        rows = jnp.zeros((8, ROWS), jnp.float32)
        for step, ref in enumerate((bits_ref, *others)):
            at = 2 * (own ^ step)
            note = ref[...].astype(jnp.float32)
            rows = jnp.where(row == at, note[0:1], jnp.where(row == at + 1, note[4:5], rows))
        groups.append(rows)
    groups.append(jnp.broadcast_to(seeds_ref[...].astype(jnp.float32), (8, ROWS)))
    out_ref[FEAT:, :] = jnp.concatenate(groups, axis=0).astype(jnp.bfloat16)


def make_list(notes, list_v):
    x, y, zlo, core, zhi, mine = position()
    shape = (BLOCKS, BLOCKS)
    row = lax.broadcasted_iota(jnp.int32, shape, 0)
    lane = lax.broadcasted_iota(jnp.int32, shape, 1)
    u_zhi, u_x = row >> 6, (row >> 4) & 3
    v_zlo, v_core, v_y = (row >> 3) & 1, (row >> 2) & 1, row & 3
    a_zhi, a_y = lane >> 6, (lane >> 4) & 3
    b_zlo, b_x, b_core = (lane >> 3) & 1, (lane >> 1) & 3, lane & 1
    forward = (a_zhi == zhi) & (b_x == x) & (a_y == v_y) & (b_zlo == v_zlo) & (b_core == v_core)
    mirror = (a_zhi == u_zhi) & (a_y == y) & (b_zlo == zlo) & (b_x == u_x) & (b_core == core)
    ahead, back = [], []
    for part in range(4):
        note = notes[part].astype(jnp.float32)
        for k in range(4):
            full = jnp.concatenate([note[2 * k : 2 * k + 1], note[2 * k + 1 : 2 * k + 2]], axis=1)
            ahead.append(jnp.broadcast_to(full, (GROUP, BLOCKS)))
        note = notes[(part ^ (mine >> 2)) * 4 + zhi].astype(jnp.float32)
        for k in range(4, 8):
            full = jnp.concatenate([note[2 * k : 2 * k + 1], note[2 * k + 1 : 2 * k + 2]], axis=1)
            back.append(full)
    ahead = jnp.concatenate(ahead, axis=0)
    back = jnp.concatenate(back * GROUP, axis=0)
    hits = jnp.where(forward, ahead, 0.0) + jnp.where(mirror, back, 0.0)
    counts = jnp.dot(
        hits.astype(jnp.bfloat16), jnp.ones(shape, jnp.bfloat16), preferred_element_type=jnp.float32
    )
    live = (counts > 0.0).astype(jnp.float32)
    upto = jnp.dot(
        (lane <= row).astype(jnp.float32).astype(jnp.bfloat16), live.astype(jnp.bfloat16),
        preferred_element_type=jnp.float32,
    )
    spot = jnp.where(lane.astype(jnp.float32) == upto - 1.0, live, 0.0)
    slot_lane = lax.broadcasted_iota(jnp.int32, (8, BLOCKS), 1)
    code = (
        (((slot_lane >> 4) & 3) * 4 + (slot_lane & 3)) * GROUP
        + ((slot_lane >> 3) & 1) * 8 + ((slot_lane >> 2) & 1) * 4 + (slot_lane >> 6)
    ).astype(jnp.float32).astype(jnp.bfloat16)
    ones = jnp.ones((8, BLOCKS), jnp.bfloat16)
    codes = jnp.dot(code, spot.astype(jnp.bfloat16), preferred_element_type=jnp.float32)
    weights = jnp.dot(ones, (spot * counts).astype(jnp.bfloat16), preferred_element_type=jnp.float32)
    found = jnp.dot(ones, live.astype(jnp.bfloat16), preferred_element_type=jnp.float32)
    line = lax.broadcasted_iota(jnp.int32, (8, BLOCKS), 0)
    table = jnp.where(line == 0, codes, jnp.where(line == 1, weights, found))
    list_v[...] = (table + 0.5).astype(jnp.int32)


def unfold(blocks, at):
    return jnp.concatenate([blocks[at, f * ROWS : (f + 1) * ROWS, :] for f in range(FOLDS)], axis=1)


def build_kernel(plane_ref, own_ref, mate_ref, far_ref, far_mate_ref,
                 tiles_ref, list_ref, deg_ref, seeds_ref, line_v, notes, sums, list_v, list_sem, line_sem, notes_sem):
    x, y, *_, mine = position()
    planes = mine & 12
    arrays = tuple(enumerate((own_ref, mate_ref, far_ref, far_mate_ref)))
    extras = [
        pltpu.make_async_copy(
            part.at[:, pl.ds(FEAT, EXTRA)], notes.at[pl.ds(at * 4, 4)], notes_sem
        )
        for at, part in arrays
    ]
    parts = [
        pltpu.make_async_copy(part.at[:, pl.ds(0, FEAT)], line_v.at[pl.ds(at * 4, 4)], line_sem)
        for at, part in arrays
    ]
    for copy in extras + parts:
        copy.start()
    for copy in extras:
        copy.wait()
    make_list(notes, list_v)
    list_copy = pltpu.make_async_copy(list_v, list_ref, list_sem)
    list_copy.start()
    for b in range(GROUP):
        seeds_ref[b : b + 1, :] = notes[b ^ planes, GROUP:, :].astype(jnp.float32)[0:1].astype(jnp.int32)
    sums[...] = jnp.zeros_like(sums)
    sharpness = FEAT**0.5
    diag_slot = (x * 4 + y) * GROUP + mine
    on_diag = (
        lax.broadcasted_iota(jnp.int32, (ROWS, ROWS), 0)
        == lax.broadcasted_iota(jnp.int32, (ROWS, ROWS), 1)
    ).astype(jnp.float32)
    list_copy.wait()
    for part in parts:
        part.wait()

    def build_chunk(group, carry):
        for k in range(CHUNK):
            at = group * CHUNK + k
            slot = list_ref[0, at]
            a, b = slot >> 4, slot & 15
            weight = list_ref[1, at].astype(jnp.float32)
            off = jnp.where(slot == diag_slot, weight, 0.0)
            scores = jnp.dot(
                unfold(line_v, b ^ planes), plane_ref[a], preferred_element_type=jnp.float32
            )
            tile = jnp.exp(sharpness * (scores - 1.0)) * (weight - on_diag * off)
            tiles_ref[at] = tile.astype(jnp.bfloat16)
            sums[b] += tile
        return carry

    lax.fori_loop(0, (list_ref[2, 0] + CHUNK - 1) // CHUNK, build_chunk, 0)
    for b in range(GROUP):
        deg_ref[b : b + 1, :] = jnp.sum(sums[b].T, axis=0, keepdims=True)


def run_apply(list_ref, tiles_ref, out_ref, total, spread):
    total[...] = jnp.zeros_like(total)

    def chunk_step(group, carry):
        for k in range(CHUNK):
            at = group * CHUNK + k
            slot = list_ref[0, at]
            total[slot >> 4] += jnp.dot(
                spread[slot & 15], tiles_ref[at], preferred_element_type=jnp.float32
            )
        return carry

    lax.fori_loop(0, (list_ref[2, 0] + CHUNK - 1) // CHUNK, chunk_step, 0)
    out_ref[...] = total[...].astype(jnp.bfloat16)


def seeded_block(seeds_ref, b):
    classes = lax.broadcasted_iota(jnp.int32, (CLASSES, ROWS), 0)
    return classes == seeds_ref[b : b + 1, :]


def first_kernel(list_ref, tiles_ref, seeds_ref, parts_ref,
                 out_ref, scale_ref, own_ref, total, spread):
    scale_ref[...] = lax.rsqrt(jnp.sum(parts_ref[...], axis=0))
    own_ref[...] = scale_ref[pl.ds(position()[5], 1), :]
    for b in range(GROUP):
        seeded = jnp.where(seeded_block(seeds_ref, b), scale_ref[b : b + 1, :], 0.0)
        spread[b] = seeded.astype(jnp.bfloat16)
    run_apply(list_ref, tiles_ref, out_ref, total, spread)


def next_kernel(list_ref, tiles_ref, seeds_ref, scale_ref, own_ref, mate_ref,
                out_ref, total, spread):
    core = lax.axis_index("core")
    classes = lax.broadcasted_iota(jnp.int32, (CLASSES, ROWS), 0)
    for k in range(GROUP // 2):
        for smooth_ref, side in ((own_ref, core), (mate_ref, 1 - core)):
            b = (k // 4) * 8 + side * 4 + k % 4
            seeded = classes == seeds_ref[pl.ds(b, 1), :]
            seed_part = jnp.where(seeded, (1.0 - BLEND) * scale_ref[pl.ds(b, 1), :], 0.0)
            spread[b] = (smooth_ref[k].astype(jnp.float32) + seed_part).astype(jnp.bfloat16)
    run_apply(list_ref, tiles_ref, out_ref, total, spread)


def call(kernel, outs, ins, out_specs, scratch=(), limit=8):
    return pl.pallas_call(
        kernel,
        out_shape=outs,
        in_specs=ins,
        out_specs=out_specs,
        scratch_shapes=list(scratch),
        compiler_params=pltpu.CompilerParams(vmem_limit_bytes=limit << 20),
    )


def array(*shape, dtype=jnp.float32):
    return jax.ShapeDtypeStruct(shape, dtype)


def exchange(blocks, axes):
    return lax.all_to_all(blocks, axes, 0, 0)


def gather(block, axes, count=GROUP):
    return exchange(jnp.broadcast_to(block[None], (count,) + block.shape), axes)


def pairs(count, step):
    return [(k, k ^ step) for k in range(count)]


def local(embeddings, tile_list, seeds):
    folded, copies, bits = call(
        prep_kernel,
        (
            array(FEAT, ROWS, dtype=jnp.bfloat16),
            array(GROUP, FEAT, ROWS, dtype=jnp.bfloat16),
            array(8, ROWS, dtype=jnp.bfloat16),
        ),
        [ANY] * 2,
        (VMEM, ANY, VMEM),
        (
            pltpu.VMEM((ROWS, FEAT), jnp.bfloat16),
            pltpu.VMEM((2, 32), jnp.int32),
            pltpu.VMEM((FEAT, ROWS), jnp.bfloat16),
            pltpu.SemaphoreType.DMA,
            pltpu.SemaphoreType.DMA,
            pltpu.SemaphoreType.DMA,
        ),
        limit=60,
    )(embeddings, tile_list.reshape(-1, 2).T)
    others = []
    for axis in PLANE:
        for step in (1, 2, 3):
            others.append(lax.ppermute(bits, axis, pairs(4, step)))
    plane = exchange(copies, PLANE)
    block = call(
        relay_kernel,
        array(FEAT + EXTRA, ROWS, dtype=jnp.bfloat16),
        [VMEM] * 9,
        VMEM,
        limit=4,
    )(folded, seeds[None, :], bits, *others)
    own = pltpu.with_memory_space_constraint(lax.all_gather(block, "zhi"), pltpu.HBM)
    mate = lax.ppermute(own, "core", pairs(2, 1))
    far = lax.ppermute(own, "zlo", pairs(2, 1))
    far, mate = lax.optimization_barrier((far, mate))
    far_mate = lax.ppermute(far, "core", pairs(2, 1))

    tiles, listing, partial_degree, line_seeds = call(
        build_kernel,
        (
            array(BLOCKS, ROWS, ROWS, dtype=jnp.bfloat16),
            array(8, BLOCKS, dtype=jnp.int32),
            array(GROUP, ROWS),
            array(GROUP, ROWS, dtype=jnp.int32),
        ),
        [VMEM] + [ANY] * 4,
        (VMEM, SMEM, VMEM, VMEM),
        (
            pltpu.VMEM((GROUP, FEAT, ROWS), jnp.bfloat16),
            pltpu.VMEM((GROUP, EXTRA, ROWS), jnp.bfloat16),
            pltpu.VMEM((GROUP, ROWS, ROWS), jnp.float32),
            pltpu.VMEM((8, BLOCKS), jnp.int32),
            pltpu.SemaphoreType.DMA,
            pltpu.SemaphoreType.DMA,
            pltpu.SemaphoreType.DMA,
        ),
        limit=14,
    )(plane, own, mate, far, far_mate)

    scratch = (
        pltpu.VMEM((GROUP, CLASSES, ROWS), jnp.float32),
        pltpu.VMEM((GROUP, CLASSES, ROWS), jnp.bfloat16),
    )
    sums_out = array(GROUP, CLASSES, ROWS, dtype=jnp.bfloat16)
    partial, scale, own_scale = call(
        first_kernel,
        (sums_out, array(GROUP, ROWS), array(1, ROWS)),
        [SMEM, VMEM, VMEM, VMEM],
        (VMEM,) * 3,
        scratch,
        limit=6,
    )(listing, tiles, line_seeds, gather(partial_degree, LINE))
    for sweep in range(3):
        if sweep:
            smooth = (BLEND * own_scale * own_scale * summed).astype(jnp.bfloat16)
            smooth = gather(smooth, ("zlo", "zhi"), GROUP // 2)
            partial = call(
                next_kernel, sums_out, [SMEM] + [VMEM] * 5, VMEM, scratch, limit=6
            )(listing, tiles, line_seeds, scale, smooth, lax.ppermute(smooth, "core", pairs(2, 1)))
        summed, own_scale, seeds = lax.optimization_barrier((exchange(partial, PLANE), own_scale, seeds))
        summed = jnp.sum(summed.astype(jnp.float32), axis=0)
    seeded = seeds[None, :] == jnp.arange(CLASSES, dtype=jnp.int32)[:, None]
    labels = BLEND * own_scale * summed + (1.0 - BLEND) * seeded.astype(jnp.float32)
    return (CLASSES * labels).T


def solution(mesh):
    fine = Mesh(mesh.devices.reshape(SIZES), AXES)
    return jax.shard_map(
        local,
        mesh=fine,
        in_specs=(P(AXES, None), P(ROW, COL, None, None), P(AXES)),
        out_specs=P(AXES, None),
        check_vma=False,
    )
```

```python
import jax
import jax.numpy as jnp
from jax import lax
from jax.experimental import pallas as pl
from jax.experimental.pallas import tpu as pltpu
from jax.sharding import Mesh
from jax.sharding import PartitionSpec as P


CLASSES = 64
BLEND = 0.8
EPSILON = 1e-06
AXES = ("zlo", "x", "core", "zhi", "y")
SIZES = (2, 4, 2, 4, 4)
ROW = ("zlo", "x", "core")
COL = ("zhi", "y")
PLANE = ("x", "y")
LINE = ("zlo", "core", "zhi")
GROUP = 16
BLOCKS = GROUP * GROUP
ROWS = 128
FEAT = 768
EXTRA = 24
LOG2_E = 1.4426950408889634
NOTHING = -10000.0
FOLDS = FEAT // ROWS
CHUNK = 32
VMEM = pl.BlockSpec(memory_space=pltpu.VMEM)
SMEM = pl.BlockSpec(memory_space=pltpu.SMEM)
ANY = pl.BlockSpec(memory_space=pl.ANY)


def position():
    x, y, zlo, core, zhi = (lax.axis_index(name) for name in ("x", "y", "zlo", "core", "zhi"))
    return x, y, zlo, core, zhi, zlo * 8 + core * 4 + zhi


def prep_kernel(emb_hbm, slots_hbm, folded_ref, copies_ref, bits_ref,
                emb_ref, slots_ref, turned_ref, emb_sem, slots_sem, out_sem):
    copies = [
        pltpu.make_async_copy(emb_hbm, emb_ref, emb_sem),
        pltpu.make_async_copy(slots_hbm, slots_ref, slots_sem),
    ]
    for copy in copies:
        copy.start()
    for copy in copies:
        copy.wait()
    features = emb_ref[...].astype(jnp.float32)
    norm = lax.rsqrt(jnp.sum(features * features, axis=1, keepdims=True) + EPSILON)
    normed = features * norm
    for k in range(FOLDS):
        part = normed[:, k * ROWS : (k + 1) * ROWS]
        folded_ref[k * ROWS : (k + 1) * ROWS, :] = part.astype(jnp.bfloat16)
        turned_ref[k * ROWS : (k + 1) * ROWS, :] = part.T.astype(jnp.bfloat16)
    sends = [pltpu.make_async_copy(turned_ref, copies_ref.at[k], out_sem) for k in range(GROUP)]
    for send in sends:
        send.start()
    first, second = slots_ref[0:1, :], slots_ref[1:2, :]
    ids = jnp.where(first >= 0, first * GROUP + second, -1)
    hits = (lax.broadcasted_iota(jnp.int32, (BLOCKS, 32), 0) == ids).astype(jnp.float32)
    bits = lax.dot_general(
        jnp.ones((8, 32), jnp.float32), hits, (((1,), (1,)), ((), ())),
        preferred_element_type=jnp.float32,
    )
    row = lax.broadcasted_iota(jnp.int32, (8, ROWS), 0)
    halves = jnp.where(row < 4, bits[:, :ROWS], bits[:, ROWS:]).astype(jnp.bfloat16)
    bits_ref[...] = halves
    for send in sends:
        send.wait()


def relay_kernel(folded_ref, seeds_ref, bits_ref, *refs):
    x, y, *_ = position()
    out_ref = refs[6]
    out_ref[:FEAT, :] = folded_ref[...]
    row = lax.broadcasted_iota(jnp.int32, (8, ROWS), 0)
    groups = []
    for own, others in ((x, refs[:3]), (y, refs[3:6])):
        rows = jnp.zeros((8, ROWS), jnp.float32)
        for step, ref in enumerate((bits_ref, *others)):
            at = 2 * (own ^ step)
            note = ref[...].astype(jnp.float32)
            rows = jnp.where(row == at, note[0:1], jnp.where(row == at + 1, note[4:5], rows))
        groups.append(rows)
    groups.append(jnp.broadcast_to(seeds_ref[...].astype(jnp.float32), (8, ROWS)))
    out_ref[FEAT:, :] = jnp.concatenate(groups, axis=0).astype(jnp.bfloat16)


def make_list(notes, list_v):
    x, y, zlo, core, zhi, mine = position()
    shape = (BLOCKS, BLOCKS)
    row = lax.broadcasted_iota(jnp.int32, shape, 0)
    lane = lax.broadcasted_iota(jnp.int32, shape, 1)
    u_zhi, u_x = row >> 6, (row >> 4) & 3
    v_zlo, v_core, v_y = (row >> 3) & 1, (row >> 2) & 1, row & 3
    a_zhi, a_y = lane >> 6, (lane >> 4) & 3
    b_zlo, b_x, b_core = (lane >> 3) & 1, (lane >> 1) & 3, lane & 1
    forward = (a_zhi == zhi) & (b_x == x) & (a_y == v_y) & (b_zlo == v_zlo) & (b_core == v_core)
    mirror = (a_zhi == u_zhi) & (a_y == y) & (b_zlo == zlo) & (b_x == u_x) & (b_core == core)
    ahead, back = [], []
    for part in range(4):
        note = notes[part].astype(jnp.float32)
        for k in range(4):
            full = jnp.concatenate([note[2 * k : 2 * k + 1], note[2 * k + 1 : 2 * k + 2]], axis=1)
            ahead.append(jnp.broadcast_to(full, (GROUP, BLOCKS)))
        note = notes[(part ^ (mine >> 2)) * 4 + zhi].astype(jnp.float32)
        for k in range(4, 8):
            full = jnp.concatenate([note[2 * k : 2 * k + 1], note[2 * k + 1 : 2 * k + 2]], axis=1)
            back.append(full)
    ahead = jnp.concatenate(ahead, axis=0)
    back = jnp.concatenate(back * GROUP, axis=0)
    hits = jnp.where(forward, ahead, 0.0) + jnp.where(mirror, back, 0.0)
    counts = jnp.dot(
        hits.astype(jnp.bfloat16), jnp.ones(shape, jnp.bfloat16), preferred_element_type=jnp.float32
    )
    live = (counts > 0.0).astype(jnp.float32)
    upto = jnp.dot(
        (lane <= row).astype(jnp.float32).astype(jnp.bfloat16), live.astype(jnp.bfloat16),
        preferred_element_type=jnp.float32,
    )
    spot = jnp.where(lane.astype(jnp.float32) == upto - 1.0, live, 0.0)
    slot_lane = lax.broadcasted_iota(jnp.int32, (8, BLOCKS), 1)
    code = (
        (((slot_lane >> 4) & 3) * 4 + (slot_lane & 3)) * GROUP
        + ((slot_lane >> 3) & 1) * 8 + ((slot_lane >> 2) & 1) * 4 + (slot_lane >> 6)
    ).astype(jnp.float32).astype(jnp.bfloat16)
    ones = jnp.ones((8, BLOCKS), jnp.bfloat16)
    codes = jnp.dot(code, spot.astype(jnp.bfloat16), preferred_element_type=jnp.float32)
    weights = jnp.dot(ones, (spot * counts).astype(jnp.bfloat16), preferred_element_type=jnp.float32)
    found = jnp.dot(ones, live.astype(jnp.bfloat16), preferred_element_type=jnp.float32)
    line = lax.broadcasted_iota(jnp.int32, (8, BLOCKS), 0)
    diag = jnp.where(codes == ((x * 4 + y) * GROUP + mine).astype(jnp.float32), weights, 0.0)
    spots = jnp.where(diag > 0.0, slot_lane.astype(jnp.float32), 0.0)
    spot_at = jnp.broadcast_to(jnp.sum(spots, axis=1, keepdims=True), spots.shape)
    tail = jnp.where(line == 2, found, spot_at)
    table = jnp.where(line == 0, codes, jnp.where(line == 1, weights - diag, tail))
    list_v[...] = (table + 0.5).astype(jnp.int32)


def unfold(blocks, at):
    return jnp.concatenate([blocks[at, f * ROWS : (f + 1) * ROWS, :] for f in range(FOLDS)], axis=1)


def build_kernel(plane_ref, own_ref, mate_ref, far_ref, far_mate_ref,
                 tiles_ref, list_ref, deg_ref, seeds_ref, line_v, notes, sums, list_v, list_sem, line_sem, notes_sem):
    x, y, *_, mine = position()
    planes = mine & 12
    arrays = tuple(enumerate((own_ref, mate_ref, far_ref, far_mate_ref)))
    extras = [
        pltpu.make_async_copy(
            part.at[:, pl.ds(FEAT, EXTRA)], notes.at[pl.ds(at * 4, 4)], notes_sem
        )
        for at, part in arrays
    ]
    parts = [
        pltpu.make_async_copy(part.at[:, pl.ds(0, FEAT)], line_v.at[pl.ds(at * 4, 4)], line_sem)
        for at, part in arrays
    ]
    for copy in extras + parts:
        copy.start()
    for copy in extras:
        copy.wait()
    make_list(notes, list_v)
    list_copy = pltpu.make_async_copy(list_v, list_ref, list_sem)
    list_copy.start()
    for b in range(GROUP):
        seeds_ref[b : b + 1, :] = notes[b ^ planes, GROUP:, :].astype(jnp.float32)[0:1].astype(jnp.int32)
    sums[...] = jnp.zeros_like(sums)
    sharpness = FEAT**0.5 * LOG2_E
    list_copy.wait()
    for part in parts:
        part.wait()

    def scores(a, b):
        return jnp.dot(
            unfold(line_v, b ^ planes), plane_ref[a], preferred_element_type=jnp.float32
        )

    def build_chunk(group, carry):
        for k in range(CHUNK):
            at = group * CHUNK + k
            slot = list_ref[0, at]
            a, b = slot >> 4, slot & 15
            offset = jnp.where(list_ref[1, at] > 0, -sharpness, NOTHING)
            tile = jnp.exp2(sharpness * scores(a, b) + offset)
            tiles_ref[at] = tile.astype(jnp.bfloat16)
            sums[b] += tile
        return carry

    lax.fori_loop(0, (list_ref[2, 0] + CHUNK - 1) // CHUNK, build_chunk, 0)
    off_diag = (
        lax.broadcasted_iota(jnp.int32, (ROWS, ROWS), 0)
        != lax.broadcasted_iota(jnp.int32, (ROWS, ROWS), 1)
    )
    tile = 2.0 * jnp.exp2(sharpness * scores(x * 4 + y, mine) - sharpness)
    tile = jnp.where(off_diag, tile, 0.0)
    tiles_ref[list_ref[3, 0]] = tile.astype(jnp.bfloat16)
    sums[mine] += tile
    for b in range(GROUP):
        deg_ref[b : b + 1, :] = jnp.sum(sums[b].T, axis=0, keepdims=True)


def run_apply(list_ref, tiles_ref, out_ref, total, spread):
    total[...] = jnp.zeros_like(total)

    def chunk_step(group, carry):
        for k in range(CHUNK):
            at = group * CHUNK + k
            slot = list_ref[0, at]
            total[slot >> 4] += jnp.dot(
                spread[slot & 15], tiles_ref[at], preferred_element_type=jnp.float32
            )
        return carry

    lax.fori_loop(0, (list_ref[2, 0] + CHUNK - 1) // CHUNK, chunk_step, 0)
    out_ref[...] = total[...].astype(jnp.bfloat16)


def seeded_block(seeds_ref, b):
    classes = lax.broadcasted_iota(jnp.int32, (CLASSES, ROWS), 0)
    return classes == seeds_ref[b : b + 1, :]


def first_kernel(list_ref, tiles_ref, seeds_ref, parts_ref,
                 out_ref, scale_ref, own_ref, total, spread):
    scale_ref[...] = lax.rsqrt(jnp.sum(parts_ref[...], axis=0))
    own_ref[...] = scale_ref[pl.ds(position()[5], 1), :]
    for b in range(GROUP):
        seeded = jnp.where(seeded_block(seeds_ref, b), scale_ref[b : b + 1, :], 0.0)
        spread[b] = seeded.astype(jnp.bfloat16)
    run_apply(list_ref, tiles_ref, out_ref, total, spread)


def next_kernel(list_ref, tiles_ref, seeds_ref, scale_ref, own_ref, mate_ref,
                out_ref, total, spread):
    core = lax.axis_index("core")
    classes = lax.broadcasted_iota(jnp.int32, (CLASSES, ROWS), 0)
    for k in range(GROUP // 2):
        for smooth_ref, side in ((own_ref, core), (mate_ref, 1 - core)):
            b = (k // 4) * 8 + side * 4 + k % 4
            seeded = classes == seeds_ref[pl.ds(b, 1), :]
            seed_part = jnp.where(seeded, (1.0 - BLEND) * scale_ref[pl.ds(b, 1), :], 0.0)
            spread[b] = (smooth_ref[k].astype(jnp.float32) + seed_part).astype(jnp.bfloat16)
    run_apply(list_ref, tiles_ref, out_ref, total, spread)


def call(kernel, outs, ins, out_specs, scratch=(), limit=8):
    return pl.pallas_call(
        kernel,
        out_shape=outs,
        in_specs=ins,
        out_specs=out_specs,
        scratch_shapes=list(scratch),
        compiler_params=pltpu.CompilerParams(vmem_limit_bytes=limit << 20),
    )


def array(*shape, dtype=jnp.float32):
    return jax.ShapeDtypeStruct(shape, dtype)


def exchange(blocks, axes):
    return lax.all_to_all(blocks, axes, 0, 0)


def gather(block, axes, count=GROUP):
    return exchange(jnp.broadcast_to(block[None], (count,) + block.shape), axes)


def pairs(count, step):
    return [(k, k ^ step) for k in range(count)]


def local(embeddings, tile_list, seeds):
    folded, copies, bits = call(
        prep_kernel,
        (
            array(FEAT, ROWS, dtype=jnp.bfloat16),
            array(GROUP, FEAT, ROWS, dtype=jnp.bfloat16),
            array(8, ROWS, dtype=jnp.bfloat16),
        ),
        [ANY] * 2,
        (VMEM, ANY, VMEM),
        (
            pltpu.VMEM((ROWS, FEAT), jnp.bfloat16),
            pltpu.VMEM((2, 32), jnp.int32),
            pltpu.VMEM((FEAT, ROWS), jnp.bfloat16),
            pltpu.SemaphoreType.DMA,
            pltpu.SemaphoreType.DMA,
            pltpu.SemaphoreType.DMA,
        ),
        limit=60,
    )(embeddings, tile_list.reshape(-1, 2).T)
    others = []
    for axis in PLANE:
        for step in (1, 2, 3):
            others.append(lax.ppermute(bits, axis, pairs(4, step)))
    plane = exchange(copies, PLANE)
    block = call(
        relay_kernel,
        array(FEAT + EXTRA, ROWS, dtype=jnp.bfloat16),
        [VMEM] * 9,
        VMEM,
        limit=4,
    )(folded, seeds[None, :], bits, *others)
    own = pltpu.with_memory_space_constraint(lax.all_gather(block, "zhi"), pltpu.HBM)
    far = lax.ppermute(own, "zlo", pairs(2, 1))
    mate = lax.ppermute(own, "core", pairs(2, 1))
    far, mate = lax.optimization_barrier((far, mate))
    far_mate = lax.ppermute(far, "core", pairs(2, 1))

    tiles, listing, partial_degree, line_seeds = call(
        build_kernel,
        (
            array(BLOCKS, ROWS, ROWS, dtype=jnp.bfloat16),
            array(8, BLOCKS, dtype=jnp.int32),
            array(GROUP, ROWS),
            array(GROUP, ROWS, dtype=jnp.int32),
        ),
        [VMEM] + [ANY] * 4,
        (VMEM, SMEM, VMEM, VMEM),
        (
            pltpu.VMEM((GROUP, FEAT, ROWS), jnp.bfloat16),
            pltpu.VMEM((GROUP, EXTRA, ROWS), jnp.bfloat16),
            pltpu.VMEM((GROUP, ROWS, ROWS), jnp.float32),
            pltpu.VMEM((8, BLOCKS), jnp.int32),
            pltpu.SemaphoreType.DMA,
            pltpu.SemaphoreType.DMA,
            pltpu.SemaphoreType.DMA,
        ),
        limit=14,
    )(plane, own, mate, far, far_mate)

    scratch = (
        pltpu.VMEM((GROUP, CLASSES, ROWS), jnp.float32),
        pltpu.VMEM((GROUP, CLASSES, ROWS), jnp.bfloat16),
    )
    sums_out = array(GROUP, CLASSES, ROWS, dtype=jnp.bfloat16)
    partial, scale, own_scale = call(
        first_kernel,
        (sums_out, array(GROUP, ROWS), array(1, ROWS)),
        [SMEM, VMEM, VMEM, VMEM],
        (VMEM,) * 3,
        scratch,
        limit=6,
    )(listing, tiles, line_seeds, gather(partial_degree, LINE))
    for sweep in range(3):
        if sweep:
            smooth = (BLEND * own_scale * own_scale * summed).astype(jnp.bfloat16)
            smooth = gather(smooth, ("zlo", "zhi"), GROUP // 2)
            partial = call(
                next_kernel, sums_out, [SMEM] + [VMEM] * 5, VMEM, scratch, limit=6
            )(listing, tiles, line_seeds, scale, smooth, lax.ppermute(smooth, "core", pairs(2, 1)))
        summed, own_scale, seeds = lax.optimization_barrier((exchange(partial, PLANE), own_scale, seeds))
        summed = jnp.sum(summed.astype(jnp.float32), axis=0)
    seeded = seeds[None, :] == jnp.arange(CLASSES, dtype=jnp.int32)[:, None]
    labels = BLEND * own_scale * summed + (1.0 - BLEND) * seeded.astype(jnp.float32)
    return (CLASSES * labels).T


def solution(mesh):
    fine = Mesh(mesh.devices.reshape(SIZES), AXES)
    return jax.shard_map(
        local,
        mesh=fine,
        in_specs=(P(AXES, None), P(ROW, COL, None, None), P(AXES)),
        out_specs=P(AXES, None),
        check_vma=False,
    )
```

```python
import jax
import jax.numpy as jnp
from jax import lax
from jax.experimental import pallas as pl
from jax.experimental.pallas import tpu as pltpu
from jax.sharding import Mesh
from jax.sharding import PartitionSpec as P


CLASSES = 64
BLEND = 0.8
EPSILON = 1e-06
AXES = ("zlo", "x", "core", "zhi", "y")
SIZES = (2, 4, 2, 4, 4)
ROW = ("zlo", "x", "core")
COL = ("zhi", "y")
PLANE = ("x", "y")
LINE = ("zlo", "core", "zhi")
GROUP = 16
BLOCKS = GROUP * GROUP
ROWS = 128
FEAT = 768
EXTRA = 24
LOG2_E = 1.4426950408889634
NOTHING = -10000.0
FOLDS = FEAT // ROWS
CHUNK = 32
VMEM = pl.BlockSpec(memory_space=pltpu.VMEM)
SMEM = pl.BlockSpec(memory_space=pltpu.SMEM)
ANY = pl.BlockSpec(memory_space=pl.ANY)


def position():
    x, y, zlo, core, zhi = (lax.axis_index(name) for name in ("x", "y", "zlo", "core", "zhi"))
    return x, y, zlo, core, zhi, zlo * 8 + core * 4 + zhi


def prep_kernel(emb_hbm, slots_hbm, folded_ref, copies_ref, bits_ref,
                emb_ref, slots_ref, turned_ref, emb_sem, slots_sem, out_sem):
    copies = [
        pltpu.make_async_copy(emb_hbm, emb_ref, emb_sem),
        pltpu.make_async_copy(slots_hbm, slots_ref, slots_sem),
    ]
    for copy in copies:
        copy.start()
    for copy in copies:
        copy.wait()
    features = emb_ref[...].astype(jnp.float32)
    norm = lax.rsqrt(jnp.sum(features * features, axis=1, keepdims=True) + EPSILON)
    normed = features * norm
    for k in range(FOLDS):
        part = normed[:, k * ROWS : (k + 1) * ROWS]
        folded_ref[k * ROWS : (k + 1) * ROWS, :] = part.astype(jnp.bfloat16)
        turned_ref[k * ROWS : (k + 1) * ROWS, :] = part.T.astype(jnp.bfloat16)
    sends = [pltpu.make_async_copy(turned_ref, copies_ref.at[k], out_sem) for k in range(GROUP)]
    for send in sends:
        send.start()
    first, second = slots_ref[0:1, :], slots_ref[1:2, :]
    ids = jnp.where(first >= 0, first * GROUP + second, -1)
    hits = (lax.broadcasted_iota(jnp.int32, (BLOCKS, 32), 0) == ids).astype(jnp.float32)
    bits = lax.dot_general(
        jnp.ones((8, 32), jnp.float32), hits, (((1,), (1,)), ((), ())),
        preferred_element_type=jnp.float32,
    )
    row = lax.broadcasted_iota(jnp.int32, (8, ROWS), 0)
    halves = jnp.where(row < 4, bits[:, :ROWS], bits[:, ROWS:]).astype(jnp.bfloat16)
    bits_ref[...] = halves
    for send in sends:
        send.wait()


def relay_kernel(folded_ref, seeds_ref, bits_ref, *refs):
    x, y, *_ = position()
    out_ref = refs[6]
    out_ref[:FEAT, :] = folded_ref[...]
    row = lax.broadcasted_iota(jnp.int32, (8, ROWS), 0)
    groups = []
    for own, others in ((x, refs[:3]), (y, refs[3:6])):
        rows = jnp.zeros((8, ROWS), jnp.float32)
        for step, ref in enumerate((bits_ref, *others)):
            at = 2 * (own ^ step)
            note = ref[...].astype(jnp.float32)
            rows = jnp.where(row == at, note[0:1], jnp.where(row == at + 1, note[4:5], rows))
        groups.append(rows)
    groups.append(jnp.broadcast_to(seeds_ref[...].astype(jnp.float32), (8, ROWS)))
    out_ref[FEAT:, :] = jnp.concatenate(groups, axis=0).astype(jnp.bfloat16)


def make_list(notes, list_v):
    x, y, zlo, core, zhi, mine = position()
    shape = (BLOCKS, BLOCKS)
    row = lax.broadcasted_iota(jnp.int32, shape, 0)
    lane = lax.broadcasted_iota(jnp.int32, shape, 1)
    u_zhi, u_x = row >> 6, (row >> 4) & 3
    v_zlo, v_core, v_y = (row >> 3) & 1, (row >> 2) & 1, row & 3
    a_zhi, a_y = lane >> 6, (lane >> 4) & 3
    b_zlo, b_x, b_core = (lane >> 3) & 1, (lane >> 1) & 3, lane & 1
    forward = (a_zhi == zhi) & (b_x == x) & (a_y == v_y) & (b_zlo == v_zlo) & (b_core == v_core)
    mirror = (a_zhi == u_zhi) & (a_y == y) & (b_zlo == zlo) & (b_x == u_x) & (b_core == core)
    ahead, back = [], []
    for part in range(4):
        note = notes[part].astype(jnp.float32)
        for k in range(4):
            full = jnp.concatenate([note[2 * k : 2 * k + 1], note[2 * k + 1 : 2 * k + 2]], axis=1)
            ahead.append(jnp.broadcast_to(full, (GROUP, BLOCKS)))
        note = notes[(part ^ (mine >> 2)) * 4 + zhi].astype(jnp.float32)
        for k in range(4, 8):
            full = jnp.concatenate([note[2 * k : 2 * k + 1], note[2 * k + 1 : 2 * k + 2]], axis=1)
            back.append(full)
    ahead = jnp.concatenate(ahead, axis=0)
    back = jnp.concatenate(back * GROUP, axis=0)
    hits = jnp.where(forward, ahead, 0.0) + jnp.where(mirror, back, 0.0)
    counts = jnp.dot(
        hits.astype(jnp.bfloat16), jnp.ones(shape, jnp.bfloat16), preferred_element_type=jnp.float32
    )
    live = (counts > 0.0).astype(jnp.float32)
    upto = jnp.dot(
        (lane <= row).astype(jnp.float32).astype(jnp.bfloat16), live.astype(jnp.bfloat16),
        preferred_element_type=jnp.float32,
    )
    spot = jnp.where(lane.astype(jnp.float32) == upto - 1.0, live, 0.0)
    slot_lane = lax.broadcasted_iota(jnp.int32, (8, BLOCKS), 1)
    code = (
        (((slot_lane >> 4) & 3) * 4 + (slot_lane & 3)) * GROUP
        + ((slot_lane >> 3) & 1) * 8 + ((slot_lane >> 2) & 1) * 4 + (slot_lane >> 6)
    ).astype(jnp.float32).astype(jnp.bfloat16)
    ones = jnp.ones((8, BLOCKS), jnp.bfloat16)
    codes = jnp.dot(code, spot.astype(jnp.bfloat16), preferred_element_type=jnp.float32)
    weights = jnp.dot(ones, (spot * counts).astype(jnp.bfloat16), preferred_element_type=jnp.float32)
    found = jnp.dot(ones, live.astype(jnp.bfloat16), preferred_element_type=jnp.float32)
    line = lax.broadcasted_iota(jnp.int32, (8, BLOCKS), 0)
    diag = jnp.where(codes == ((x * 4 + y) * GROUP + mine).astype(jnp.float32), weights, 0.0)
    spots = jnp.where(diag > 0.0, slot_lane.astype(jnp.float32), 0.0)
    spot_at = jnp.broadcast_to(jnp.sum(spots, axis=1, keepdims=True), spots.shape)
    tail = jnp.where(line == 2, found, spot_at)
    table = jnp.where(line == 0, codes, jnp.where(line == 1, weights - diag, tail))
    list_v[...] = (table + 0.5).astype(jnp.int32)


def unfold(blocks, at):
    return jnp.concatenate([blocks[at, f * ROWS : (f + 1) * ROWS, :] for f in range(FOLDS)], axis=1)


def build_kernel(plane_ref, own_ref, mate_ref, far_ref, far_mate_ref,
                 tiles_ref, list_ref, deg_ref, seeds_ref, line_v, notes, sums, list_v, list_sem, line_sem, notes_sem):
    x, y, *_, mine = position()
    planes = mine & 12
    arrays = tuple(enumerate((own_ref, mate_ref, far_ref, far_mate_ref)))
    extras = [
        pltpu.make_async_copy(
            part.at[:, pl.ds(FEAT, EXTRA)], notes.at[pl.ds(at * 4, 4)], notes_sem
        )
        for at, part in arrays
    ]
    parts = [
        pltpu.make_async_copy(part.at[:, pl.ds(0, FEAT)], line_v.at[pl.ds(at * 4, 4)], line_sem)
        for at, part in arrays
    ]
    for copy in extras + parts:
        copy.start()
    for copy in extras:
        copy.wait()
    make_list(notes, list_v)
    list_copy = pltpu.make_async_copy(list_v, list_ref, list_sem)
    list_copy.start()
    for b in range(GROUP):
        seeds_ref[b : b + 1, :] = notes[b ^ planes, GROUP:, :].astype(jnp.float32)[0:1].astype(jnp.int32)
    sums[...] = jnp.zeros_like(sums)
    sharpness = FEAT**0.5 * LOG2_E
    list_copy.wait()
    for part in parts:
        part.wait()

    def scores(a, b):
        return jnp.dot(
            unfold(line_v, b ^ planes), plane_ref[a], preferred_element_type=jnp.float32
        )

    def build_chunk(group, carry):
        for k in range(CHUNK):
            at = group * CHUNK + k
            slot = list_ref[0, at]
            a, b = slot >> 4, slot & 15
            offset = jnp.where(list_ref[1, at] > 0, -sharpness, NOTHING)
            tile = jnp.exp2(sharpness * scores(a, b) + offset)
            tiles_ref[at] = tile.astype(jnp.bfloat16)
            sums[b] += tile
        return carry

    lax.fori_loop(0, (list_ref[2, 0] + CHUNK - 1) // CHUNK, build_chunk, 0)
    off_diag = (
        lax.broadcasted_iota(jnp.int32, (ROWS, ROWS), 0)
        != lax.broadcasted_iota(jnp.int32, (ROWS, ROWS), 1)
    )
    tile = 2.0 * jnp.exp2(sharpness * scores(x * 4 + y, mine) - sharpness)
    tile = jnp.where(off_diag, tile, 0.0)
    tiles_ref[list_ref[3, 0]] = tile.astype(jnp.bfloat16)
    sums[mine] += tile
    rows = [jnp.sum(sums[b].T, axis=0, keepdims=True) for b in range(GROUP)]
    deg_ref[...] = jnp.concatenate(rows, axis=0).astype(jnp.bfloat16)


def run_apply(list_ref, tiles_ref, out_ref, total, spread):
    total[...] = jnp.zeros_like(total)

    def chunk_step(group, carry):
        for k in range(CHUNK):
            at = group * CHUNK + k
            slot = list_ref[0, at]
            total[slot >> 4] += jnp.dot(
                spread[slot & 15], tiles_ref[at], preferred_element_type=jnp.float32
            )
        return carry

    lax.fori_loop(0, (list_ref[2, 0] + CHUNK - 1) // CHUNK, chunk_step, 0)
    out_ref[...] = total[...].astype(jnp.bfloat16)


def seeded_block(seeds_ref, b):
    classes = lax.broadcasted_iota(jnp.int32, (CLASSES, ROWS), 0)
    return classes == seeds_ref[b : b + 1, :]


def first_kernel(list_ref, tiles_ref, seeds_ref, parts_ref,
                 out_ref, scale_ref, own_ref, total, spread):
    scale_ref[...] = lax.rsqrt(jnp.sum(parts_ref[...].astype(jnp.float32), axis=0))
    own_ref[...] = scale_ref[pl.ds(position()[5], 1), :]
    for b in range(GROUP):
        seeded = jnp.where(seeded_block(seeds_ref, b), scale_ref[b : b + 1, :], 0.0)
        spread[b] = seeded.astype(jnp.bfloat16)
    run_apply(list_ref, tiles_ref, out_ref, total, spread)


def next_kernel(list_ref, tiles_ref, seeds_ref, scale_ref, own_ref, mate_ref,
                out_ref, total, spread):
    core = lax.axis_index("core")
    classes = lax.broadcasted_iota(jnp.int32, (CLASSES, ROWS), 0)
    for k in range(GROUP // 2):
        for smooth_ref, side in ((own_ref, core), (mate_ref, 1 - core)):
            b = (k // 4) * 8 + side * 4 + k % 4
            seeded = classes == seeds_ref[pl.ds(b, 1), :]
            seed_part = jnp.where(seeded, (1.0 - BLEND) * scale_ref[pl.ds(b, 1), :], 0.0)
            spread[b] = (smooth_ref[k].astype(jnp.float32) + seed_part).astype(jnp.bfloat16)
    run_apply(list_ref, tiles_ref, out_ref, total, spread)


def call(kernel, outs, ins, out_specs, scratch=(), limit=8):
    return pl.pallas_call(
        kernel,
        out_shape=outs,
        in_specs=ins,
        out_specs=out_specs,
        scratch_shapes=list(scratch),
        compiler_params=pltpu.CompilerParams(vmem_limit_bytes=limit << 20),
    )


def array(*shape, dtype=jnp.float32):
    return jax.ShapeDtypeStruct(shape, dtype)


def exchange(blocks, axes):
    return lax.all_to_all(blocks, axes, 0, 0)


def gather(block, axes, count=GROUP):
    return exchange(jnp.broadcast_to(block[None], (count,) + block.shape), axes)


def pairs(count, step):
    return [(k, k ^ step) for k in range(count)]


def local(embeddings, tile_list, seeds):
    folded, copies, bits = call(
        prep_kernel,
        (
            array(FEAT, ROWS, dtype=jnp.bfloat16),
            array(GROUP, FEAT, ROWS, dtype=jnp.bfloat16),
            array(8, ROWS, dtype=jnp.bfloat16),
        ),
        [ANY] * 2,
        (VMEM, ANY, VMEM),
        (
            pltpu.VMEM((ROWS, FEAT), jnp.bfloat16),
            pltpu.VMEM((2, 32), jnp.int32),
            pltpu.VMEM((FEAT, ROWS), jnp.bfloat16),
            pltpu.SemaphoreType.DMA,
            pltpu.SemaphoreType.DMA,
            pltpu.SemaphoreType.DMA,
        ),
        limit=60,
    )(embeddings, tile_list.reshape(-1, 2).T)
    others = []
    for axis in PLANE:
        near = lax.ppermute(bits, axis, pairs(4, 1))
        last = lax.ppermute(bits, axis, pairs(4, 3))
        passed = lax.ppermute(near, axis, pairs(4, 3))
        others += [near, passed, last]
    plane = exchange(copies, PLANE)
    block = call(
        relay_kernel,
        array(FEAT + EXTRA, ROWS, dtype=jnp.bfloat16),
        [VMEM] * 9,
        VMEM,
        limit=4,
    )(folded, seeds[None, :], bits, *others)
    own = pltpu.with_memory_space_constraint(lax.all_gather(block, "zhi"), pltpu.HBM)
    far = lax.ppermute(own, "zlo", pairs(2, 1))
    mate = lax.ppermute(own, "core", pairs(2, 1))
    far, mate = lax.optimization_barrier((far, mate))
    far_mate = lax.ppermute(far, "core", pairs(2, 1))

    tiles, listing, partial_degree, line_seeds = call(
        build_kernel,
        (
            array(BLOCKS, ROWS, ROWS, dtype=jnp.bfloat16),
            array(8, BLOCKS, dtype=jnp.int32),
            array(GROUP, ROWS, dtype=jnp.bfloat16),
            array(GROUP, ROWS, dtype=jnp.int32),
        ),
        [VMEM] + [ANY] * 4,
        (VMEM, SMEM, VMEM, VMEM),
        (
            pltpu.VMEM((GROUP, FEAT, ROWS), jnp.bfloat16),
            pltpu.VMEM((GROUP, EXTRA, ROWS), jnp.bfloat16),
            pltpu.VMEM((GROUP, ROWS, ROWS), jnp.float32),
            pltpu.VMEM((8, BLOCKS), jnp.int32),
            pltpu.SemaphoreType.DMA,
            pltpu.SemaphoreType.DMA,
            pltpu.SemaphoreType.DMA,
        ),
        limit=14,
    )(plane, own, mate, far, far_mate)

    scratch = (
        pltpu.VMEM((GROUP, CLASSES, ROWS), jnp.float32),
        pltpu.VMEM((GROUP, CLASSES, ROWS), jnp.bfloat16),
    )
    sums_out = array(GROUP, CLASSES, ROWS, dtype=jnp.bfloat16)
    partial, scale, own_scale = call(
        first_kernel,
        (sums_out, array(GROUP, ROWS), array(1, ROWS)),
        [SMEM, VMEM, VMEM, VMEM],
        (VMEM,) * 3,
        scratch,
        limit=6,
    )(listing, tiles, line_seeds, gather(partial_degree, LINE))
    for sweep in range(3):
        if sweep:
            smooth = (BLEND * own_scale * own_scale * summed).astype(jnp.bfloat16)
            smooth = gather(smooth, ("zlo", "zhi"), GROUP // 2)
            partial = call(
                next_kernel, sums_out, [SMEM] + [VMEM] * 5, VMEM, scratch, limit=6
            )(listing, tiles, line_seeds, scale, smooth, lax.ppermute(smooth, "core", pairs(2, 1)))
        summed, own_scale, seeds = lax.optimization_barrier((exchange(partial, PLANE), own_scale, seeds))
        summed = jnp.sum(summed.astype(jnp.float32), axis=0)
    seeded = seeds[None, :] == jnp.arange(CLASSES, dtype=jnp.int32)[:, None]
    labels = BLEND * own_scale * summed + (1.0 - BLEND) * seeded.astype(jnp.float32)
    return (CLASSES * labels).T


def solution(mesh):
    fine = Mesh(mesh.devices.reshape(SIZES), AXES)
    return jax.shard_map(
        local,
        mesh=fine,
        in_specs=(P(AXES, None), P(ROW, COL, None, None), P(AXES)),
        out_specs=P(AXES, None),
        check_vma=False,
    )
```

```python
import jax
import jax.numpy as jnp
from jax import lax
from jax.experimental import pallas as pl
from jax.experimental.pallas import tpu as pltpu
from jax.sharding import Mesh
from jax.sharding import PartitionSpec as P


CLASSES = 64
BLEND = 0.8
EPSILON = 1e-06
AXES = ("zlo", "x", "core", "zhi", "y")
SIZES = (2, 4, 2, 4, 4)
ROW = ("zlo", "x", "core")
COL = ("zhi", "y")
PLANE = ("x", "y")
LINE = ("zlo", "core", "zhi")
GROUP = 16
BLOCKS = GROUP * GROUP
ROWS = 128
FEAT = 768
EXTRA = 24
LOG2_E = 1.4426950408889634
NOTHING = -10000.0
FOLDS = FEAT // ROWS
CHUNK = 32
VMEM = pl.BlockSpec(memory_space=pltpu.VMEM)
SMEM = pl.BlockSpec(memory_space=pltpu.SMEM)
ANY = pl.BlockSpec(memory_space=pl.ANY)


def position():
    x, y, zlo, core, zhi = (lax.axis_index(name) for name in ("x", "y", "zlo", "core", "zhi"))
    return x, y, zlo, core, zhi, zlo * 8 + core * 4 + zhi


def prep_kernel(emb_hbm, slots_hbm, folded_ref, copies_ref, bits_ref,
                emb_ref, slots_ref, turned_ref, emb_sem, slots_sem, out_sem):
    copies = [
        pltpu.make_async_copy(emb_hbm, emb_ref, emb_sem),
        pltpu.make_async_copy(slots_hbm, slots_ref, slots_sem),
    ]
    for copy in copies:
        copy.start()
    for copy in copies:
        copy.wait()
    features = emb_ref[...].astype(jnp.float32)
    norm = lax.rsqrt(jnp.sum(features * features, axis=1, keepdims=True) + EPSILON)
    normed = features * norm
    for k in range(FOLDS):
        part = normed[:, k * ROWS : (k + 1) * ROWS]
        folded_ref[k * ROWS : (k + 1) * ROWS, :] = part.astype(jnp.bfloat16)
        turned_ref[k * ROWS : (k + 1) * ROWS, :] = part.T.astype(jnp.bfloat16)
    sends = [pltpu.make_async_copy(turned_ref, copies_ref.at[k], out_sem) for k in range(GROUP)]
    for send in sends:
        send.start()
    first, second = slots_ref[0:1, :], slots_ref[1:2, :]
    ids = jnp.where(first >= 0, first * GROUP + second, -1)
    hits = (lax.broadcasted_iota(jnp.int32, (BLOCKS, 32), 0) == ids).astype(jnp.float32)
    bits = lax.dot_general(
        jnp.ones((8, 32), jnp.float32), hits, (((1,), (1,)), ((), ())),
        preferred_element_type=jnp.float32,
    )
    row = lax.broadcasted_iota(jnp.int32, (8, ROWS), 0)
    halves = jnp.where(row < 4, bits[:, :ROWS], bits[:, ROWS:]).astype(jnp.bfloat16)
    bits_ref[...] = halves
    for send in sends:
        send.wait()


def relay_kernel(folded_ref, seeds_ref, bits_ref, *refs):
    x, y, *_ = position()
    out_ref = refs[6]
    out_ref[:FEAT, :] = folded_ref[...]
    row = lax.broadcasted_iota(jnp.int32, (8, ROWS), 0)
    groups = []
    for own, others in ((x, refs[:3]), (y, refs[3:6])):
        rows = jnp.zeros((8, ROWS), jnp.float32)
        for step, ref in enumerate((bits_ref, *others)):
            at = 2 * (own ^ step)
            note = ref[...].astype(jnp.float32)
            rows = jnp.where(row == at, note[0:1], jnp.where(row == at + 1, note[4:5], rows))
        groups.append(rows)
    groups.append(jnp.broadcast_to(seeds_ref[...].astype(jnp.float32), (8, ROWS)))
    out_ref[FEAT:, :] = jnp.concatenate(groups, axis=0).astype(jnp.bfloat16)


def make_list(notes, list_v):
    x, y, zlo, core, zhi, mine = position()
    shape = (BLOCKS, BLOCKS)
    row = lax.broadcasted_iota(jnp.int32, shape, 0)
    lane = lax.broadcasted_iota(jnp.int32, shape, 1)
    u_zhi, u_x = row >> 6, (row >> 4) & 3
    v_zlo, v_core, v_y = (row >> 3) & 1, (row >> 2) & 1, row & 3
    a_zhi, a_y = lane >> 6, (lane >> 4) & 3
    b_zlo, b_x, b_core = (lane >> 3) & 1, (lane >> 1) & 3, lane & 1
    forward = (a_zhi == zhi) & (b_x == x) & (a_y == v_y) & (b_zlo == v_zlo) & (b_core == v_core)
    mirror = (a_zhi == u_zhi) & (a_y == y) & (b_zlo == zlo) & (b_x == u_x) & (b_core == core)
    ahead, back = [], []
    for part in range(4):
        note = notes[part].astype(jnp.float32)
        for k in range(4):
            full = jnp.concatenate([note[2 * k : 2 * k + 1], note[2 * k + 1 : 2 * k + 2]], axis=1)
            ahead.append(jnp.broadcast_to(full, (GROUP, BLOCKS)))
        note = notes[(part ^ (mine >> 2)) * 4 + zhi].astype(jnp.float32)
        for k in range(4, 8):
            full = jnp.concatenate([note[2 * k : 2 * k + 1], note[2 * k + 1 : 2 * k + 2]], axis=1)
            back.append(full)
    ahead = jnp.concatenate(ahead, axis=0)
    back = jnp.concatenate(back * GROUP, axis=0)
    hits = jnp.where(forward, ahead, 0.0) + jnp.where(mirror, back, 0.0)
    counts = jnp.dot(
        hits.astype(jnp.bfloat16), jnp.ones(shape, jnp.bfloat16), preferred_element_type=jnp.float32
    )
    live = (counts > 0.0).astype(jnp.float32)
    upto = jnp.dot(
        (lane <= row).astype(jnp.float32).astype(jnp.bfloat16), live.astype(jnp.bfloat16),
        preferred_element_type=jnp.float32,
    )
    spot = jnp.where(lane.astype(jnp.float32) == upto - 1.0, live, 0.0)
    slot_lane = lax.broadcasted_iota(jnp.int32, (8, BLOCKS), 1)
    code = (
        (((slot_lane >> 4) & 3) * 4 + (slot_lane & 3)) * GROUP
        + ((slot_lane >> 3) & 1) * 8 + ((slot_lane >> 2) & 1) * 4 + (slot_lane >> 6)
    ).astype(jnp.float32).astype(jnp.bfloat16)
    ones = jnp.ones((8, BLOCKS), jnp.bfloat16)
    codes = jnp.dot(code, spot.astype(jnp.bfloat16), preferred_element_type=jnp.float32)
    weights = jnp.dot(ones, (spot * counts).astype(jnp.bfloat16), preferred_element_type=jnp.float32)
    found = jnp.dot(ones, live.astype(jnp.bfloat16), preferred_element_type=jnp.float32)
    line = lax.broadcasted_iota(jnp.int32, (8, BLOCKS), 0)
    diag = jnp.where(codes == ((x * 4 + y) * GROUP + mine).astype(jnp.float32), weights, 0.0)
    spots = jnp.where(diag > 0.0, slot_lane.astype(jnp.float32), 0.0)
    spot_at = jnp.broadcast_to(jnp.sum(spots, axis=1, keepdims=True), spots.shape)
    tail = jnp.where(line == 2, found, spot_at)
    table = jnp.where(line == 0, codes, jnp.where(line == 1, weights - diag, tail))
    list_v[...] = (table + 0.5).astype(jnp.int32)


def unfold(blocks, at):
    return jnp.concatenate([blocks[at, f * ROWS : (f + 1) * ROWS, :] for f in range(FOLDS)], axis=1)


def build_kernel(plane_ref, own_ref, mate_ref, far_ref, far_mate_ref,
                 tiles_ref, list_ref, deg_ref, seeds_ref, line_v, notes, sums, list_v, list_sem, line_sem, notes_sem):
    x, y, *_, mine = position()
    planes = mine & 12
    arrays = tuple(enumerate((own_ref, mate_ref, far_ref, far_mate_ref)))
    extras = [
        pltpu.make_async_copy(
            part.at[:, pl.ds(FEAT, EXTRA)], notes.at[pl.ds(at * 4, 4)], notes_sem
        )
        for at, part in arrays
    ]
    parts = [
        pltpu.make_async_copy(part.at[:, pl.ds(0, FEAT)], line_v.at[pl.ds(at * 4, 4)], line_sem)
        for at, part in arrays
    ]
    for copy in extras + parts:
        copy.start()
    for copy in extras:
        copy.wait()
    make_list(notes, list_v)
    list_copy = pltpu.make_async_copy(list_v, list_ref, list_sem)
    list_copy.start()
    for b in range(GROUP):
        seeds_ref[b : b + 1, :] = notes[b ^ planes, GROUP:, :].astype(jnp.float32)[0:1].astype(jnp.int32)
    sums[...] = jnp.zeros_like(sums)
    sharpness = FEAT**0.5 * LOG2_E
    list_copy.wait()
    for part in parts:
        part.wait()

    def scores(a, b):
        return jnp.dot(
            unfold(line_v, b ^ planes), plane_ref[a], preferred_element_type=jnp.float32
        )

    def build_chunk(group, carry):
        for k in range(CHUNK):
            at = group * CHUNK + k
            slot = list_ref[0, at]
            a, b = slot >> 4, slot & 15
            offset = jnp.where(list_ref[1, at] > 0, -sharpness, NOTHING)
            tile = jnp.exp2(sharpness * scores(a, b) + offset)
            tiles_ref[at] = tile.astype(jnp.bfloat16)
            sums[b] += tile
        return carry

    lax.fori_loop(0, (list_ref[2, 0] + CHUNK - 1) // CHUNK, build_chunk, 0)
    off_diag = (
        lax.broadcasted_iota(jnp.int32, (ROWS, ROWS), 0)
        != lax.broadcasted_iota(jnp.int32, (ROWS, ROWS), 1)
    )
    tile = 2.0 * jnp.exp2(sharpness * scores(x * 4 + y, mine) - sharpness)
    tile = jnp.where(off_diag, tile, 0.0)
    tiles_ref[list_ref[3, 0]] = tile.astype(jnp.bfloat16)
    sums[mine] += tile
    ones = jnp.ones((8, 2 * ROWS), jnp.bfloat16)
    rows = []
    for b in range(GROUP):
        high = sums[b].astype(jnp.bfloat16)
        low = (sums[b] - high.astype(jnp.float32)).astype(jnp.bfloat16)
        row = lax.dot_general(
            ones, jnp.concatenate([high, low], axis=1), (((1,), (1,)), ((), ())),
            preferred_element_type=jnp.float32,
        )
        rows.append(row[0:1])
    deg_ref[...] = jnp.concatenate(rows, axis=0).astype(jnp.bfloat16)


def run_apply(list_ref, tiles_ref, out_ref, total, spread):
    total[...] = jnp.zeros_like(total)

    def chunk_step(group, carry):
        for k in range(CHUNK):
            at = group * CHUNK + k
            slot = list_ref[0, at]
            total[slot >> 4] += jnp.dot(
                spread[slot & 15], tiles_ref[at], preferred_element_type=jnp.float32
            )
        return carry

    lax.fori_loop(0, (list_ref[2, 0] + CHUNK - 1) // CHUNK, chunk_step, 0)
    out_ref[...] = total[...].astype(jnp.bfloat16)


def seeded_block(seeds_ref, b):
    classes = lax.broadcasted_iota(jnp.int32, (CLASSES, ROWS), 0)
    return classes == seeds_ref[b : b + 1, :]


def first_kernel(list_ref, tiles_ref, seeds_ref, parts_ref,
                 out_ref, scale_ref, own_ref, total, spread):
    scale_ref[...] = lax.rsqrt(jnp.sum(parts_ref[...].astype(jnp.float32), axis=0))
    own_ref[...] = scale_ref[pl.ds(position()[5], 1), :]
    for b in range(GROUP):
        seeded = jnp.where(seeded_block(seeds_ref, b), scale_ref[b : b + 1, :], 0.0)
        spread[b] = seeded.astype(jnp.bfloat16)
    run_apply(list_ref, tiles_ref, out_ref, total, spread)


def next_kernel(list_ref, tiles_ref, seeds_ref, scale_ref, own_ref, mate_ref,
                out_ref, total, spread):
    core = lax.axis_index("core")
    classes = lax.broadcasted_iota(jnp.int32, (CLASSES, ROWS), 0)
    for k in range(GROUP // 2):
        for smooth_ref, side in ((own_ref, core), (mate_ref, 1 - core)):
            b = (k // 4) * 8 + side * 4 + k % 4
            seeded = classes == seeds_ref[pl.ds(b, 1), :]
            seed_part = jnp.where(seeded, (1.0 - BLEND) * scale_ref[pl.ds(b, 1), :], 0.0)
            spread[b] = (smooth_ref[k].astype(jnp.float32) + seed_part).astype(jnp.bfloat16)
    run_apply(list_ref, tiles_ref, out_ref, total, spread)


def call(kernel, outs, ins, out_specs, scratch=(), limit=8):
    return pl.pallas_call(
        kernel,
        out_shape=outs,
        in_specs=ins,
        out_specs=out_specs,
        scratch_shapes=list(scratch),
        compiler_params=pltpu.CompilerParams(vmem_limit_bytes=limit << 20),
    )


def array(*shape, dtype=jnp.float32):
    return jax.ShapeDtypeStruct(shape, dtype)


def exchange(blocks, axes):
    return lax.all_to_all(blocks, axes, 0, 0)


def gather(block, axes, count=GROUP):
    return exchange(jnp.broadcast_to(block[None], (count,) + block.shape), axes)


def pairs(count, step):
    return [(k, k ^ step) for k in range(count)]


def local(embeddings, tile_list, seeds):
    folded, copies, bits = call(
        prep_kernel,
        (
            array(FEAT, ROWS, dtype=jnp.bfloat16),
            array(GROUP, FEAT, ROWS, dtype=jnp.bfloat16),
            array(8, ROWS, dtype=jnp.bfloat16),
        ),
        [ANY] * 2,
        (VMEM, ANY, VMEM),
        (
            pltpu.VMEM((ROWS, FEAT), jnp.bfloat16),
            pltpu.VMEM((2, 32), jnp.int32),
            pltpu.VMEM((FEAT, ROWS), jnp.bfloat16),
            pltpu.SemaphoreType.DMA,
            pltpu.SemaphoreType.DMA,
            pltpu.SemaphoreType.DMA,
        ),
        limit=60,
    )(embeddings, tile_list.reshape(-1, 2).T)
    others = []
    for axis in PLANE:
        near = lax.ppermute(bits, axis, pairs(4, 1))
        last = lax.ppermute(bits, axis, pairs(4, 3))
        passed = lax.ppermute(near, axis, pairs(4, 3))
        others += [near, passed, last]
    plane = exchange(copies, PLANE)
    block = call(
        relay_kernel,
        array(FEAT + EXTRA, ROWS, dtype=jnp.bfloat16),
        [VMEM] * 9,
        VMEM,
        limit=4,
    )(folded, seeds[None, :], bits, *others)
    own = pltpu.with_memory_space_constraint(lax.all_gather(block, "zhi"), pltpu.HBM)
    far = lax.ppermute(own, "zlo", pairs(2, 1))
    mate = lax.ppermute(own, "core", pairs(2, 1))
    far, mate = lax.optimization_barrier((far, mate))
    far_mate = lax.ppermute(far, "core", pairs(2, 1))

    tiles, listing, partial_degree, line_seeds = call(
        build_kernel,
        (
            array(BLOCKS, ROWS, ROWS, dtype=jnp.bfloat16),
            array(8, BLOCKS, dtype=jnp.int32),
            array(GROUP, ROWS, dtype=jnp.bfloat16),
            array(GROUP, ROWS, dtype=jnp.int32),
        ),
        [VMEM] + [ANY] * 4,
        (VMEM, SMEM, VMEM, VMEM),
        (
            pltpu.VMEM((GROUP, FEAT, ROWS), jnp.bfloat16),
            pltpu.VMEM((GROUP, EXTRA, ROWS), jnp.bfloat16),
            pltpu.VMEM((GROUP, ROWS, ROWS), jnp.float32),
            pltpu.VMEM((8, BLOCKS), jnp.int32),
            pltpu.SemaphoreType.DMA,
            pltpu.SemaphoreType.DMA,
            pltpu.SemaphoreType.DMA,
        ),
        limit=14,
    )(plane, own, mate, far, far_mate)

    scratch = (
        pltpu.VMEM((GROUP, CLASSES, ROWS), jnp.float32),
        pltpu.VMEM((GROUP, CLASSES, ROWS), jnp.bfloat16),
    )
    sums_out = array(GROUP, CLASSES, ROWS, dtype=jnp.bfloat16)
    partial, scale, own_scale = call(
        first_kernel,
        (sums_out, array(GROUP, ROWS), array(1, ROWS)),
        [SMEM, VMEM, VMEM, VMEM],
        (VMEM,) * 3,
        scratch,
        limit=6,
    )(listing, tiles, line_seeds, gather(partial_degree, LINE))
    for sweep in range(3):
        if sweep:
            smooth = (BLEND * own_scale * own_scale * summed).astype(jnp.bfloat16)
            smooth = gather(smooth, ("zlo", "zhi"), GROUP // 2)
            partial = call(
                next_kernel, sums_out, [SMEM] + [VMEM] * 5, VMEM, scratch, limit=6
            )(listing, tiles, line_seeds, scale, smooth, lax.ppermute(smooth, "core", pairs(2, 1)))
        summed, own_scale, seeds = lax.optimization_barrier((exchange(partial, PLANE), own_scale, seeds))
        summed = jnp.sum(summed.astype(jnp.float32), axis=0)
    seeded = seeds[None, :] == jnp.arange(CLASSES, dtype=jnp.int32)[:, None]
    labels = BLEND * own_scale * summed + (1.0 - BLEND) * seeded.astype(jnp.float32)
    return (CLASSES * labels).T


def solution(mesh):
    fine = Mesh(mesh.devices.reshape(SIZES), AXES)
    return jax.shard_map(
        local,
        mesh=fine,
        in_specs=(P(AXES, None), P(ROW, COL, None, None), P(AXES)),
        out_specs=P(AXES, None),
        check_vma=False,
    )
```
